32 devices in a mesh: shard: 8 (over z, x), rep: 4 (over y, core).
Axes of the slice: x: 2, y: 2, z: 4, core: 2. Of those that a mesh axis runs over, the one named last changes fastest.
Arguments:
- hidden_in: bfloat16 [16384, 2048], P(('shard', 'rep')), may hold values from -6 to 6
- doc_ids: int32 [32, 512], P(('shard', 'rep')), may hold values from 0 to 3, never falling along the last dimension, each value on 1 to 256 neighbouring positions
- expert_ids: int32 [16384, 8], P(('shard', 'rep')), may hold values from 0 to 63, as said below
- slot_rows: int32 [32, 2, 128], P(('shard', 'rep')), may hold values from 0 to 512, as said below
- out_grad: bfloat16 [16384, 2048], P(('shard', 'rep')), may hold values from -6 to 6
- attn_gain: bfloat16 [2048], P('shard'), may hold values from 0.5 to 1.5
- w_query: bfloat16 [2048, 2048], P('shard'), may hold values from -0.125 to 0.125
- w_key: bfloat16 [2048, 2048], P('shard'), may hold values from -0.125 to 0.125
- w_value: bfloat16 [2048, 2048], P('shard'), may hold values from -0.125 to 0.125
- query_gain: bfloat16 [2048], P('shard'), may hold values from 0.5 to 1.5
- key_gain: bfloat16 [2048], P('shard'), may hold values from 0.5 to 1.5
- w_output: bfloat16 [2048, 2048], P('shard'), may hold values from -0.75 to 0.75
- ffn_gain: bfloat16 [2048], P('shard'), may hold values from 0.5 to 1.5
- w_router: bfloat16 [2048, 64], P('shard'), may hold values from -0.0625 to 0.0625
- w_gate: bfloat16 [2, 2048, 1024], P(None, 'shard'), may hold values from -0.125 to 0.125
- w_up: bfloat16 [2, 2048, 1024], P(None, 'shard'), may hold values from -0.125 to 0.125
- w_down: bfloat16 [2, 1024, 2048], P(None, 'shard'), may hold values from -24 to 24
Outputs:
- hidden_out: bfloat16 [16384, 2048], P(('shard', 'rep'))
- input_grad: float32 [16384, 2048], P(('shard', 'rep'))
- attn_gain_grad: float32 [2048], P('shard')
- w_query_grad: float32 [2048, 2048], P('shard')
- w_key_grad: float32 [2048, 2048], P('shard')
- w_value_grad: float32 [2048, 2048], P('shard')
- query_gain_grad: float32 [2048], P('shard')
- key_gain_grad: float32 [2048], P('shard')
- w_output_grad: float32 [2048, 2048], P('shard')
- ffn_gain_grad: float32 [2048], P('shard')
- w_router_grad: float32 [2048, 64], P('shard')
- w_gate_grad: float32 [2, 2048, 1024], P(None, 'shard')
- w_up_grad: float32 [2, 2048, 1024], P(None, 'shard')
- w_down_grad: float32 [2, 1024, 2048], P(None, 'shard')
The draws below stay inside these ranges and needn't reach their ends.
Inputs may be any that keep to these rules, and one draw needn't show every extreme that they name: `expert_ids`: each row names 8 different experts. `slot_rows`: for each sequence and each expert e below 2: the entries, without repeats, are the places in the sequence of exactly the tokens whose row of expert_ids names e, in any order, followed by the filler 512; 64 or more are live, and in each sequence some expert fills all 128 slots. `doc_ids`: document numbers never fall along a sequence; a document has at most 256 tokens.
All inputs are finite; a program needn't handle non-finite values.
Results may differ from the reference program's by a relative error of at most 0.02.
Values may be sent and summed in bfloat16 or wider, within the bound.
No kernel may reach another device: no remote copies, remote signals or barrier semaphores. Data moves between devices by JAX's collectives and lax.ppermute only.
A program may use at most 320 MiB of HBM per device.

```python
import math
import jax
import jax.numpy as jnp
import numpy as np
from jax import lax

D = 2048
HEADS = 16
HEAD_DIM = 128
FF = 1024
ROUTED = 64
TOP = 8
EXPERTS = 2
TOK_DEV = 512
DOCS = 4
CAP = 128
DOC_MOST = 256
BLOCKS = 32
TOKENS = 16384


def routing_tables(key):
    base = jax.random.fold_in(key, 41)

    def one_block(block):
        block_key = jax.random.fold_in(base, block)
        count_key, full_key, perm_key, score_key, order_key = jax.random.split(block_key, 5)
        counts = jax.random.randint(count_key, (EXPERTS,), CAP // 2, CAP + 1)
        fullest = jax.random.randint(full_key, (), 0, EXPERTS)
        counts = jnp.where(jnp.arange(EXPERTS) == fullest, CAP, counts)
        perms = jax.vmap(lambda single: jax.random.permutation(single, TOK_DEV))(jax.random.split(perm_key, EXPERTS))
        live = jnp.arange(CAP)[None, :] < counts[:, None]
        slots = jnp.where(live, perms[:, :CAP], TOK_DEV).astype(jnp.int32)
        member = jnp.zeros((TOK_DEV + 1, EXPERTS), jnp.int32).at[slots, jnp.arange(EXPERTS)[:, None]].set(1)[:TOK_DEV]
        scores = jax.random.randint(score_key, (TOK_DEV, ROUTED), 0, 2 ** 20) * ROUTED + jnp.arange(ROUTED)[None, :]
        window_scores = jnp.where(member == 1, 2 ** 30, -1)
        scores = jnp.concatenate([window_scores, scores[:, EXPERTS:]], 1).astype(jnp.int32)
        top_scores, picked = lax.top_k(scores, TOP)
        order_keys = jax.random.randint(order_key, (TOK_DEV, TOP), 0, 2 ** 20) * TOP + jnp.arange(TOP)[None, :]
        order = jnp.argsort(order_keys, axis=1)
        picked = jnp.take_along_axis(picked, order, 1)
        return (picked.astype(jnp.int32), slots)
    picks, slots = jax.vmap(one_block)(jnp.arange(BLOCKS))
    return (picks.reshape(TOKENS, TOP), slots)


def draw_expert_ids(key, part):
    return routing_tables(key)[0]


def draw_slot_rows(key, part):
    return routing_tables(key)[1]


def level_of(rng, shape, cuts, low, largest):
    loudness, own = 1.0, jax.random.fold_in(rng, 6)
    for position, blocks in cuts:
        heights = jnp.exp(jax.random.uniform(jax.random.fold_in(own, position), (blocks,), jnp.float32, low / len(cuts), largest / len(cuts)))
        loudness = loudness * jnp.repeat(heights, shape[position] // blocks).reshape([-1 if axis == position else 1 for axis in range(len(shape))])
    return loudness


def profile(count, total, most, skew):
    weights = [(1 << 20) // math.isqrt(standing ** skew) + 1 for standing in range(2, count + 1)]
    spare, holding = total - most - (count - 1), [1] * (count - 1)
    while spare > 0:
        free = [i for i in range(count - 1) if holding[i] < most]
        whole, remaining = sum([weights[i] for i in free]), spare
        for i in free:
            extra = min(most - holding[i], max(1, remaining * weights[i] // whole), spare)
            holding[i] = holding[i] + extra
            spare = spare - extra
    return np.array([most] + holding)


def ragged_sizes(stream_key, count, total, limit, lean):
    if count == 2:
        one = jax.random.randint(stream_key, (), max(1, total - limit), min(limit, total - 1) + 1)
        return jnp.stack([one, total - one])
    lengths = jnp.asarray(profile(count, total, limit, lean), jnp.int32)
    twos = (count - 1) // 2
    giver, receiver = lengths[1:1 + 2 * twos:2], lengths[2:2 + 2 * twos:2]
    room = jnp.minimum(giver - 1, limit - receiver)
    moved = jax.random.randint(jax.random.fold_in(stream_key, 1), (twos,), 0, 1 << 20) % (room + 1)
    lengths = lengths.at[1:1 + 2 * twos:2].set(giver - moved).at[2:2 + 2 * twos:2].set(receiver + moved)
    return lengths[jax.random.permutation(jax.random.fold_in(stream_key, 2), count)]


def bell_draw(rng, shape, deviation, bound, cuts=(), kind=jnp.bfloat16):
    values = jax.random.normal(rng, shape, jnp.float32) * deviation
    if len(cuts) > 0:
        values = level_of(rng, shape, cuts, -0.22, 0.18) * values
    return jnp.clip(values, min=-bound, max=bound).astype(kind)


def setup_inputs(seed: int = 0) -> dict:
    seeds = jax.random.split(jax.random.key(seed), 18)
    hidden_in = bell_draw(seeds[0], (TOKENS, D), 1.0, 6.0, ((0, 32),))
    doc_ids = jax.vmap(lambda own: jnp.searchsorted(jnp.cumsum(ragged_sizes(own, DOCS, TOK_DEV, DOC_MOST, 1)), jnp.arange(TOK_DEV), side="right"))(jax.random.split(seeds[1], BLOCKS)).reshape((BLOCKS, TOK_DEV)).astype(jnp.int32)
    expert_ids = draw_expert_ids(jax.random.fold_in(seeds[17], 71), 0)
    slot_rows = draw_slot_rows(jax.random.fold_in(seeds[17], 71), 0)
    out_grad = bell_draw(seeds[4], (TOKENS, D), 1.0, 6.0, ((0, 32),))
    attn_gain = jnp.clip(1.0 + 0.1 * jax.random.normal(seeds[5], (D,), jnp.float32), 0.5, 1.5).astype(jnp.bfloat16)
    w_query = bell_draw(seeds[6], (D, D), D ** -0.5, 0.125, ((0, 8),))
    w_key = bell_draw(seeds[7], (D, D), D ** -0.5, 0.125, ((0, 8),))
    w_value = bell_draw(seeds[8], (D, D), D ** -0.5, 0.125, ((0, 8),))
    query_gain = jnp.clip(1.0 + 0.1 * jax.random.normal(seeds[9], (D,), jnp.float32), 0.5, 1.5).astype(jnp.bfloat16)
    key_gain = jnp.clip(1.0 + 0.1 * jax.random.normal(seeds[10], (D,), jnp.float32), 0.5, 1.5).astype(jnp.bfloat16)
    w_output = bell_draw(seeds[11], (D, D), (D // 32) ** -0.5, 0.75, ((0, 8),))
    ffn_gain = jnp.clip(1.0 + 0.1 * jax.random.normal(seeds[12], (D,), jnp.float32), 0.5, 1.5).astype(jnp.bfloat16)
    w_router = bell_draw(seeds[13], (D, ROUTED), (4 * D) ** -0.5, 0.0625, ((0, 8),))
    w_gate = bell_draw(seeds[14], (EXPERTS, D, FF), D ** -0.5, 0.125, ((1, 8),))
    w_up = bell_draw(seeds[15], (EXPERTS, D, FF), D ** -0.5, 0.125, ((1, 8),))
    w_down = bell_draw(seeds[16], (EXPERTS, FF, D), 4.0, 24.0, ((1, 8),))
    return {"hidden_in": hidden_in, "doc_ids": doc_ids, "expert_ids": expert_ids, "slot_rows": slot_rows, "out_grad": out_grad, "attn_gain": attn_gain, "w_query": w_query, "w_key": w_key, "w_value": w_value, "query_gain": query_gain, "key_gain": key_gain, "w_output": w_output, "ffn_gain": ffn_gain, "w_router": w_router, "w_gate": w_gate, "w_up": w_up, "w_down": w_down}


HIGH = lax.Precision.HIGHEST
EPSILON = 1e-05
THETA = 10000.0

@jax.custom_vjp
def low(v):
    return lax.optimization_barrier(v.astype(jnp.bfloat16)).astype(jnp.float32)

@jax.custom_vjp
def low_back(v):
    return v

def low_keep(v):
    return (low(v), None)

def low_pass(kept, grad):
    return (grad,)

def back_keep(v):
    return (v, None)

def back_low(kept, grad):
    return (low(grad),)
low.defvjp(low_keep, low_pass)
low_back.defvjp(back_keep, back_low)

def rms_norm(values, gain):
    return values * lax.rsqrt(lax.optimization_barrier(jnp.mean(values * values, -1, keepdims=True)) + EPSILON) * gain

def doc_places(docs):
    places = jnp.arange(docs.shape[-1], dtype=jnp.int32)
    earlier = jnp.concatenate([docs[..., :1], docs[..., :-1]], -1)
    starts = lax.cummax(jnp.where(docs != earlier, places, jnp.zeros_like(places)).astype(jnp.int32), axis=docs.ndim - 1)
    return (places - starts).astype(jnp.float32)

def rope_tables(positions, head_dim):
    half = head_dim // 2
    inverse_rates = THETA ** (-jnp.arange(half, dtype=jnp.float32) * 2.0 / head_dim)
    angles = positions[..., None] * inverse_rates
    cosine = jnp.concatenate([jnp.cos(angles), jnp.cos(angles)], -1)[..., None, :]
    sine = jnp.concatenate([jnp.sin(angles), jnp.sin(angles)], -1)[..., None, :]
    return (cosine, sine)

def rotate(values, cosine, sine):
    half = values.shape[-1] // 2
    turned = jnp.concatenate([-values[..., half:], values[..., :half]], -1)
    return values * cosine + turned * sine

def attend(pieces):
    queries, keys, values, docs = pieces
    places = jnp.arange(docs.shape[0])
    allowed = (docs[:, None] == docs[None, :]) & (places[None, :] <= places[:, None])
    scores = low_back(jnp.einsum('ihd,jhd->hij', queries, keys, precision=HIGH) * HEAD_DIM ** (-0.5))
    scores = jnp.where(allowed[None], scores, -jnp.inf)
    probs = low(jax.nn.softmax(scores, axis=-1))
    return jnp.einsum('hij,jhd->ihd', probs, values, precision=HIGH)

def forward(params, doc_ids, onehot, slot_index, cosine, sine):
    hidden, attn_gain, w_query, w_key, w_value, query_gain, key_gain, w_output, ffn_gain, w_router, w_gate, w_up, w_down = params
    tokens = hidden.shape[0]
    normed = low(rms_norm(hidden, attn_gain))
    query_raw = low_back(jnp.dot(normed, w_query, precision=HIGH))
    key_raw = low_back(jnp.dot(normed, w_key, precision=HIGH))
    values = low(low_back(jnp.dot(normed, w_value, precision=HIGH)))
    layout = (BLOCKS, TOK_DEV, HEADS, HEAD_DIM)
    queries = low(rotate(rms_norm(query_raw, query_gain).reshape(layout), cosine, sine))
    keys = low(rotate(rms_norm(key_raw, key_gain).reshape(layout), cosine, sine))
    mixed = lax.map(jax.checkpoint(attend), (queries, keys, values.reshape(layout), doc_ids))
    mixed = low(low_back(mixed.reshape(tokens, D)))
    residual = hidden + low_back(jnp.dot(mixed, w_output, precision=HIGH))
    inner = low(rms_norm(residual, ffn_gain))
    logits = low_back(jnp.dot(inner, w_router, precision=HIGH))
    probs_all = jax.nn.softmax(logits, axis=-1)
    gates = lax.optimization_barrier(jnp.sum(onehot * probs_all[:, None, :], -1))
    window = lax.optimization_barrier(jnp.sum(gates[:, :, None] * onehot[:, :, :EXPERTS], 1))
    inner_pad = jnp.concatenate([inner, jnp.zeros((1, D), jnp.float32)], 0)
    window_pad = jnp.concatenate([window, jnp.zeros((1, EXPERTS), jnp.float32)], 0)
    slot_inputs = inner_pad[slot_index]
    slot_gates = window_pad[slot_index, jnp.arange(EXPERTS)[:, None]]
    gate_part = low_back(jnp.einsum('erd,edf->erf', slot_inputs, w_gate, precision=HIGH))
    up_part = low_back(jnp.einsum('erd,edf->erf', slot_inputs, w_up, precision=HIGH))
    activated = low(jax.nn.silu(gate_part) * up_part)
    returned = low_back(jnp.einsum('erf,efd->erd', activated, w_down, precision=HIGH))
    experts_sum = jnp.zeros((tokens + 1, D), jnp.float32).at[slot_index].add(slot_gates[:, :, None] * returned)
    return residual + experts_sum[:tokens]

def reference(hidden_in, doc_ids, expert_ids, slot_rows, out_grad, attn_gain, w_query, w_key, w_value, query_gain, key_gain, w_output, ffn_gain, w_router, w_gate, w_up, w_down):
    onehot = (expert_ids[:, :, None] == jnp.arange(ROUTED, dtype=jnp.int32)[None, None, :]).astype(jnp.float32)
    offsets = (jnp.arange(BLOCKS) * TOK_DEV).astype(jnp.int32)
    global_rows = jnp.where(slot_rows < TOK_DEV, slot_rows + offsets[:, None, None], TOKENS).astype(jnp.int32)
    slot_index = jnp.transpose(global_rows, (1, 0, 2)).reshape(EXPERTS, BLOCKS * CAP)
    cosine, sine = rope_tables(doc_places(doc_ids), HEAD_DIM)
    params = tuple((array.astype(jnp.float32) for array in (hidden_in, attn_gain, w_query, w_key, w_value, query_gain, key_gain, w_output, ffn_gain, w_router, w_gate, w_up, w_down)))
    output, pullback = jax.vjp(lambda *items: forward(items, doc_ids, onehot, slot_index, cosine, sine), *params)
    grads = pullback(out_grad.astype(jnp.float32))
    return (output.astype(jnp.bfloat16), grads[0], grads[1], grads[2], grads[3], grads[4], grads[5], grads[6], grads[7], grads[8], grads[9], grads[10], grads[11], grads[12])
```

```python
import functools

import jax
import jax.numpy as jnp
from jax import lax
from jax.experimental import pallas as pl
from jax.experimental.pallas import tpu as pltpu
from jax.sharding import PartitionSpec as P

HEADS = 16
EPSILON = 1e-05
THETA = 10000.0
REACH = 2
ROWS = 128
F32 = jnp.float32
BF16 = jnp.bfloat16


def rms_scale(values):
    return lax.rsqrt(jnp.mean(values * values, -1, keepdims=True) + EPSILON)


def norm_back(values, scale, gain, upstream):
    gain_grad = jnp.sum(upstream * values * scale, 0)
    weighted = upstream * gain
    inner_mean = jnp.mean(weighted * values, -1, keepdims=True)
    return (scale * weighted - values * scale * scale * scale * inner_mean, gain_grad)


def dot(a, b, dims=((1,), (0,))):
    return lax.dot_general(a, b, (dims, ((), ())), preferred_element_type=F32)


def swap(x, mask):
    return lax.ppermute(x, "rep", [(i, i ^ mask) for i in range(4)])


def flip(x, mask):
    return jnp.stack([x[j ^ mask] for j in range(4)])


def rep_sum(x):
    x = x + flip(swap(x, 1), 1)
    return x + flip(swap(x, 2), 2)


def rep_gather(x):
    one, two = swap(x, 1), swap(x, 2)
    return [x, one, two, swap(two, 1)]


def in_order(pieces, rep):
    low = rep % 2 == 1
    high = rep // 2 == 1
    a, b, c, d = pieces
    a, b = jnp.where(low, b, a), jnp.where(low, a, b)
    c, d = jnp.where(low, d, c), jnp.where(low, c, d)
    return (
        jnp.where(high, c, a),
        jnp.where(high, d, b),
        jnp.where(high, a, c),
        jnp.where(high, b, d),
    )


def mask_bias(bias, doc_col, doc_row):
    length = doc_col.shape[0]
    rows = lax.broadcasted_iota(jnp.int32, (length, length), 0)
    cols = lax.broadcasted_iota(jnp.int32, (length, length), 1)
    allowed = (doc_col[...] == doc_row[0]) & (cols <= rows)
    bias[...] = jnp.where(allowed, 0.0, -jnp.inf).astype(F32)


def turn(values, cosine, sine):
    half = values.shape[-1] // 2
    lanes = lax.broadcasted_iota(jnp.int32, values.shape, 1)
    turned = jnp.where(lanes < half, -1.0, 1.0) * pltpu.roll(values, half, 1)
    return values * cosine + turned * sine


def turn_back(values, cosine, sine):
    half = values.shape[-1] // 2
    lanes = lax.broadcasted_iota(jnp.int32, values.shape, 1)
    moved = pltpu.roll(values * sine, half, 1)
    return values * cosine + jnp.where(lanes < half, 1.0, -1.0) * moved


def spans(length):
    return [
        (i * ROWS, (i + 1) * ROWS, max(0, (i - REACH) * ROWS)) for i in range(length // ROWS)
    ]


def attend_kernel(
    factor,
    q_ref,
    k_ref,
    v_ref,
    q_scale,
    k_scale,
    q_gain,
    k_gain,
    cosine,
    sine,
    doc_col,
    doc_row,
    mixed_ref,
    queries_ref,
    keys_ref,
    values_ref,
    bias,
):
    @pl.when(pl.program_id(1) == 0)
    def _():
        mask_bias(bias, doc_col, doc_row)

    cos, sin = cosine[...], sine[...]
    queries_ref[...] = turn(q_ref[...] * q_scale[...] * q_gain[...], cos, sin).astype(BF16)
    keys_ref[...] = turn(k_ref[...] * k_scale[...] * k_gain[...], cos, sin).astype(BF16)
    values_ref[...] = v_ref[...].astype(BF16)
    for start, end, low in spans(q_ref.shape[0]):
        scores = dot(queries_ref[start:end], keys_ref[low:end], ((1,), (1,))) * factor
        scores = scores + bias[start:end, low:end]
        weights = jnp.exp(scores - jnp.max(scores, -1, keepdims=True))
        probs = (weights * (1.0 / jnp.sum(weights, -1, keepdims=True))).astype(BF16)
        mixed_ref[start:end] = dot(probs, values_ref[low:end]).astype(BF16)


def attend_back_kernel(
    factor,
    queries,
    keys,
    values,
    grads,
    cosine,
    sine,
    doc_col,
    doc_row,
    dq_ref,
    dk_ref,
    dv_ref,
    bias,
    dk_sum,
    dv_sum,
):
    @pl.when(pl.program_id(1) == 0)
    def _():
        mask_bias(bias, doc_col, doc_row)

    cos, sin = cosine[...], sine[...]
    dk_sum[...] = jnp.zeros_like(dk_sum)
    dv_sum[...] = jnp.zeros_like(dv_sum)
    for start, end, low in spans(queries.shape[0]):
        q, g = queries[start:end], grads[start:end]
        k, v = keys[low:end], values[low:end]
        scores = dot(q, k, ((1,), (1,))) * factor + bias[start:end, low:end]
        weights = jnp.exp(scores - jnp.max(scores, -1, keepdims=True))
        probs = weights * (1.0 / jnp.sum(weights, -1, keepdims=True))
        dv_sum[low:end] += dot(probs.astype(BF16), g, ((0,), (0,)))
        prob_grad = dot(g, v, ((1,), (1,)))
        score_grad = probs * (prob_grad - jnp.sum(probs * prob_grad, -1, keepdims=True))
        score_grad = score_grad.astype(BF16)
        dq_ref[start:end] = turn_back(dot(score_grad, k) * factor, cos[start:end], sin[start:end])
        dk_sum[low:end] += dot(score_grad, q, ((0,), (0,)))
    dk_ref[...] = turn_back(dk_sum[...] * factor, cos, sin)
    dv_ref[...] = dv_sum[...].astype(BF16)


def cost(flops, moved, exps=0):
    return pl.CostEstimate(flops=flops, bytes_accessed=moved, transcendentals=exps)


def attend(qkv, q_scale, k_scale, q_gain, k_gain, cosine, sine, doc_col, doc_row, heads, dim):
    tokens = qkv.shape[0]
    length = doc_row.shape[-1]
    block = lambda off: pl.BlockSpec((length, dim), lambda j, h: (j, off + h))
    per_row = pl.BlockSpec((length, 1), lambda j, h: (j, 0))
    table = pl.BlockSpec((length, dim), lambda j, h: (j, 0))
    gain = pl.BlockSpec((1, dim), lambda j, h: (0, h))
    row = pl.BlockSpec((1, 1, length), lambda j, h: (j, 0, 0))
    out = jax.ShapeDtypeStruct((tokens, heads * dim), BF16)
    return pl.pallas_call(
        functools.partial(attend_kernel, dim ** (-0.5)),
        grid=(tokens // length, heads),
        in_specs=[block(0), block(heads), block(2 * heads), per_row, per_row, gain, gain]
        + [table, table, per_row, row],
        out_specs=[block(0)] * 4,
        out_shape=[out] * 4,
        scratch_shapes=[pltpu.VMEM((length, length), F32)],
        cost_estimate=cost(
            4 * tokens * length * heads * dim, tokens * heads * dim * 20, tokens * length * heads
        ),
        name="attend",
    )(qkv, qkv, qkv, q_scale, k_scale, q_gain, k_gain, cosine, sine, doc_col, doc_row)


def attend_back(queries, keys, values, grads, cosine, sine, doc_col, doc_row, heads, dim):
    tokens = queries.shape[0]
    length = doc_row.shape[-1]
    block = pl.BlockSpec((length, dim), lambda j, h: (j, h))
    per_row = pl.BlockSpec((length, 1), lambda j, h: (j, 0))
    table = pl.BlockSpec((length, dim), lambda j, h: (j, 0))
    row = pl.BlockSpec((1, 1, length), lambda j, h: (j, 0, 0))
    wide = jax.ShapeDtypeStruct((tokens, heads * dim), F32)
    return pl.pallas_call(
        functools.partial(attend_back_kernel, dim ** (-0.5)),
        grid=(tokens // length, heads),
        in_specs=[block] * 4 + [table, table, per_row, row],
        out_specs=[block] * 3,
        out_shape=[wide, wide, jax.ShapeDtypeStruct((tokens, heads * dim), BF16)],
        scratch_shapes=[
            pltpu.VMEM((length, length), F32),
            pltpu.VMEM((length, dim), F32),
            pltpu.VMEM((length, dim), F32),
        ],
        cost_estimate=cost(
            10 * tokens * length * heads * dim, tokens * heads * dim * 18, tokens * length * heads
        ),
        name="attend_back",
    )(queries, keys, values, grads, cosine, sine, doc_col, doc_row)


def shard_gather(x):
    return lax.all_gather(x, "shard", axis=0, tiled=True)


def shard_scatter(x):
    return lax.psum_scatter(x, "shard", scatter_dimension=0, tiled=True).astype(F32)


def split_sum(x):
    high = x.astype(BF16)
    return high, (x - high.astype(F32)).astype(BF16)


def local(
    n_shard,
    hidden_in,
    doc_ids,
    expert_ids,
    slot_rows,
    out_grad,
    attn_gain,
    w_query,
    w_key,
    w_value,
    query_gain,
    key_gain,
    w_output,
    ffn_gain,
    w_router,
    w_gate,
    w_up,
    w_down,
):
    length, width = hidden_in.shape
    dim = width // HEADS
    heads = HEADS // 4
    part = width // 4
    routed = w_router.shape[1]
    experts = w_gate.shape[0]
    hidden_units = w_gate.shape[2]
    half_units = hidden_units // 2
    cap = slot_rows.shape[2]
    rep = lax.axis_index("rep")
    shard = lax.axis_index("shard")
    core, side = rep % 2, rep // 2
    my_rows = width // n_shard
    quarter = my_rows // 4

    cut = lambda w: lax.dynamic_slice_in_dim(w, rep * part, part, 1)
    qkv_block = jnp.concatenate([cut(w_query), cut(w_key), cut(w_value)], 1)
    output_block = lax.dynamic_slice_in_dim(w_output, rep * quarter, quarter, 0)
    pick = lambda w: lax.dynamic_index_in_dim(w, core, 0, keepdims=False)
    down_rows = hidden_units // n_shard
    unit = jnp.arange(half_units)
    unit = (unit // (down_rows // 2)) * down_rows + unit % (down_rows // 2)
    choose = lambda which: (
        jnp.arange(hidden_units)[:, None] == (unit + which * (down_rows // 2))[None, :]
    ).astype(BF16)
    mine = choose(side)
    gate_up_block = jnp.concatenate(
        [dot(pick(w_gate), mine).astype(BF16), dot(pick(w_up), mine).astype(BF16)], 1
    )
    down_block = lax.dynamic_slice_in_dim(pick(w_down), side * (down_rows // 2), down_rows // 2, 0)
    w_qkv = shard_gather(qkv_block)
    gains = lax.all_gather(
        jnp.stack([attn_gain, query_gain, key_gain, ffn_gain]), "shard", axis=1, tiled=True
    ).astype(F32)
    router_w = shard_gather(w_router)
    w_out_part = shard_gather(output_block).reshape(n_shard, quarter, width)
    w_gu = shard_gather(gate_up_block)
    w_dn = shard_gather(down_block)
    gain_one, gain_two = gains[0], gains[3]
    gain_query = lax.dynamic_slice_in_dim(gains[1:2], rep * part, part, 1)
    gain_key = lax.dynamic_slice_in_dim(gains[2:3], rep * part, part, 1)
    output_w = jnp.stack(in_order(rep_gather(w_out_part), rep), 1).reshape(width, width)

    hidden_all = jnp.concatenate(rep_gather(hidden_in), 0)
    docs_all = jnp.concatenate(rep_gather(doc_ids), 0)
    slots = slot_rows[0].reshape(experts * cap)
    select = (slots[:, None] == jnp.arange(length, dtype=jnp.int32)[None, :]).astype(BF16)
    upstream = out_grad.astype(F32)

    def to_experts(x):
        own = lax.dynamic_index_in_dim(x, core, 0, keepdims=False)
        other = lax.dynamic_index_in_dim(x, 1 - core, 0, keepdims=False)
        pair = jnp.stack([own, swap(other, 1)])
        return jnp.concatenate([pair, swap(pair, 2)], 0)

    def from_experts(x, send):
        pair = x[:2] + swap(x[2:].astype(send), 2).astype(F32)
        other = swap(pair[1].astype(send), 1).astype(F32)
        first = jnp.where(core == 0, pair[0], other)
        return jnp.stack([first, jnp.where(core == 0, other, pair[0])])

    def add_slots(x):
        high, low = split_sum(x.reshape(experts * cap, width))
        return dot(select, high, ((0,), (0,))) + dot(select, low, ((0,), (0,)))

    slot_upstream = to_experts(dot(select, out_grad).astype(BF16).reshape(experts, cap, width))

    normed_scale = rms_scale(hidden_all.astype(F32))
    normed = (hidden_all.astype(F32) * normed_scale * gain_one).astype(BF16)
    before = docs_all[:, None, :] < docs_all[:, :, None]
    starts = jnp.sum(before.astype(jnp.int32), -1)
    places = (jnp.arange(length, dtype=jnp.int32)[None, :] - starts).astype(F32).reshape(-1)
    rates = THETA ** (-jnp.arange(dim // 2, dtype=F32) * 2.0 / dim)
    angles = places[:, None] * jnp.concatenate([rates, rates])[None, :]
    cosine, sine = jnp.cos(angles), jnp.sin(angles)
    doc_col = docs_all.reshape(-1, 1)
    doc_row = docs_all.reshape(4, 1, length)

    qkv = dot(normed, w_qkv)
    query_raw, key_raw = qkv[:, :part], qkv[:, part : 2 * part]
    squares = jnp.stack([jnp.sum(query_raw * query_raw, -1), jnp.sum(key_raw * key_raw, -1)], -1)
    squares = rep_sum(squares.reshape(4, length, 2)).reshape(-1, 2)
    scales = lax.rsqrt(squares / width + EPSILON)
    query_scale, key_scale = scales[:, :1], scales[:, 1:]
    mixed_heads, queries, keys, values = attend(
        qkv,
        query_scale,
        key_scale,
        gain_query,
        gain_key,
        cosine,
        sine,
        doc_col,
        doc_row,
        heads,
        dim,
    )
    blocks = mixed_heads.reshape(4, length, part)
    from_side = swap(blocks[2:], 2)
    mixed = jnp.concatenate(
        in_order([blocks[0], swap(blocks[1], 1), from_side[0], swap(from_side[1], 1)], rep), 1
    )
    hidden = hidden_in.astype(F32)
    residual = hidden + dot(mixed, output_w)
    scale_two = rms_scale(residual)
    inner = (residual * scale_two * gain_two).astype(BF16)
    logits = dot(inner, router_w)
    probs_all = jax.nn.softmax(logits, axis=-1)
    named = jnp.sum(
        (expert_ids[:, :, None] == jnp.arange(experts, dtype=jnp.int32)).astype(F32), 1
    )
    window = probs_all[:, :experts] * named
    select_wide = select.reshape(experts, cap, length).astype(F32)
    slot_gates = to_experts(jnp.sum(select_wide * window.T[:, None, :], -1))
    slot_inputs = to_experts(dot(select, inner).astype(BF16).reshape(experts, cap, width))
    slot_inputs = slot_inputs.reshape(4 * cap, width)

    gate_up = dot(slot_inputs, w_gu)
    gate_part, up_part = gate_up[:, :half_units], gate_up[:, half_units:]
    sigma = jax.nn.sigmoid(gate_part)
    swished = gate_part * sigma
    activated = (swished * up_part).astype(BF16)
    returned = dot(activated, w_dn).reshape(4, cap, width)
    slot_gate_grad = from_experts(jnp.sum(returned * slot_upstream.astype(F32), -1), F32)
    returned_grad = (slot_gates[:, :, None] * slot_upstream.astype(F32)).astype(BF16)
    returned_grad = returned_grad.reshape(4 * cap, width)
    act_grad = dot(returned_grad, w_dn, ((1,), (1,)))
    gate_grad = act_grad * up_part * sigma * (1.0 + gate_part * (1.0 - sigma))
    gate_up_grad = jnp.concatenate([gate_grad.astype(BF16), (act_grad * swished).astype(BF16)], 1)
    slot_input_grad = dot(gate_up_grad, w_gu, ((1,), (1,))).reshape(4, cap, width)
    slot_input_grad = from_experts(slot_input_grad, BF16)
    down_owned = shard_scatter(dot(activated, returned_grad, ((0,), (0,))).astype(BF16))
    gate_up_owned = shard_scatter(dot(slot_inputs, gate_up_grad, ((0,), (0,))).astype(BF16))
    own_gates = jnp.sum(select_wide * window.T[:, None, :], -1)
    returned = from_experts(returned, BF16)
    output = (residual + add_slots(own_gates[:, :, None] * returned)).astype(BF16)

    window_grad = jnp.sum(select_wide * slot_gate_grad[:, :, None], 1).T
    chosen_grad = jnp.concatenate(
        [window_grad * named, jnp.zeros((length, routed - experts), F32)], 1
    )
    logits_grad = (
        probs_all * (chosen_grad - jnp.sum(probs_all * chosen_grad, -1, keepdims=True))
    ).astype(BF16)
    router_grad = dot(logits_grad, inner, ((0,), (0,)))
    inner_grad = add_slots(slot_input_grad) + dot(logits_grad, router_w, ((1,), (1,)))
    residual_part, gain_two_grad = norm_back(residual, scale_two, gain_two, inner_grad)
    residual_grad = upstream + residual_part
    branch_grad = residual_grad.astype(BF16)
    mixed_grad = dot(branch_grad, output_w, ((1,), (1,))).astype(BF16)
    piece = lambda j: lax.dynamic_slice_in_dim(mixed_grad, (rep ^ j) * part, part, 1)
    from_side = swap(jnp.stack([piece(2), piece(3)]), 2)
    grads = jnp.concatenate([piece(0), swap(piece(1), 1), from_side[0], swap(from_side[1], 1)], 0)
    out_w_grad = dot(mixed, branch_grad, ((0,), (0,))).astype(BF16)
    out_w_grad = out_w_grad.reshape(n_shard, 2, 2, quarter, width)
    at = lambda x, i, axis: lax.dynamic_index_in_dim(x, i, axis, keepdims=False)
    out_w_grad = at(out_w_grad, core, 2).astype(F32) + swap(at(out_w_grad, 1 - core, 2), 1)
    out_w_grad = out_w_grad.astype(BF16)
    out_w_grad = at(out_w_grad, side, 1).astype(F32) + swap(at(out_w_grad, 1 - side, 1), 2)
    out_owned = shard_scatter(out_w_grad.astype(BF16).reshape(n_shard * quarter, width))

    query_grad, key_grad, value_grad = attend_back(
        queries, keys, values, grads, cosine, sine, doc_col, doc_row, heads, dim
    )
    weighted_q, weighted_k = query_grad * gain_query, key_grad * gain_key
    means = jnp.stack(
        [jnp.sum(weighted_q * query_raw, -1), jnp.sum(weighted_k * key_raw, -1)], -1
    )
    means = rep_sum(means.reshape(4, length, 2)).reshape(-1, 2) / width
    gain_query_grad = jnp.sum(query_grad * query_raw * query_scale, 0)
    gain_key_grad = jnp.sum(key_grad * key_raw * key_scale, 0)
    query_raw_grad = query_scale * weighted_q - query_raw * query_scale**3 * means[:, :1]
    key_raw_grad = key_scale * weighted_k - key_raw * key_scale**3 * means[:, 1:]
    qkv_grad = jnp.concatenate(
        [query_raw_grad.astype(BF16), key_raw_grad.astype(BF16), value_grad], 1
    )
    qkv_owned = shard_scatter(dot(normed, qkv_grad, ((0,), (0,))).astype(BF16))
    normed_grad = dot(qkv_grad, w_qkv, ((1,), (1,)))
    gain_one_grad = jnp.sum(normed_grad * hidden_all.astype(F32) * normed_scale, 0)
    normed_grad = normed_grad.reshape(4, length, width)
    from_core = swap(normed_grad[1::2].astype(BF16), 1).astype(F32)
    pair_two = (normed_grad[2] + from_core[1]).astype(BF16)
    normed_grad = normed_grad[0] + from_core[0] + swap(pair_two, 2).astype(F32)
    weighted = normed_grad * gain_one
    scale_one = normed_scale[:length]
    inner_mean = jnp.mean(weighted * hidden, -1, keepdims=True)
    hidden_part = scale_one * weighted - hidden * scale_one * scale_one * scale_one * inner_mean
    input_grad = residual_grad + hidden_part

    place = lambda g: lax.dynamic_update_slice_in_dim(
        jnp.zeros((1, width), F32), g[None], rep * part, 1
    )
    small = jnp.concatenate(
        [
            router_grad,
            gain_one_grad[None],
            place(gain_query_grad),
            place(gain_key_grad),
            gain_two_grad[None],
            jnp.zeros((4, width), F32),
        ],
        0,
    )
    small = lax.psum(small, ("shard", "rep"))
    small = lax.dynamic_slice_in_dim(small, shard * my_rows, my_rows, 1)
    qkv_pieces = in_order(rep_gather(qkv_owned.astype(BF16)), rep)
    spread = lambda i: jnp.concatenate(
        [p[:, i * part : (i + 1) * part] for p in qkv_pieces], 1
    ).astype(F32)
    out_full = jnp.concatenate(in_order(rep_gather(out_owned.astype(BF16)), rep), 0).astype(F32)
    gu_pieces = in_order(rep_gather(gate_up_owned.astype(BF16)), rep)
    dn_pieces = in_order(rep_gather(down_owned.astype(BF16)), rep)
    one, two = choose(0), choose(1)
    join = lambda i: jnp.stack(
        [
            dot(gu_pieces[e][:, i * half_units : (i + 1) * half_units], one, ((1,), (1,)))
            + dot(gu_pieces[2 + e][:, i * half_units : (i + 1) * half_units], two, ((1,), (1,)))
            for e in range(experts)
        ]
    )
    down_full = jnp.stack(
        [jnp.concatenate([dn_pieces[e], dn_pieces[2 + e]], 0) for e in range(experts)]
    ).astype(F32)
    return (
        output,
        input_grad,
        small[routed],
        spread(0),
        spread(1),
        spread(2),
        small[routed + 1],
        small[routed + 2],
        out_full,
        small[routed + 3],
        small[:routed].T,
        join(0),
        join(1),
        down_full,
    )


def solution(mesh):
    tokens = P(("shard", "rep"), None)
    rows = P("shard", None)
    middle = P(None, "shard", None)
    return jax.shard_map(
        functools.partial(local, mesh.shape["shard"]),
        mesh=mesh,
        in_specs=(
            tokens,
            tokens,
            tokens,
            P(("shard", "rep"), None, None),
            tokens,
            P("shard"),
            rows,
            rows,
            rows,
            P("shard"),
            P("shard"),
            rows,
            P("shard"),
            rows,
            middle,
            middle,
            middle,
        ),
        out_specs=(
            tokens,
            tokens,
            P("shard"),
            rows,
            rows,
            rows,
            P("shard"),
            P("shard"),
            rows,
            P("shard"),
            rows,
            middle,
            middle,
            middle,
        ),
        check_vma=False,
    )
```

```python
import functools

import jax
import jax.numpy as jnp
from jax import lax
from jax.experimental import pallas as pl
from jax.experimental.pallas import tpu as pltpu
from jax.sharding import PartitionSpec as P

HEADS = 16
EPSILON = 1e-05
THETA = 10000.0
REACH = 2
ROWS = 128
F32 = jnp.float32
BF16 = jnp.bfloat16


def rms_scale(values):
    return lax.rsqrt(jnp.mean(values * values, -1, keepdims=True) + EPSILON)


def norm_back(values, scale, gain, upstream):
    gain_grad = jnp.sum(upstream * values * scale, 0)
    weighted = upstream * gain
    inner_mean = jnp.mean(weighted * values, -1, keepdims=True)
    return (scale * weighted - values * scale * scale * scale * inner_mean, gain_grad)


def dot(a, b, dims=((1,), (0,))):
    return lax.dot_general(a, b, (dims, ((), ())), preferred_element_type=F32)


def swap(x, mask):
    return lax.ppermute(x, "rep", [(i, i ^ mask) for i in range(4)])


def flip(x, mask):
    return jnp.stack([x[j ^ mask] for j in range(4)])


def rep_sum(x):
    x = x + flip(swap(x, 1), 1)
    return x + flip(swap(x, 2), 2)


def rep_gather(x):
    one, two = swap(x, 1), swap(x, 2)
    return [x, one, two, swap(two, 1)]


def in_order(pieces, rep):
    low = rep % 2 == 1
    high = rep // 2 == 1
    a, b, c, d = pieces
    a, b = jnp.where(low, b, a), jnp.where(low, a, b)
    c, d = jnp.where(low, d, c), jnp.where(low, c, d)
    return (
        jnp.where(high, c, a),
        jnp.where(high, d, b),
        jnp.where(high, a, c),
        jnp.where(high, b, d),
    )


def mask_bias(bias, doc_col, doc_row):
    length = doc_col.shape[0]
    rows = lax.broadcasted_iota(jnp.int32, (length, length), 0)
    cols = lax.broadcasted_iota(jnp.int32, (length, length), 1)
    allowed = (doc_col[...] == doc_row[0]) & (cols <= rows)
    bias[...] = jnp.where(allowed, 0.0, -jnp.inf).astype(F32)


def turn(values, cosine, sine):
    half = values.shape[-1] // 2
    lanes = lax.broadcasted_iota(jnp.int32, values.shape, 1)
    turned = jnp.where(lanes < half, -1.0, 1.0) * pltpu.roll(values, half, 1)
    return values * cosine + turned * sine


def turn_back(values, cosine, sine):
    half = values.shape[-1] // 2
    lanes = lax.broadcasted_iota(jnp.int32, values.shape, 1)
    moved = pltpu.roll(values * sine, half, 1)
    return values * cosine + jnp.where(lanes < half, 1.0, -1.0) * moved


def spans(length):
    return [
        (i * ROWS, (i + 1) * ROWS, max(0, (i - REACH) * ROWS)) for i in range(length // ROWS)
    ]


def attend_kernel(
    factor,
    q_ref,
    k_ref,
    v_ref,
    q_scale,
    k_scale,
    q_gain,
    k_gain,
    cosine,
    sine,
    doc_col,
    doc_row,
    mixed_ref,
    queries_ref,
    keys_ref,
    values_ref,
    bias,
):
    @pl.when(pl.program_id(1) == 0)
    def _():
        mask_bias(bias, doc_col, doc_row)

    cos, sin = cosine[...], sine[...]
    queries_ref[...] = turn(q_ref[...] * q_scale[...] * q_gain[...], cos, sin).astype(BF16)
    keys_ref[...] = turn(k_ref[...] * k_scale[...] * k_gain[...], cos, sin).astype(BF16)
    values_ref[...] = v_ref[...].astype(BF16)
    for start, end, low in spans(q_ref.shape[0]):
        scores = dot(queries_ref[start:end], keys_ref[low:end], ((1,), (1,))) * factor
        scores = scores + bias[start:end, low:end]
        weights = jnp.exp(scores - jnp.max(scores, -1, keepdims=True))
        probs = (weights * (1.0 / jnp.sum(weights, -1, keepdims=True))).astype(BF16)
        mixed_ref[start:end] = dot(probs, values_ref[low:end]).astype(BF16)


def attend_back_kernel(
    factor,
    queries,
    keys,
    values,
    grads,
    cosine,
    sine,
    doc_col,
    doc_row,
    dq_ref,
    dk_ref,
    dv_ref,
    bias,
    dk_sum,
    dv_sum,
):
    @pl.when(pl.program_id(1) == 0)
    def _():
        mask_bias(bias, doc_col, doc_row)

    cos, sin = cosine[...], sine[...]
    dk_sum[...] = jnp.zeros_like(dk_sum)
    dv_sum[...] = jnp.zeros_like(dv_sum)
    for start, end, low in spans(queries.shape[0]):
        q, g = queries[start:end], grads[start:end]
        k, v = keys[low:end], values[low:end]
        scores = dot(q, k, ((1,), (1,))) * factor + bias[start:end, low:end]
        weights = jnp.exp(scores - jnp.max(scores, -1, keepdims=True))
        probs = weights * (1.0 / jnp.sum(weights, -1, keepdims=True))
        dv_sum[low:end] += dot(probs.astype(BF16), g, ((0,), (0,)))
        prob_grad = dot(g, v, ((1,), (1,)))
        score_grad = probs * (prob_grad - jnp.sum(probs * prob_grad, -1, keepdims=True))
        score_grad = score_grad.astype(BF16)
        dq_ref[start:end] = turn_back(dot(score_grad, k) * factor, cos[start:end], sin[start:end])
        dk_sum[low:end] += dot(score_grad, q, ((0,), (0,)))
    dk_ref[...] = turn_back(dk_sum[...] * factor, cos, sin)
    dv_ref[...] = dv_sum[...].astype(BF16)


def cost(flops, moved, exps=0):
    return pl.CostEstimate(flops=flops, bytes_accessed=moved, transcendentals=exps)


def attend(qkv, q_scale, k_scale, q_gain, k_gain, cosine, sine, doc_col, doc_row, heads, dim):
    tokens = qkv.shape[0]
    length = doc_row.shape[-1]
    block = lambda off: pl.BlockSpec((length, dim), lambda j, h: (j, off + h))
    per_row = pl.BlockSpec((length, 1), lambda j, h: (j, 0))
    table = pl.BlockSpec((length, dim), lambda j, h: (j, 0))
    gain = pl.BlockSpec((1, dim), lambda j, h: (0, h))
    row = pl.BlockSpec((1, 1, length), lambda j, h: (j, 0, 0))
    out = jax.ShapeDtypeStruct((tokens, heads * dim), BF16)
    return pl.pallas_call(
        functools.partial(attend_kernel, dim ** (-0.5)),
        grid=(tokens // length, heads),
        in_specs=[block(0), block(heads), block(2 * heads), per_row, per_row, gain, gain]
        + [table, table, per_row, row],
        out_specs=[block(0)] * 4,
        out_shape=[out] * 4,
        scratch_shapes=[pltpu.VMEM((length, length), F32)],
        cost_estimate=cost(
            4 * tokens * length * heads * dim, tokens * heads * dim * 20, tokens * length * heads
        ),
        name="attend",
    )(qkv, qkv, qkv, q_scale, k_scale, q_gain, k_gain, cosine, sine, doc_col, doc_row)


def attend_back(queries, keys, values, grads, cosine, sine, doc_col, doc_row, heads, dim):
    tokens = queries.shape[0]
    length = doc_row.shape[-1]
    block = pl.BlockSpec((length, dim), lambda j, h: (j, h))
    per_row = pl.BlockSpec((length, 1), lambda j, h: (j, 0))
    table = pl.BlockSpec((length, dim), lambda j, h: (j, 0))
    row = pl.BlockSpec((1, 1, length), lambda j, h: (j, 0, 0))
    wide = jax.ShapeDtypeStruct((tokens, heads * dim), F32)
    return pl.pallas_call(
        functools.partial(attend_back_kernel, dim ** (-0.5)),
        grid=(tokens // length, heads),
        in_specs=[block] * 4 + [table, table, per_row, row],
        out_specs=[block] * 3,
        out_shape=[wide, wide, jax.ShapeDtypeStruct((tokens, heads * dim), BF16)],
        scratch_shapes=[
            pltpu.VMEM((length, length), F32),
            pltpu.VMEM((length, dim), F32),
            pltpu.VMEM((length, dim), F32),
        ],
        cost_estimate=cost(
            10 * tokens * length * heads * dim, tokens * heads * dim * 18, tokens * length * heads
        ),
        name="attend_back",
    )(queries, keys, values, grads, cosine, sine, doc_col, doc_row)


def tie(*arrays):
    return lax.optimization_barrier(arrays)


def ring_of(n):
    return list(range(0, n, 2)) + list(range(n - 1, 0, -2))


def ring_step(x, n, back=False):
    ring = ring_of(n)
    pairs = [(ring[i], ring[(i + 1) % n]) for i in range(n)]
    return lax.ppermute(x, "shard", [(b, a) for a, b in pairs] if back else pairs)


def ring_ids(n, shard):
    ring = ring_of(n)
    places = jnp.asarray([ring.index(i) for i in range(n)], jnp.int32)
    return jnp.asarray(ring, jnp.int32)[(places[shard] + jnp.arange(n, dtype=jnp.int32)) % n]


def ring_gather(block, n, due):
    half = block.shape[0] // 2
    pieces = [(block, 0, 0)]
    ahead = behind = block
    for k in range(1, n // 2):
        behind, ahead = tie(ring_step(behind, n), ring_step(ahead, n, True))
        if k == n // 2 - 1:
            behind, ahead, *due = tie(behind, ahead, *due)
        pieces += [(behind, n - k, 0), (ahead, k, 0)]
    pieces.append((ring_step(behind[:half], n), n // 2, 0))
    pieces.append((ring_step(ahead[half:], n, True), n // 2, half))
    return pieces, due


def place_kernel(n, cut, starts, *refs):
    ins, outs, bufs = refs[:n], refs[n : n + 2], refs[n + 2 : 2 * n + 2]
    sem_in, sem_out = refs[-2], refs[-1]
    loads = [pltpu.make_async_copy(ins[i], bufs[i], sem_in.at[i]) for i in range(n)]
    for load in loads:
        load.start()
    stores = []
    for i in range(n):
        loads[i].wait()
        at = pl.multiple_of(starts[i], 16)
        rows, cols = bufs[i].shape
        for o, first, size in ((0, 0, cut), (1, cut, cols - cut)):
            stores.append(
                pltpu.make_async_copy(
                    bufs[i].at[:, pl.ds(first, size)],
                    outs[o].at[pl.ds(at, rows)],
                    sem_out.at[2 * i + o],
                )
            )
            stores[-1].start()
    for store in stores:
        store.wait()


def place_rows(pieces, starts, rows, cut):
    cols = pieces[0].shape[1]
    n = len(pieces)
    anywhere = pl.BlockSpec(memory_space=pl.ANY)
    return pl.pallas_call(
        functools.partial(place_kernel, n, cut),
        grid_spec=pltpu.PrefetchScalarGridSpec(
            num_scalar_prefetch=1,
            grid=(),
            in_specs=[anywhere] * n,
            out_specs=[anywhere] * 2,
            scratch_shapes=[pltpu.VMEM(x.shape, x.dtype) for x in pieces]
            + [pltpu.SemaphoreType.DMA((n,)), pltpu.SemaphoreType.DMA((2 * n,))],
        ),
        out_shape=[
            jax.ShapeDtypeStruct((rows, size), pieces[0].dtype) for size in (cut, cols - cut)
        ],
        cost_estimate=cost(0, 4 * rows * cols),
        name="place_rows",
    )(starts, *pieces)


def ring_scatter(parts, n, shard, due):
    rows = parts[0].shape[0] // n
    half = rows // 2
    ids = ring_ids(n, shard)
    chunk = lambda k, first=0, size=rows: jnp.concatenate(
        [lax.dynamic_slice_in_dim(x, ids[k % n] * rows + first, size, 0) for x in parts], 1
    )
    done = []
    ahead = ring_step(chunk(n // 2, 0, half), n)
    behind = ring_step(chunk(n // 2, half, half), n, True)
    for k in range(n // 2 - 1, -1, -1):
        at = n // 2 - 1 - k
        ahead, behind, *got = tie(ahead, behind, *(due[at](*done) if at < len(due) else ()))
        done = got or done
        if k == 0:
            break
        a, b = chunk(k), chunk(n - k)
        if at == 0:
            a = jnp.concatenate([a[:half].astype(F32) + ahead, a[half:]], 0)
            b = jnp.concatenate([b[:half], b[half:].astype(F32) + behind], 0)
        else:
            a, b = a.astype(F32) + ahead, b.astype(F32) + behind
        ahead, behind = ring_step(a.astype(BF16), n), ring_step(b.astype(BF16), n, True)
    return chunk(0).astype(F32) + ahead + behind, done


def shard_gather(x):
    return lax.all_gather(x, "shard", axis=0, tiled=True)


def shard_scatter(x):
    return lax.psum_scatter(x, "shard", scatter_dimension=0, tiled=True).astype(F32)


def split_sum(x):
    high = x.astype(BF16)
    return high, (x - high.astype(F32)).astype(BF16)


def local(
    n_shard,
    hidden_in,
    doc_ids,
    expert_ids,
    slot_rows,
    out_grad,
    attn_gain,
    w_query,
    w_key,
    w_value,
    query_gain,
    key_gain,
    w_output,
    ffn_gain,
    w_router,
    w_gate,
    w_up,
    w_down,
):
    length, width = hidden_in.shape
    dim = width // HEADS
    heads = HEADS // 4
    part = width // 4
    routed = w_router.shape[1]
    experts = w_gate.shape[0]
    hidden_units = w_gate.shape[2]
    half_units = hidden_units // 2
    cap = slot_rows.shape[2]
    rep = lax.axis_index("rep")
    shard = lax.axis_index("shard")
    core, side = rep % 2, rep // 2
    my_rows = width // n_shard
    quarter = my_rows // 4

    cut = lambda w: lax.dynamic_slice_in_dim(w, rep * part, part, 1)
    qkv_block = jnp.concatenate([cut(w_query), cut(w_key), cut(w_value)], 1)
    output_block = lax.dynamic_slice_in_dim(w_output, rep * quarter, quarter, 0)
    pick = lambda w: lax.dynamic_index_in_dim(w, core, 0, keepdims=False)
    down_rows = hidden_units // n_shard
    unit = jnp.arange(half_units)
    unit = (unit // (down_rows // 2)) * down_rows + unit % (down_rows // 2)
    choose = lambda which: (
        jnp.arange(hidden_units)[:, None] == (unit + which * (down_rows // 2))[None, :]
    ).astype(BF16)
    mine = choose(side)
    gate_up_block = jnp.concatenate(
        [dot(pick(w_gate), mine).astype(BF16), dot(pick(w_up), mine).astype(BF16)], 1
    )
    down_block = lax.dynamic_slice_in_dim(pick(w_down), side * (down_rows // 2), down_rows // 2, 0)
    small_block = jnp.concatenate(
        [w_router, jnp.stack([attn_gain, query_gain, key_gain, ffn_gain], 1)]
        + [jnp.zeros((my_rows, 128 - 4 - routed), BF16)],
        1,
    )

    docs_all = jnp.concatenate(rep_gather(doc_ids), 0)
    before = docs_all[:, None, :] < docs_all[:, :, None]
    starts = jnp.sum(before.astype(jnp.int32), -1)
    places = (jnp.arange(length, dtype=jnp.int32)[None, :] - starts).astype(F32).reshape(-1)
    rates = THETA ** (-jnp.arange(dim // 2, dtype=F32) * 2.0 / dim)
    angles = places[:, None] * jnp.concatenate([rates, rates])[None, :]
    cosine, sine = jnp.cos(angles), jnp.sin(angles)
    doc_col = docs_all.reshape(-1, 1)
    doc_row = docs_all.reshape(4, 1, length)
    slots = slot_rows[0].reshape(experts * cap)
    select = (slots[:, None] == jnp.arange(length, dtype=jnp.int32)[None, :]).astype(BF16)
    own_upstream = dot(select, out_grad).astype(BF16)

    pieces, (hidden_side, cosine, sine, own_upstream) = ring_gather(
        jnp.concatenate([qkv_block, small_block], 1),
        n_shard,
        (swap(hidden_in, 2), cosine, sine, own_upstream),
    )
    piece, k, first = pieces[-3]
    piece, output_block, gate_up_block, down_block = tie(
        piece, output_block, gate_up_block, down_block
    )
    pieces[-3] = (piece, k, first)
    hidden_all = jnp.concatenate(
        [hidden_in, swap(hidden_in, 1), hidden_side, swap(hidden_side, 1)], 0
    )
    normed_scale = rms_scale(hidden_all.astype(F32))
    piece, k, first = pieces[-1]
    piece, normed_scale = tie(piece, normed_scale)
    pieces[-1] = (piece, k, first)
    ids = ring_ids(n_shard, shard)
    starts = jnp.stack([ids[k] * my_rows + first for _, k, first in pieces])
    w_qkv, small_w = place_rows([piece for piece, _, _ in pieces], starts, width, 3 * part)
    router_w = small_w[:, :routed]
    gains = small_w[:, routed : routed + 4].T.astype(F32)
    w_out_part = shard_gather(output_block).reshape(n_shard, quarter, width)
    w_gu = shard_gather(gate_up_block)
    w_dn = shard_gather(down_block)
    gain_one, gain_two = gains[0], gains[3]
    gain_query = lax.dynamic_slice_in_dim(gains[1:2], rep * part, part, 1)
    gain_key = lax.dynamic_slice_in_dim(gains[2:3], rep * part, part, 1)

    upstream = out_grad.astype(F32)

    def to_experts(x):
        own = lax.dynamic_index_in_dim(x, core, 0, keepdims=False)
        other = lax.dynamic_index_in_dim(x, 1 - core, 0, keepdims=False)
        pair = jnp.stack([own, swap(other, 1)])
        return jnp.concatenate([pair, swap(pair, 2)], 0)

    def send_side(x, send):
        return swap(x[2:].astype(send), 2)

    def from_experts(x, there, send):
        pair = x[:2] + there.astype(F32)
        other = swap(pair[1].astype(send), 1).astype(F32)
        first = jnp.where(core == 0, pair[0], other)
        return jnp.stack([first, jnp.where(core == 0, other, pair[0])])

    def add_slots(x):
        high, low = split_sum(x.reshape(experts * cap, width))
        return dot(select, high, ((0,), (0,))) + dot(select, low, ((0,), (0,)))

    slot_upstream = to_experts(own_upstream.reshape(experts, cap, width))
    normed = (hidden_all.astype(F32) * normed_scale * gain_one).astype(BF16)
    w_qkv, slot_upstream = tie(w_qkv, slot_upstream)
    qkv = dot(normed, w_qkv)
    query_raw, key_raw = qkv[:, :part], qkv[:, part : 2 * part]
    squares = jnp.stack([jnp.sum(query_raw * query_raw, -1), jnp.sum(key_raw * key_raw, -1)], -1)
    squares = rep_sum(squares.reshape(4, length, 2)).reshape(-1, 2)
    scales = lax.rsqrt(squares / width + EPSILON)
    query_scale, key_scale = scales[:, :1], scales[:, 1:]
    scales, w_out_part = tie(scales, w_out_part)
    out_pieces = in_order(rep_gather(w_out_part), rep)
    mixed_heads, queries, keys, values = attend(
        qkv,
        query_scale,
        key_scale,
        gain_query,
        gain_key,
        cosine,
        sine,
        doc_col,
        doc_row,
        heads,
        dim,
    )
    blocks = mixed_heads.reshape(4, length, part)
    from_side = swap(blocks[2:], 2)
    from_side, w_gu, *out_pieces = tie(from_side, w_gu, *out_pieces)
    output_w = jnp.stack(out_pieces, 1).reshape(width, width)
    mixed = jnp.concatenate(
        in_order([blocks[0], swap(blocks[1], 1), from_side[0], swap(from_side[1], 1)], rep), 1
    )
    hidden = hidden_in.astype(F32)
    residual = hidden + dot(mixed, output_w)
    scale_two = rms_scale(residual)
    inner = (residual * scale_two * gain_two).astype(BF16)
    logits = dot(inner, router_w)
    probs_all = jax.nn.softmax(logits, axis=-1)
    named = jnp.sum(
        (expert_ids[:, :, None] == jnp.arange(experts, dtype=jnp.int32)).astype(F32), 1
    )
    window = probs_all[:, :experts] * named
    select_wide = select.reshape(experts, cap, length).astype(F32)
    slot_gates = to_experts(jnp.sum(select_wide * window.T[:, None, :], -1))
    slot_inputs = to_experts(dot(select, inner).astype(BF16).reshape(experts, cap, width))
    slot_inputs = slot_inputs.reshape(4 * cap, width)

    gate_up = dot(slot_inputs, w_gu)
    gate_part, up_part = gate_up[:, :half_units], gate_up[:, half_units:]
    sigma = jax.nn.sigmoid(gate_part)
    swished = gate_part * sigma
    activated = (swished * up_part).astype(BF16)
    returned = dot(activated, w_dn).reshape(4, cap, width)
    slot_gate_grad = jnp.sum(returned * slot_upstream.astype(F32), -1)
    slot_gate_grad = from_experts(slot_gate_grad, send_side(slot_gate_grad, F32), F32)
    returned_grad = (slot_gates[:, :, None] * slot_upstream.astype(F32)).astype(BF16)
    returned_grad = returned_grad.reshape(4 * cap, width)
    act_grad = dot(returned_grad, w_dn, ((1,), (1,)))
    gate_grad = act_grad * up_part * sigma * (1.0 + gate_part * (1.0 - sigma))
    gate_up_grad = jnp.concatenate([gate_grad.astype(BF16), (act_grad * swished).astype(BF16)], 1)
    slot_input_grad = dot(gate_up_grad, w_gu, ((1,), (1,))).reshape(4, cap, width)
    down_w_grad = dot(activated, returned_grad, ((0,), (0,))).astype(BF16)
    gate_up_w_grad = dot(slot_inputs, gate_up_grad, ((0,), (0,))).astype(BF16)
    there, down_w_grad, gate_up_w_grad = tie(
        send_side(slot_input_grad, BF16), down_w_grad, gate_up_w_grad
    )
    slot_input_grad = from_experts(slot_input_grad, there, BF16)
    gate_up_owned = shard_scatter(gate_up_w_grad)
    down_owned = shard_scatter(down_w_grad)

    window_grad = jnp.sum(select_wide * slot_gate_grad[:, :, None], 1).T
    chosen_grad = jnp.concatenate(
        [window_grad * named, jnp.zeros((length, routed - experts), F32)], 1
    )
    logits_grad = (
        probs_all * (chosen_grad - jnp.sum(probs_all * chosen_grad, -1, keepdims=True))
    ).astype(BF16)
    router_grad = dot(inner, logits_grad, ((0,), (0,)))
    inner_grad = add_slots(slot_input_grad) + dot(logits_grad, router_w, ((1,), (1,)))
    residual_part, gain_two_grad = norm_back(residual, scale_two, gain_two, inner_grad)
    residual_grad = upstream + residual_part
    branch_grad = residual_grad.astype(BF16)
    mixed_grad = dot(branch_grad, output_w, ((1,), (1,))).astype(BF16)
    piece = lambda j: lax.dynamic_slice_in_dim(mixed_grad, (rep ^ j) * part, part, 1)
    from_side = swap(jnp.stack([piece(2), piece(3)]), 2)
    from_core, branch_grad = tie(swap(piece(1), 1), branch_grad)
    out_w_grad = dot(mixed, branch_grad, ((0,), (0,))).astype(BF16)
    out_w_grad = out_w_grad.reshape(n_shard, 2, 2, quarter, width)
    at = lambda x, i, axis: lax.dynamic_index_in_dim(x, i, axis, keepdims=False)
    out_w_grad = at(out_w_grad, core, 2).astype(F32) + swap(at(out_w_grad, 1 - core, 2), 1)
    out_w_grad = out_w_grad.astype(BF16)
    from_side, out_w_grad, returned = tie(from_side, out_w_grad, returned)
    grads = jnp.concatenate([piece(0), from_core, from_side[0], swap(from_side[1], 1)], 0)
    returned_there = send_side(returned, BF16)

    query_grad, key_grad, value_grad = attend_back(
        queries, keys, values, grads, cosine, sine, doc_col, doc_row, heads, dim
    )
    value_grad, returned_there = tie(value_grad, returned_there)
    own_gates = jnp.sum(select_wide * window.T[:, None, :], -1)
    returned = from_experts(returned, returned_there, BF16)
    output = (residual + add_slots(own_gates[:, :, None] * returned)).astype(BF16)
    weighted_q, weighted_k = query_grad * gain_query, key_grad * gain_key
    means = jnp.stack(
        [jnp.sum(weighted_q * query_raw, -1), jnp.sum(weighted_k * key_raw, -1)], -1
    )
    means = rep_sum(means.reshape(4, length, 2)).reshape(-1, 2) / width
    means, out_w_grad, gate_up_owned = tie(means, out_w_grad, gate_up_owned)
    out_there = swap(at(out_w_grad, 1 - side, 1), 2)
    gain_query_grad = jnp.sum(query_grad * query_raw * query_scale, 0)
    gain_key_grad = jnp.sum(key_grad * key_raw * key_scale, 0)
    query_raw_grad = query_scale * weighted_q - query_raw * query_scale**3 * means[:, :1]
    key_raw_grad = key_scale * weighted_k - key_raw * key_scale**3 * means[:, 1:]
    qkv_grad = jnp.concatenate(
        [query_raw_grad.astype(BF16), key_raw_grad.astype(BF16), value_grad], 1
    )
    qkv_w_grad = dot(normed, qkv_grad, ((0,), (0,))).astype(BF16)
    qkv_grad, qkv_w_grad = tie(qkv_grad, qkv_w_grad)
    place = lambda g: lax.dynamic_update_slice_in_dim(
        jnp.zeros((width,), F32), g, rep * part, 0
    )
    small = jnp.stack([gain_two_grad, place(gain_query_grad), place(gain_key_grad)], 1)
    small = jnp.concatenate(
        [router_grad, small, jnp.zeros((width, 128 - 3 - routed), F32)], 1
    ).astype(BF16)
    slot_grads = qkv_grad.reshape(4, length, 3 * part)
    back = lambda j: dot(slot_grads[j], w_qkv, ((1,), (1,)))
    due = (
        lambda: (back(1), back(3), out_there),
        lambda one, three, there: (
            back(2),
            swap(jnp.stack([one, three]).astype(BF16), 1),
            (at(out_w_grad, side, 1).astype(F32) + there).astype(BF16),
        ),
        lambda two, from_core, total: (
            back(0) + from_core[0].astype(F32),
            (two + from_core[1].astype(F32)).astype(BF16),
            total,
            down_owned,
        ),
        lambda zero, two, total, down: (
            zero,
            swap(two, 2),
            shard_scatter(total.reshape(n_shard * quarter, width)),
            down,
        ),
    )
    qkv_owned, (normed_grad, from_side, out_owned, down_owned) = ring_scatter(
        [qkv_w_grad, small], n_shard, shard, due
    )
    normed_grad = normed_grad + from_side.astype(F32)
    weighted = normed_grad * gain_one
    scale_one = normed_scale[:length]
    inner_mean = jnp.mean(weighted * hidden, -1, keepdims=True)
    hidden_part = scale_one * weighted - hidden * scale_one * scale_one * scale_one * inner_mean
    input_grad = residual_grad + hidden_part

    qkv_pieces = in_order(rep_gather(qkv_owned.astype(BF16)), rep)
    spread = lambda i: jnp.concatenate(
        [p[:, i * part : (i + 1) * part] for p in qkv_pieces], 1
    ).astype(F32)
    grads_qkv = [spread(i) for i in range(3)]
    small = sum(p[:, 3 * part :].astype(F32) for p in qkv_pieces)
    gain_one_grad = sum(
        jnp.sum(w.astype(F32) * g, 1) for w, g in zip((w_query, w_key, w_value), grads_qkv)
    ) / attn_gain.astype(F32)
    out_full = jnp.concatenate(in_order(rep_gather(out_owned.astype(BF16)), rep), 0).astype(F32)
    gu_pieces = in_order(rep_gather(gate_up_owned.astype(BF16)), rep)
    dn_pieces = in_order(rep_gather(down_owned.astype(BF16)), rep)
    one, two = choose(0), choose(1)
    join = lambda i: jnp.stack(
        [
            dot(gu_pieces[e][:, i * half_units : (i + 1) * half_units], one, ((1,), (1,)))
            + dot(gu_pieces[2 + e][:, i * half_units : (i + 1) * half_units], two, ((1,), (1,)))
            for e in range(experts)
        ]
    )
    down_full = jnp.stack(
        [jnp.concatenate([dn_pieces[e], dn_pieces[2 + e]], 0) for e in range(experts)]
    ).astype(F32)
    return (
        output,
        input_grad,
        gain_one_grad,
        *grads_qkv,
        small[:, routed + 1],
        small[:, routed + 2],
        out_full,
        small[:, routed],
        small[:, :routed],
        join(0),
        join(1),
        down_full,
    )


def solution(mesh):
    tokens = P(("shard", "rep"), None)
    rows = P("shard", None)
    middle = P(None, "shard", None)
    return jax.shard_map(
        functools.partial(local, mesh.shape["shard"]),
        mesh=mesh,
        in_specs=(
            tokens,
            tokens,
            tokens,
            P(("shard", "rep"), None, None),
            tokens,
            P("shard"),
            rows,
            rows,
            rows,
            P("shard"),
            P("shard"),
            rows,
            P("shard"),
            rows,
            middle,
            middle,
            middle,
        ),
        out_specs=(
            tokens,
            tokens,
            P("shard"),
            rows,
            rows,
            rows,
            P("shard"),
            P("shard"),
            rows,
            P("shard"),
            rows,
            middle,
            middle,
            middle,
        ),
        check_vma=False,
    )
```

```python
import functools

import jax
import jax.numpy as jnp
import numpy as np
from jax import lax
from jax.experimental import pallas as pl
from jax.experimental.pallas import tpu as pltpu
from jax.sharding import PartitionSpec as P

HEADS = 16
EPSILON = 1e-05
THETA = 10000.0
REACH = 2
ROWS = 128
F32 = jnp.float32
BF16 = jnp.bfloat16


def rms_scale(values):
    return lax.rsqrt(jnp.mean(values * values, -1, keepdims=True) + EPSILON)


def norm_back(values, scale, gain, upstream):
    gain_grad = jnp.sum(upstream * values * scale, 0)
    weighted = upstream * gain
    inner_mean = jnp.mean(weighted * values, -1, keepdims=True)
    return (scale * weighted - values * scale * scale * scale * inner_mean, gain_grad)


def dot(a, b, dims=((1,), (0,))):
    return lax.dot_general(a, b, (dims, ((), ())), preferred_element_type=F32)


def swap(x, mask):
    return lax.ppermute(x, "rep", [(i, i ^ mask) for i in range(4)])


def flip(x, mask):
    return jnp.stack([x[j ^ mask] for j in range(4)])


def rep_sum(x):
    x = x + flip(swap(x, 1), 1)
    return x + flip(swap(x, 2), 2)


def rep_gather(x):
    one, two = swap(x, 1), swap(x, 2)
    return [x, one, two, swap(two, 1)]


def in_order(pieces, rep):
    low = rep % 2 == 1
    high = rep // 2 == 1
    a, b, c, d = pieces
    a, b = jnp.where(low, b, a), jnp.where(low, a, b)
    c, d = jnp.where(low, d, c), jnp.where(low, c, d)
    return (
        jnp.where(high, c, a),
        jnp.where(high, d, b),
        jnp.where(high, a, c),
        jnp.where(high, b, d),
    )


def mask_bias(bias, doc_col, doc_row):
    length = doc_col.shape[0]
    rows = lax.broadcasted_iota(jnp.int32, (length, length), 0)
    cols = lax.broadcasted_iota(jnp.int32, (length, length), 1)
    allowed = (doc_col[...] == doc_row[0]) & (cols <= rows)
    bias[...] = jnp.where(allowed, 0.0, -jnp.inf).astype(F32)


def turn(values, cosine, sine):
    half = values.shape[-1] // 2
    lanes = lax.broadcasted_iota(jnp.int32, values.shape, 1)
    turned = jnp.where(lanes < half, -1.0, 1.0) * pltpu.roll(values, half, 1)
    return values * cosine + turned * sine


def turn_back(values, cosine, sine):
    half = values.shape[-1] // 2
    lanes = lax.broadcasted_iota(jnp.int32, values.shape, 1)
    moved = pltpu.roll(values * sine, half, 1)
    return values * cosine + jnp.where(lanes < half, 1.0, -1.0) * moved


def spans(length):
    return [
        (i * ROWS, (i + 1) * ROWS, max(0, (i - REACH) * ROWS)) for i in range(length // ROWS)
    ]


def attend_kernel(
    factor,
    q_ref,
    k_ref,
    v_ref,
    q_scale,
    k_scale,
    q_gain,
    k_gain,
    cosine,
    sine,
    doc_col,
    doc_row,
    mixed_ref,
    queries_ref,
    keys_ref,
    values_ref,
    bias,
):
    @pl.when(pl.program_id(1) == 0)
    def _():
        mask_bias(bias, doc_col, doc_row)

    cos, sin = cosine[...], sine[...]
    queries_ref[...] = turn(q_ref[...] * q_scale[...] * q_gain[...], cos, sin).astype(BF16)
    keys_ref[...] = turn(k_ref[...] * k_scale[...] * k_gain[...], cos, sin).astype(BF16)
    values_ref[...] = v_ref[...].astype(BF16)
    for start, end, low in spans(q_ref.shape[0]):
        scores = dot(queries_ref[start:end], keys_ref[low:end], ((1,), (1,))) * factor
        scores = scores + bias[start:end, low:end]
        weights = jnp.exp(scores - jnp.max(scores, -1, keepdims=True))
        probs = (weights * (1.0 / jnp.sum(weights, -1, keepdims=True))).astype(BF16)
        mixed_ref[start:end] = dot(probs, values_ref[low:end]).astype(BF16)


def attend_back_kernel(
    factor,
    queries,
    keys,
    values,
    grads,
    cosine,
    sine,
    doc_col,
    doc_row,
    dq_ref,
    dk_ref,
    dv_ref,
    bias,
    dk_sum,
    dv_sum,
):
    @pl.when(pl.program_id(1) == 0)
    def _():
        mask_bias(bias, doc_col, doc_row)

    cos, sin = cosine[...], sine[...]
    dk_sum[...] = jnp.zeros_like(dk_sum)
    dv_sum[...] = jnp.zeros_like(dv_sum)
    for start, end, low in spans(queries.shape[0]):
        q, g = queries[start:end], grads[start:end]
        k, v = keys[low:end], values[low:end]
        scores = dot(q, k, ((1,), (1,))) * factor + bias[start:end, low:end]
        weights = jnp.exp(scores - jnp.max(scores, -1, keepdims=True))
        probs = weights * (1.0 / jnp.sum(weights, -1, keepdims=True))
        dv_sum[low:end] += dot(probs.astype(BF16), g, ((0,), (0,)))
        prob_grad = dot(g, v, ((1,), (1,)))
        score_grad = probs * (prob_grad - jnp.sum(probs * prob_grad, -1, keepdims=True))
        score_grad = score_grad.astype(BF16)
        dq_ref[start:end] = turn_back(dot(score_grad, k) * factor, cos[start:end], sin[start:end])
        dk_sum[low:end] += dot(score_grad, q, ((0,), (0,)))
    dk_ref[...] = turn_back(dk_sum[...] * factor, cos, sin)
    dv_ref[...] = dv_sum[...].astype(BF16)


def cost(flops, moved, exps=0):
    return pl.CostEstimate(flops=flops, bytes_accessed=moved, transcendentals=exps)


def attend(qkv, q_scale, k_scale, q_gain, k_gain, cosine, sine, doc_col, doc_row, heads, dim):
    tokens = qkv.shape[0]
    length = doc_row.shape[-1]
    block = lambda off: pl.BlockSpec((length, dim), lambda j, h: (j, off + h))
    per_row = pl.BlockSpec((length, 1), lambda j, h: (j, 0))
    table = pl.BlockSpec((length, dim), lambda j, h: (j, 0))
    gain = pl.BlockSpec((1, dim), lambda j, h: (0, h))
    row = pl.BlockSpec((1, 1, length), lambda j, h: (j, 0, 0))
    out = jax.ShapeDtypeStruct((tokens, heads * dim), BF16)
    return pl.pallas_call(
        functools.partial(attend_kernel, dim ** (-0.5)),
        grid=(tokens // length, heads),
        in_specs=[block(0), block(heads), block(2 * heads), per_row, per_row, gain, gain]
        + [table, table, per_row, row],
        out_specs=[block(0)] * 4,
        out_shape=[out] * 4,
        scratch_shapes=[pltpu.VMEM((length, length), F32)],
        cost_estimate=cost(
            4 * tokens * length * heads * dim, tokens * heads * dim * 20, tokens * length * heads
        ),
        name="attend",
    )(qkv, qkv, qkv, q_scale, k_scale, q_gain, k_gain, cosine, sine, doc_col, doc_row)


def attend_back(queries, keys, values, grads, cosine, sine, doc_col, doc_row, heads, dim):
    tokens = queries.shape[0]
    length = doc_row.shape[-1]
    block = pl.BlockSpec((length, dim), lambda j, h: (j, h))
    per_row = pl.BlockSpec((length, 1), lambda j, h: (j, 0))
    table = pl.BlockSpec((length, dim), lambda j, h: (j, 0))
    row = pl.BlockSpec((1, 1, length), lambda j, h: (j, 0, 0))
    wide = jax.ShapeDtypeStruct((tokens, heads * dim), F32)
    return pl.pallas_call(
        functools.partial(attend_back_kernel, dim ** (-0.5)),
        grid=(tokens // length, heads),
        in_specs=[block] * 4 + [table, table, per_row, row],
        out_specs=[block] * 3,
        out_shape=[wide, wide, jax.ShapeDtypeStruct((tokens, heads * dim), BF16)],
        scratch_shapes=[
            pltpu.VMEM((length, length), F32),
            pltpu.VMEM((length, dim), F32),
            pltpu.VMEM((length, dim), F32),
        ],
        cost_estimate=cost(
            10 * tokens * length * heads * dim, tokens * heads * dim * 18, tokens * length * heads
        ),
        name="attend_back",
    )(queries, keys, values, grads, cosine, sine, doc_col, doc_row)


def tie(*arrays):
    return lax.optimization_barrier(arrays)


def ring_of(n):
    return list(range(0, n, 2)) + list(range(n - 1, 0, -2))


def ring_step(x, n, back=False):
    ring = ring_of(n)
    pairs = [(ring[i], ring[(i + 1) % n]) for i in range(n)]
    return lax.ppermute(x, "shard", [(b, a) for a, b in pairs] if back else pairs)


def ring_ids(n):
    ring = ring_of(n)
    return np.array([[ring[(ring.index(s) + i) % n] for i in range(n)] for s in range(n)], np.int32)


def of_shard(table, shard):
    return lax.dynamic_index_in_dim(jnp.asarray(table), shard, 0, keepdims=False)


def ring_gather(block, n, due):
    half = block.shape[0] // 2
    pieces = [(block, 0, 0)]
    ahead = behind = block
    for k in range(1, n // 2):
        behind, ahead = tie(ring_step(behind, n), ring_step(ahead, n, True))
        if k == n // 2 - 1:
            behind, ahead, *due = tie(behind, ahead, *due)
        pieces += [(behind, n - k, 0), (ahead, k, 0)]
    pieces.append((ring_step(behind[:half], n), n // 2, 0))
    pieces.append((ring_step(ahead[half:], n, True), n // 2, half))
    return pieces, due


def place_kernel(n, cut, starts, *refs):
    ins, outs, bufs = refs[:n], refs[n : n + 2], refs[n + 2 : 2 * n + 2]
    sem_in, sem_out = refs[-2], refs[-1]
    loads = [pltpu.make_async_copy(ins[i], bufs[i], sem_in.at[i]) for i in range(n)]
    for load in loads:
        load.start()
    stores = []
    for i in range(n):
        loads[i].wait()
        at = pl.multiple_of(starts[i], 16)
        rows, cols = bufs[i].shape
        for o, first, size in ((0, 0, cut), (1, cut, cols - cut)):
            stores.append(
                pltpu.make_async_copy(
                    bufs[i].at[:, pl.ds(first, size)],
                    outs[o].at[pl.ds(at, rows)],
                    sem_out.at[2 * i + o],
                )
            )
            stores[-1].start()
    for store in stores:
        store.wait()


def place_rows(pieces, starts, rows, cut):
    cols = pieces[0].shape[1]
    n = len(pieces)
    anywhere = pl.BlockSpec(memory_space=pl.ANY)
    return pl.pallas_call(
        functools.partial(place_kernel, n, cut),
        grid_spec=pltpu.PrefetchScalarGridSpec(
            num_scalar_prefetch=1,
            grid=(),
            in_specs=[anywhere] * n,
            out_specs=[anywhere] * 2,
            scratch_shapes=[pltpu.VMEM(x.shape, x.dtype) for x in pieces]
            + [pltpu.SemaphoreType.DMA((n,)), pltpu.SemaphoreType.DMA((2 * n,))],
        ),
        out_shape=[
            jax.ShapeDtypeStruct((rows, size), pieces[0].dtype) for size in (cut, cols - cut)
        ],
        cost_estimate=cost(0, 4 * rows * cols),
        name="place_rows",
    )(starts, *pieces)


def ring_scatter(parts, n, shard, due):
    rows = parts[0].shape[0] // n
    half = rows // 2
    starts = of_shard(ring_ids(n) * rows, shard)
    chunk = lambda k, first=0, size=rows: jnp.concatenate(
        [lax.dynamic_slice_in_dim(x, starts[k % n] + first, size, 0) for x in parts], 1
    )
    done = []
    ahead = ring_step(chunk(n // 2, 0, half), n)
    behind = ring_step(chunk(n // 2, half, half), n, True)
    for k in range(n // 2 - 1, -1, -1):
        at = n // 2 - 1 - k
        ahead, behind, *got = tie(ahead, behind, *(due[at](*done) if at < len(due) else ()))
        done = got or done
        if k == 0:
            break
        a, b = chunk(k), chunk(n - k)
        if at == 0:
            a = jnp.concatenate([a[:half].astype(F32) + ahead, a[half:]], 0)
            b = jnp.concatenate([b[:half], b[half:].astype(F32) + behind], 0)
        else:
            a, b = a.astype(F32) + ahead, b.astype(F32) + behind
        ahead, behind = ring_step(a.astype(BF16), n), ring_step(b.astype(BF16), n, True)
    return chunk(0).astype(F32) + ahead + behind, done


def shard_gather(x):
    return lax.all_gather(x, "shard", axis=0, tiled=True)


def shard_scatter(x):
    return lax.psum_scatter(x, "shard", scatter_dimension=0, tiled=True).astype(F32)


def split_sum(x):
    high = x.astype(BF16)
    return high, (x - high.astype(F32)).astype(BF16)


def local(
    n_shard,
    hidden_in,
    doc_ids,
    expert_ids,
    slot_rows,
    out_grad,
    attn_gain,
    w_query,
    w_key,
    w_value,
    query_gain,
    key_gain,
    w_output,
    ffn_gain,
    w_router,
    w_gate,
    w_up,
    w_down,
):
    length, width = hidden_in.shape
    dim = width // HEADS
    heads = HEADS // 4
    part = width // 4
    routed = w_router.shape[1]
    experts = w_gate.shape[0]
    hidden_units = w_gate.shape[2]
    half_units = hidden_units // 2
    cap = slot_rows.shape[2]
    rep = lax.axis_index("rep")
    shard = lax.axis_index("shard")
    core, side = rep % 2, rep // 2
    my_rows = width // n_shard
    quarter = my_rows // 4

    cut = lambda w: lax.dynamic_slice_in_dim(w, rep * part, part, 1)
    qkv_block = jnp.concatenate([cut(w_query), cut(w_key), cut(w_value)], 1)
    output_block = lax.dynamic_slice_in_dim(w_output, rep * quarter, quarter, 0)
    pick = lambda w: lax.dynamic_index_in_dim(w, core, 0, keepdims=False)
    down_rows = hidden_units // n_shard
    unit = jnp.arange(half_units)
    unit = (unit // (down_rows // 2)) * down_rows + unit % (down_rows // 2)
    choose = lambda which: (
        jnp.arange(hidden_units)[:, None] == (unit + which * (down_rows // 2))[None, :]
    ).astype(BF16)
    mine = choose(side)
    gate_up_block = jnp.concatenate(
        [dot(pick(w_gate), mine).astype(BF16), dot(pick(w_up), mine).astype(BF16)], 1
    )
    down_block = lax.dynamic_slice_in_dim(pick(w_down), side * (down_rows // 2), down_rows // 2, 0)
    small_block = jnp.concatenate(
        [w_router, jnp.stack([attn_gain, query_gain, key_gain, ffn_gain], 1)]
        + [jnp.zeros((my_rows, 128 - 4 - routed), BF16)],
        1,
    )

    docs_all = jnp.concatenate(rep_gather(doc_ids), 0)
    before = docs_all[:, None, :] < docs_all[:, :, None]
    starts = jnp.sum(before.astype(jnp.int32), -1)
    places = (jnp.arange(length, dtype=jnp.int32)[None, :] - starts).astype(F32).reshape(-1)
    rates = THETA ** (-jnp.arange(dim // 2, dtype=F32) * 2.0 / dim)
    angles = places[:, None] * jnp.concatenate([rates, rates])[None, :]
    cosine, sine = jnp.cos(angles), jnp.sin(angles)
    doc_col = docs_all.reshape(-1, 1)
    doc_row = docs_all.reshape(4, 1, length)
    slots = slot_rows[0].reshape(experts * cap)
    select = (slots[:, None] == jnp.arange(length, dtype=jnp.int32)[None, :]).astype(BF16)

    def to_experts(x):
        own = lax.dynamic_index_in_dim(x, core, 0, keepdims=False)
        other = lax.dynamic_index_in_dim(x, 1 - core, 0, keepdims=False)
        pair = jnp.stack([own, swap(other, 1)])
        return jnp.concatenate([pair, swap(pair, 2)], 0)

    slot_upstream = to_experts(dot(select, out_grad).astype(BF16).reshape(experts, cap, width))

    pieces, arrays = ring_gather(
        jnp.concatenate([qkv_block, small_block], 1),
        n_shard,
        (swap(hidden_in, 2), cosine, sine, slot_upstream, output_block, gate_up_block, down_block),
    )
    hidden_side, cosine, sine, slot_upstream, output_block, gate_up_block, down_block = arrays
    hidden_all = jnp.concatenate(
        [hidden_in, swap(hidden_in, 1), hidden_side, swap(hidden_side, 1)], 0
    )
    normed_scale = rms_scale(hidden_all.astype(F32))
    piece, k, first = pieces[-1]
    piece, normed_scale = tie(piece, normed_scale)
    pieces[-1] = (piece, k, first)
    ids = ring_ids(n_shard)
    starts = np.stack([ids[:, k] * my_rows + first for _, k, first in pieces], 1)
    starts = of_shard(starts, shard)
    w_qkv, small_w = place_rows([piece for piece, _, _ in pieces], starts, width, 3 * part)
    router_w = small_w[:, :routed]
    gains = small_w[:, routed : routed + 4].T.astype(F32)
    w_out_part = shard_gather(output_block).reshape(n_shard, quarter, width)
    w_gu = shard_gather(gate_up_block)
    w_dn = shard_gather(down_block)
    gain_one, gain_two = gains[0], gains[3]
    gain_query = lax.dynamic_slice_in_dim(gains[1:2], rep * part, part, 1)
    gain_key = lax.dynamic_slice_in_dim(gains[2:3], rep * part, part, 1)

    upstream = out_grad.astype(F32)

    def send_side(x, send):
        return swap(x[2:].astype(send), 2)

    def from_experts(x, there, send):
        pair = x[:2] + there.astype(F32)
        other = swap(pair[1].astype(send), 1).astype(F32)
        first = jnp.where(core == 0, pair[0], other)
        return jnp.stack([first, jnp.where(core == 0, other, pair[0])])

    def add_slots(x):
        high, low = split_sum(x.reshape(experts * cap, width))
        return dot(select, high, ((0,), (0,))) + dot(select, low, ((0,), (0,)))

    normed = (hidden_all.astype(F32) * normed_scale * gain_one).astype(BF16)
    qkv = dot(normed, w_qkv)
    query_raw, key_raw = qkv[:, :part], qkv[:, part : 2 * part]
    squares = jnp.stack([jnp.sum(query_raw * query_raw, -1), jnp.sum(key_raw * key_raw, -1)], -1)
    squares = rep_sum(squares.reshape(4, length, 2)).reshape(-1, 2)
    scales = lax.rsqrt(squares / width + EPSILON)
    query_scale, key_scale = scales[:, :1], scales[:, 1:]
    scales, w_out_part = tie(scales, w_out_part)
    out_core, out_side = swap(w_out_part, 1), swap(w_out_part, 2)
    mixed_heads, queries, keys, values = attend(
        qkv,
        query_scale,
        key_scale,
        gain_query,
        gain_key,
        cosine,
        sine,
        doc_col,
        doc_row,
        heads,
        dim,
    )
    mixed_heads, out_core, out_side = tie(mixed_heads, out_core, out_side)
    blocks = mixed_heads.reshape(4, length, part)
    from_side = swap(blocks[2:], 2)
    out_pieces = in_order([w_out_part, out_core, out_side, swap(out_side, 1)], rep)
    output_w = jnp.stack(out_pieces, 1).reshape(width, width)
    from_side, w_gu, output_w = tie(from_side, w_gu, output_w)
    mixed = jnp.concatenate(
        in_order([blocks[0], swap(blocks[1], 1), from_side[0], swap(from_side[1], 1)], rep), 1
    )
    hidden = hidden_in.astype(F32)
    residual = hidden + dot(mixed, output_w)
    scale_two = rms_scale(residual)
    inner = (residual * scale_two * gain_two).astype(BF16)
    logits = dot(inner, router_w)
    probs_all = jax.nn.softmax(logits, axis=-1)
    named = jnp.sum(
        (expert_ids[:, :, None] == jnp.arange(experts, dtype=jnp.int32)).astype(F32), 1
    )
    window = probs_all[:, :experts] * named
    select_wide = select.reshape(experts, cap, length).astype(F32)
    slot_gates = to_experts(jnp.sum(select_wide * window.T[:, None, :], -1))
    slot_inputs = to_experts(dot(select, inner).astype(BF16).reshape(experts, cap, width))
    slot_inputs = slot_inputs.reshape(4 * cap, width)

    gate_up = dot(slot_inputs, w_gu)
    gate_part, up_part = gate_up[:, :half_units], gate_up[:, half_units:]
    sigma = jax.nn.sigmoid(gate_part)
    swished = gate_part * sigma
    activated = (swished * up_part).astype(BF16)
    returned = dot(activated, w_dn).reshape(4, cap, width)
    slot_gate_grad = jnp.sum(returned * slot_upstream.astype(F32), -1)
    slot_gate_grad = from_experts(slot_gate_grad, send_side(slot_gate_grad, F32), F32)
    returned_grad = (slot_gates[:, :, None] * slot_upstream.astype(F32)).astype(BF16)
    returned_grad = returned_grad.reshape(4 * cap, width)
    act_grad = dot(returned_grad, w_dn, ((1,), (1,)))
    gate_grad = act_grad * up_part * sigma * (1.0 + gate_part * (1.0 - sigma))
    gate_up_grad = jnp.concatenate([gate_grad.astype(BF16), (act_grad * swished).astype(BF16)], 1)
    slot_input_grad = dot(gate_up_grad, w_gu, ((1,), (1,))).reshape(4, cap, width)
    down_w_grad = dot(activated, returned_grad, ((0,), (0,))).astype(BF16)
    gate_up_w_grad = dot(slot_inputs, gate_up_grad, ((0,), (0,))).astype(BF16)
    there, down_w_grad, gate_up_w_grad = tie(
        send_side(slot_input_grad, BF16), down_w_grad, gate_up_w_grad
    )
    slot_input_grad = from_experts(slot_input_grad, there, BF16)
    gate_up_owned = shard_scatter(gate_up_w_grad)
    down_owned = shard_scatter(down_w_grad)

    window_grad = jnp.sum(select_wide * slot_gate_grad[:, :, None], 1).T
    chosen_grad = jnp.concatenate(
        [window_grad * named, jnp.zeros((length, routed - experts), F32)], 1
    )
    logits_grad = (
        probs_all * (chosen_grad - jnp.sum(probs_all * chosen_grad, -1, keepdims=True))
    ).astype(BF16)
    router_grad = dot(inner, logits_grad, ((0,), (0,)))
    inner_grad = add_slots(slot_input_grad) + dot(logits_grad, router_w, ((1,), (1,)))
    residual_part, gain_two_grad = norm_back(residual, scale_two, gain_two, inner_grad)
    residual_grad = upstream + residual_part
    branch_grad = residual_grad.astype(BF16)
    mixed_grad = dot(branch_grad, output_w, ((1,), (1,))).astype(BF16)
    piece = lambda j: lax.dynamic_slice_in_dim(mixed_grad, (rep ^ j) * part, part, 1)
    from_side = swap(jnp.stack([piece(2), piece(3)]), 2)
    from_core, branch_grad = tie(swap(piece(1), 1), branch_grad)
    at = lambda x, i, axis: lax.dynamic_index_in_dim(x, i, axis, keepdims=False)
    out_w_grad = dot(mixed, branch_grad, ((0,), (0,))).astype(BF16)
    from_side, out_w_grad, returned = tie(from_side, out_w_grad, returned)
    grads = jnp.concatenate([piece(0), from_core, from_side[0], swap(from_side[1], 1)], 0)
    returned_there = send_side(returned, BF16)
    out_w_grad = out_w_grad.reshape(n_shard, 2, 2, quarter, width)
    out_there = swap(at(out_w_grad, 1 - core, 2), 1)

    query_grad, key_grad, value_grad = attend_back(
        queries, keys, values, grads, cosine, sine, doc_col, doc_row, heads, dim
    )
    value_grad, returned_there, out_there = tie(value_grad, returned_there, out_there)
    out_w_grad = (at(out_w_grad, core, 2).astype(F32) + out_there).astype(BF16)
    own_gates = jnp.sum(select_wide * window.T[:, None, :], -1)
    returned = from_experts(returned, returned_there, BF16)
    output = (residual + add_slots(own_gates[:, :, None] * returned)).astype(BF16)
    weighted_q, weighted_k = query_grad * gain_query, key_grad * gain_key
    means = jnp.stack(
        [jnp.sum(weighted_q * query_raw, -1), jnp.sum(weighted_k * key_raw, -1)], -1
    )
    means = rep_sum(means.reshape(4, length, 2)).reshape(-1, 2) / width
    means, out_w_grad = tie(means, out_w_grad)
    out_there = swap(at(out_w_grad, 1 - side, 1), 2)
    gain_query_grad = jnp.sum(query_grad * query_raw * query_scale, 0)
    gain_key_grad = jnp.sum(key_grad * key_raw * key_scale, 0)
    query_raw_grad = query_scale * weighted_q - query_raw * query_scale**3 * means[:, :1]
    key_raw_grad = key_scale * weighted_k - key_raw * key_scale**3 * means[:, 1:]
    qkv_grad = jnp.concatenate(
        [query_raw_grad.astype(BF16), key_raw_grad.astype(BF16), value_grad], 1
    )
    qkv_w_grad = dot(normed, qkv_grad, ((0,), (0,))).astype(BF16)
    qkv_grad, qkv_w_grad, out_there, gate_up_owned = tie(
        qkv_grad, qkv_w_grad, out_there, gate_up_owned
    )
    out_w_grad = (at(out_w_grad, side, 1).astype(F32) + out_there).astype(BF16)
    out_owned = shard_scatter(out_w_grad.reshape(n_shard * quarter, width))
    place = lambda g: lax.dynamic_update_slice_in_dim(
        jnp.zeros((width,), F32), g, rep * part, 0
    )
    small = jnp.stack([gain_two_grad, place(gain_query_grad), place(gain_key_grad)], 1)
    small = jnp.concatenate(
        [router_grad, small, jnp.zeros((width, 128 - 3 - routed), F32)], 1
    ).astype(BF16)
    slot_grads = qkv_grad.reshape(4, length, 3 * part)
    back = lambda j: dot(slot_grads[j], w_qkv, ((1,), (1,)))
    due = (
        lambda: (back(1), back(3)),
        lambda one, three: (back(2), swap(jnp.stack([one, three]).astype(BF16), 1)),
        lambda two, from_core: (
            back(0) + from_core[0].astype(F32),
            two + from_core[1].astype(F32),
            down_owned,
        ),
        lambda zero, two, down: (zero, swap(two.astype(BF16), 2), down),
    )
    qkv_owned, (normed_grad, from_side, down_owned) = ring_scatter(
        [qkv_w_grad, small], n_shard, shard, due
    )
    normed_grad = normed_grad + from_side.astype(F32)
    weighted = normed_grad * gain_one
    scale_one = normed_scale[:length]
    inner_mean = jnp.mean(weighted * hidden, -1, keepdims=True)
    hidden_part = scale_one * weighted - hidden * scale_one * scale_one * scale_one * inner_mean
    input_grad = residual_grad + hidden_part

    qkv_owned = qkv_owned.astype(BF16)
    qkv_core, qkv_side, out_owned = tie(swap(qkv_owned, 1), swap(qkv_owned, 2), out_owned)
    qkv_pieces = in_order([qkv_owned, qkv_core, qkv_side, swap(qkv_side, 1)], rep)
    spread = lambda i: jnp.concatenate(
        [p[:, i * part : (i + 1) * part] for p in qkv_pieces], 1
    ).astype(F32)
    grads_qkv = [spread(i) for i in range(3)]
    small = sum(p[:, 3 * part :].astype(F32) for p in qkv_pieces)
    gain_one_grad = sum(
        jnp.sum(w.astype(F32) * g, 1) for w, g in zip((w_query, w_key, w_value), grads_qkv)
    ) / attn_gain.astype(F32)
    out_full = jnp.concatenate(in_order(rep_gather(out_owned.astype(BF16)), rep), 0).astype(F32)
    gu_pieces = in_order(rep_gather(gate_up_owned.astype(BF16)), rep)
    dn_pieces = in_order(rep_gather(down_owned.astype(BF16)), rep)
    one, two = choose(0), choose(1)
    join = lambda i: jnp.stack(
        [
            dot(gu_pieces[e][:, i * half_units : (i + 1) * half_units], one, ((1,), (1,)))
            + dot(gu_pieces[2 + e][:, i * half_units : (i + 1) * half_units], two, ((1,), (1,)))
            for e in range(experts)
        ]
    )
    down_full = jnp.stack(
        [jnp.concatenate([dn_pieces[e], dn_pieces[2 + e]], 0) for e in range(experts)]
    ).astype(F32)
    return (
        output,
        input_grad,
        gain_one_grad,
        *grads_qkv,
        small[:, routed + 1],
        small[:, routed + 2],
        out_full,
        small[:, routed],
        small[:, :routed],
        join(0),
        join(1),
        down_full,
    )


def solution(mesh):
    tokens = P(("shard", "rep"), None)
    rows = P("shard", None)
    middle = P(None, "shard", None)
    return jax.shard_map(
        functools.partial(local, mesh.shape["shard"]),
        mesh=mesh,
        in_specs=(
            tokens,
            tokens,
            tokens,
            P(("shard", "rep"), None, None),
            tokens,
            P("shard"),
            rows,
            rows,
            rows,
            P("shard"),
            P("shard"),
            rows,
            P("shard"),
            rows,
            middle,
            middle,
            middle,
        ),
        out_specs=(
            tokens,
            tokens,
            P("shard"),
            rows,
            rows,
            rows,
            P("shard"),
            P("shard"),
            rows,
            P("shard"),
            rows,
            middle,
            middle,
            middle,
        ),
        check_vma=False,
    )
```

```python
import functools

import jax
import jax.numpy as jnp
import numpy as np
from jax import lax
from jax.experimental import pallas as pl
from jax.experimental.pallas import tpu as pltpu
from jax.sharding import PartitionSpec as P

HEADS = 16
EPSILON = 1e-05
THETA = 10000.0
REACH = 2
ROWS = 128
F32 = jnp.float32
BF16 = jnp.bfloat16


def rms_scale(values):
    return lax.rsqrt(jnp.mean(values * values, -1, keepdims=True) + EPSILON)


def norm_back(values, scale, gain, upstream):
    gain_grad = jnp.sum(upstream * values * scale, 0)
    weighted = upstream * gain
    inner_mean = jnp.mean(weighted * values, -1, keepdims=True)
    return (scale * weighted - values * scale * scale * scale * inner_mean, gain_grad)


def dot(a, b, dims=((1,), (0,))):
    return lax.dot_general(a, b, (dims, ((), ())), preferred_element_type=F32)


def swap(x, mask):
    return lax.ppermute(x, "rep", [(i, i ^ mask) for i in range(4)])


def flip(x, mask):
    return jnp.stack([x[j ^ mask] for j in range(4)])


def rep_sum(x):
    x = x + flip(swap(x, 1), 1)
    return x + flip(swap(x, 2), 2)


def rep_gather(x):
    one, two = swap(x, 1), swap(x, 2)
    return [x, one, two, swap(two, 1)]


def in_order(pieces, rep):
    low = rep % 2 == 1
    high = rep // 2 == 1
    a, b, c, d = pieces
    a, b = jnp.where(low, b, a), jnp.where(low, a, b)
    c, d = jnp.where(low, d, c), jnp.where(low, c, d)
    return (
        jnp.where(high, c, a),
        jnp.where(high, d, b),
        jnp.where(high, a, c),
        jnp.where(high, b, d),
    )


def mask_bias(bias, doc_col, doc_row):
    length = doc_col.shape[0]
    rows = lax.broadcasted_iota(jnp.int32, (length, length), 0)
    cols = lax.broadcasted_iota(jnp.int32, (length, length), 1)
    allowed = (doc_col[...] == doc_row[0]) & (cols <= rows)
    bias[...] = jnp.where(allowed, 0.0, -jnp.inf).astype(F32)


def turn(values, cosine, sine):
    half = values.shape[-1] // 2
    lanes = lax.broadcasted_iota(jnp.int32, values.shape, 1)
    turned = jnp.where(lanes < half, -1.0, 1.0) * pltpu.roll(values, half, 1)
    return values * cosine + turned * sine


def turn_back(values, cosine, sine):
    half = values.shape[-1] // 2
    lanes = lax.broadcasted_iota(jnp.int32, values.shape, 1)
    moved = pltpu.roll(values * sine, half, 1)
    return values * cosine + jnp.where(lanes < half, 1.0, -1.0) * moved


def spans(length):
    return [
        (i * ROWS, (i + 1) * ROWS, max(0, (i - REACH) * ROWS)) for i in range(length // ROWS)
    ]


def attend_kernel(
    factor,
    q_ref,
    k_ref,
    v_ref,
    q_scale,
    k_scale,
    q_gain,
    k_gain,
    cosine,
    sine,
    doc_col,
    doc_row,
    mixed_ref,
    queries_ref,
    keys_ref,
    values_ref,
    bias,
):
    @pl.when(pl.program_id(1) == 0)
    def _():
        mask_bias(bias, doc_col, doc_row)

    cos, sin = cosine[...], sine[...]
    queries_ref[...] = turn(q_ref[...] * q_scale[...] * q_gain[...], cos, sin).astype(BF16)
    keys_ref[...] = turn(k_ref[...] * k_scale[...] * k_gain[...], cos, sin).astype(BF16)
    values_ref[...] = v_ref[...].astype(BF16)
    for start, end, low in spans(q_ref.shape[0]):
        scores = dot(queries_ref[start:end], keys_ref[low:end], ((1,), (1,))) * factor
        scores = scores + bias[start:end, low:end]
        weights = jnp.exp(scores - jnp.max(scores, -1, keepdims=True))
        probs = (weights * (1.0 / jnp.sum(weights, -1, keepdims=True))).astype(BF16)
        mixed_ref[start:end] = dot(probs, values_ref[low:end]).astype(BF16)


def attend_back_kernel(
    factor,
    queries,
    keys,
    values,
    grads,
    cosine,
    sine,
    doc_col,
    doc_row,
    dq_ref,
    dk_ref,
    dv_ref,
    bias,
    dk_sum,
    dv_sum,
):
    @pl.when(pl.program_id(1) == 0)
    def _():
        mask_bias(bias, doc_col, doc_row)

    cos, sin = cosine[...], sine[...]
    dk_sum[...] = jnp.zeros_like(dk_sum)
    dv_sum[...] = jnp.zeros_like(dv_sum)
    for start, end, low in spans(queries.shape[0]):
        q, g = queries[start:end], grads[start:end]
        k, v = keys[low:end], values[low:end]
        scores = dot(q, k, ((1,), (1,))) * factor + bias[start:end, low:end]
        weights = jnp.exp(scores - jnp.max(scores, -1, keepdims=True))
        probs = weights * (1.0 / jnp.sum(weights, -1, keepdims=True))
        dv_sum[low:end] += dot(probs.astype(BF16), g, ((0,), (0,)))
        prob_grad = dot(g, v, ((1,), (1,)))
        score_grad = probs * (prob_grad - jnp.sum(probs * prob_grad, -1, keepdims=True))
        score_grad = score_grad.astype(BF16)
        dq_ref[start:end] = turn_back(dot(score_grad, k) * factor, cos[start:end], sin[start:end])
        dk_sum[low:end] += dot(score_grad, q, ((0,), (0,)))
    dk_ref[...] = turn_back(dk_sum[...] * factor, cos, sin)
    dv_ref[...] = dv_sum[...].astype(BF16)


def cost(flops, moved, exps=0):
    return pl.CostEstimate(flops=flops, bytes_accessed=moved, transcendentals=exps)


def attend(qkv, q_scale, k_scale, q_gain, k_gain, cosine, sine, doc_col, doc_row, heads, dim):
    tokens = qkv.shape[0]
    length = doc_row.shape[-1]
    block = lambda off: pl.BlockSpec((length, dim), lambda j, h: (j, off + h))
    per_row = pl.BlockSpec((length, 1), lambda j, h: (j, 0))
    table = pl.BlockSpec((length, dim), lambda j, h: (j, 0))
    gain = pl.BlockSpec((1, dim), lambda j, h: (0, h))
    row = pl.BlockSpec((1, 1, length), lambda j, h: (j, 0, 0))
    out = jax.ShapeDtypeStruct((tokens, heads * dim), BF16)
    return pl.pallas_call(
        functools.partial(attend_kernel, dim ** (-0.5)),
        grid=(tokens // length, heads),
        in_specs=[block(0), block(heads), block(2 * heads), per_row, per_row, gain, gain]
        + [table, table, per_row, row],
        out_specs=[block(0)] * 4,
        out_shape=[out] * 4,
        scratch_shapes=[pltpu.VMEM((length, length), F32)],
        cost_estimate=cost(
            4 * tokens * length * heads * dim, tokens * heads * dim * 20, tokens * length * heads
        ),
        name="attend",
    )(qkv, qkv, qkv, q_scale, k_scale, q_gain, k_gain, cosine, sine, doc_col, doc_row)


def attend_back(queries, keys, values, grads, cosine, sine, doc_col, doc_row, heads, dim):
    tokens = queries.shape[0]
    length = doc_row.shape[-1]
    block = pl.BlockSpec((length, dim), lambda j, h: (j, h))
    per_row = pl.BlockSpec((length, 1), lambda j, h: (j, 0))
    table = pl.BlockSpec((length, dim), lambda j, h: (j, 0))
    row = pl.BlockSpec((1, 1, length), lambda j, h: (j, 0, 0))
    wide = jax.ShapeDtypeStruct((tokens, heads * dim), F32)
    return pl.pallas_call(
        functools.partial(attend_back_kernel, dim ** (-0.5)),
        grid=(tokens // length, heads),
        in_specs=[block] * 4 + [table, table, per_row, row],
        out_specs=[block] * 3,
        out_shape=[wide, wide, jax.ShapeDtypeStruct((tokens, heads * dim), BF16)],
        scratch_shapes=[
            pltpu.VMEM((length, length), F32),
            pltpu.VMEM((length, dim), F32),
            pltpu.VMEM((length, dim), F32),
        ],
        cost_estimate=cost(
            10 * tokens * length * heads * dim, tokens * heads * dim * 18, tokens * length * heads
        ),
        name="attend_back",
    )(queries, keys, values, grads, cosine, sine, doc_col, doc_row)


def tie(*arrays):
    return lax.optimization_barrier(arrays)


def ring_of(n):
    return list(range(0, n, 2)) + list(range(n - 1, 0, -2))


def ring_step(x, n, back=False):
    ring = ring_of(n)
    pairs = [(ring[i], ring[(i + 1) % n]) for i in range(n)]
    return lax.ppermute(x, "shard", [(b, a) for a, b in pairs] if back else pairs)


def ring_ids(n):
    ring = ring_of(n)
    return np.array([[ring[(ring.index(s) + i) % n] for i in range(n)] for s in range(n)], np.int32)


def of_shard(table, shard):
    return lax.dynamic_index_in_dim(jnp.asarray(table), shard, 0, keepdims=False)


def ring_gather(block, n, due):
    half = block.shape[0] // 2
    pieces = [(block, 0, 0)]
    ahead = behind = block
    for k in range(1, n // 2):
        behind, ahead = tie(ring_step(behind, n), ring_step(ahead, n, True))
        if k == n // 2 - 1:
            behind, ahead, *due = tie(behind, ahead, *due)
        pieces += [(behind, n - k, 0), (ahead, k, 0)]
    pieces.append((ring_step(behind[:half], n), n // 2, 0))
    pieces.append((ring_step(ahead[half:], n, True), n // 2, half))
    return pieces, due


def place_kernel(n, cut, starts, *refs):
    ins, outs, bufs = refs[:n], refs[n : n + 2], refs[n + 2 : 2 * n + 2]
    sem_in, sem_out = refs[-2], refs[-1]
    loads = [pltpu.make_async_copy(ins[i], bufs[i], sem_in.at[i]) for i in range(n)]
    for load in loads:
        load.start()
    stores = []
    for i in range(n):
        loads[i].wait()
        at = pl.multiple_of(starts[i], 16)
        rows, cols = bufs[i].shape
        for o, first, size in ((0, 0, cut), (1, cut, cols - cut)):
            stores.append(
                pltpu.make_async_copy(
                    bufs[i].at[:, pl.ds(first, size)],
                    outs[o].at[pl.ds(at, rows)],
                    sem_out.at[2 * i + o],
                )
            )
            stores[-1].start()
    for store in stores:
        store.wait()


def place_rows(pieces, starts, rows, cut):
    cols = pieces[0].shape[1]
    n = len(pieces)
    anywhere = pl.BlockSpec(memory_space=pl.ANY)
    return pl.pallas_call(
        functools.partial(place_kernel, n, cut),
        grid_spec=pltpu.PrefetchScalarGridSpec(
            num_scalar_prefetch=1,
            grid=(),
            in_specs=[anywhere] * n,
            out_specs=[anywhere] * 2,
            scratch_shapes=[pltpu.VMEM(x.shape, x.dtype) for x in pieces]
            + [pltpu.SemaphoreType.DMA((n,)), pltpu.SemaphoreType.DMA((2 * n,))],
        ),
        out_shape=[
            jax.ShapeDtypeStruct((rows, size), pieces[0].dtype) for size in (cut, cols - cut)
        ],
        cost_estimate=cost(0, 4 * rows * cols),
        name="place_rows",
    )(starts, *pieces)


def normed_kernel(ids, hidden, scale, gain, out):
    out[...] = (hidden[...].astype(F32) * scale[...] * gain[...]).astype(BF16)


def normed_in_order(ids, hidden, scale, gain):
    n = ids.shape[0]
    rows, cols = hidden.shape
    if cols // n % 128:
        normed = (hidden.astype(F32) * scale * gain).astype(BF16)
        return normed.reshape(rows, n, cols // n)[:, ids].reshape(rows, cols)
    return pl.pallas_call(
        normed_kernel,
        grid_spec=pltpu.PrefetchScalarGridSpec(
            num_scalar_prefetch=1,
            grid=(n,),
            in_specs=[
                pl.BlockSpec((rows, cols // n), lambda i, ids: (0, ids[i])),
                pl.BlockSpec((rows, 1), lambda i, ids: (0, 0)),
                pl.BlockSpec((1, cols // n), lambda i, ids: (0, ids[i])),
            ],
            out_specs=pl.BlockSpec((rows, cols // n), lambda i, ids: (0, i)),
        ),
        out_shape=jax.ShapeDtypeStruct((rows, cols), BF16),
        cost_estimate=cost(2 * rows * cols, 4 * rows * cols),
        name="normed_in_order",
    )(ids, hidden, scale, gain)


def rows_kernel(ids, x, out):
    out[...] = x[...].astype(out.dtype)


def rows_in_order(ids, x):
    n = ids.shape[0]
    rows, cols = x.shape
    return pl.pallas_call(
        rows_kernel,
        grid_spec=pltpu.PrefetchScalarGridSpec(
            num_scalar_prefetch=1,
            grid=(n,),
            in_specs=[pl.BlockSpec((rows // n, cols), lambda i, ids: (ids[i], 0))],
            out_specs=pl.BlockSpec((rows // n, cols), lambda i, ids: (i, 0)),
        ),
        out_shape=jax.ShapeDtypeStruct((rows, cols), BF16),
        cost_estimate=cost(0, 4 * rows * cols),
        name="rows_in_order",
    )(ids, x)


def ring_scatter(parts, n, due):
    rows = parts[0].shape[0] // n
    half = rows // 2
    chunk = lambda k, first=0, size=rows: jnp.concatenate(
        [x[k % n * rows + first : k % n * rows + first + size] for x in parts], 1
    )
    done = []
    ahead = ring_step(chunk(n // 2, 0, half), n)
    behind = ring_step(chunk(n // 2, half, half), n, True)
    for k in range(n // 2 - 1, -1, -1):
        at = n // 2 - 1 - k
        ahead, behind, *got = tie(ahead, behind, *(due[at](*done) if at < len(due) else ()))
        done = got or done
        if k == 0:
            break
        a, b = chunk(k), chunk(n - k)
        if at == 0:
            a = jnp.concatenate([a[:half].astype(F32) + ahead, a[half:]], 0)
            b = jnp.concatenate([b[:half], b[half:].astype(F32) + behind], 0)
        else:
            a, b = a.astype(F32) + ahead, b.astype(F32) + behind
        ahead, behind = ring_step(a.astype(BF16), n), ring_step(b.astype(BF16), n, True)
    return chunk(0).astype(F32) + ahead + behind, done


def shard_gather(x):
    return lax.all_gather(x, "shard", axis=0, tiled=True)


def shard_scatter(x):
    return lax.psum_scatter(x, "shard", scatter_dimension=0, tiled=True).astype(F32)


def split_sum(x):
    high = x.astype(BF16)
    return high, (x - high.astype(F32)).astype(BF16)


def local(
    n_shard,
    hidden_in,
    doc_ids,
    expert_ids,
    slot_rows,
    out_grad,
    attn_gain,
    w_query,
    w_key,
    w_value,
    query_gain,
    key_gain,
    w_output,
    ffn_gain,
    w_router,
    w_gate,
    w_up,
    w_down,
):
    length, width = hidden_in.shape
    dim = width // HEADS
    heads = HEADS // 4
    part = width // 4
    routed = w_router.shape[1]
    experts = w_gate.shape[0]
    hidden_units = w_gate.shape[2]
    half_units = hidden_units // 2
    cap = slot_rows.shape[2]
    rep = lax.axis_index("rep")
    shard = lax.axis_index("shard")
    core, side = rep % 2, rep // 2
    my_rows = width // n_shard
    quarter = my_rows // 4

    cut = lambda w: lax.dynamic_slice_in_dim(w, rep * part, part, 1)
    qkv_block = jnp.concatenate([cut(w_query), cut(w_key), cut(w_value)], 1)
    output_block = lax.dynamic_slice_in_dim(w_output, rep * quarter, quarter, 0)
    pick = lambda w: lax.dynamic_index_in_dim(w, core, 0, keepdims=False)
    down_rows = hidden_units // n_shard
    unit = jnp.arange(half_units)
    unit = (unit // (down_rows // 2)) * down_rows + unit % (down_rows // 2)
    choose = lambda which: (
        jnp.arange(hidden_units)[:, None] == (unit + which * (down_rows // 2))[None, :]
    ).astype(BF16)
    mine = choose(side)
    gate_up_block = jnp.concatenate(
        [dot(pick(w_gate), mine).astype(BF16), dot(pick(w_up), mine).astype(BF16)], 1
    )
    down_block = lax.dynamic_slice_in_dim(pick(w_down), side * (down_rows // 2), down_rows // 2, 0)
    small_block = jnp.concatenate(
        [w_router, jnp.stack([attn_gain, query_gain, key_gain, ffn_gain], 1)]
        + [jnp.zeros((my_rows, 128 - 4 - routed), BF16)],
        1,
    )

    docs_all = jnp.concatenate(rep_gather(doc_ids), 0)
    before = docs_all[:, None, :] < docs_all[:, :, None]
    starts = jnp.sum(before.astype(jnp.int32), -1)
    places = (jnp.arange(length, dtype=jnp.int32)[None, :] - starts).astype(F32).reshape(-1)
    rates = THETA ** (-jnp.arange(dim // 2, dtype=F32) * 2.0 / dim)
    angles = places[:, None] * jnp.concatenate([rates, rates])[None, :]
    cosine, sine = jnp.cos(angles), jnp.sin(angles)
    doc_col = docs_all.reshape(-1, 1)
    doc_row = docs_all.reshape(4, 1, length)
    slots = slot_rows[0].reshape(experts * cap)
    select = (slots[:, None] == jnp.arange(length, dtype=jnp.int32)[None, :]).astype(BF16)

    def to_pair(x):
        own = lax.dynamic_index_in_dim(x, core, 0, keepdims=False)
        other = lax.dynamic_index_in_dim(x, 1 - core, 0, keepdims=False)
        return jnp.stack([own, swap(other, 1)])

    def to_experts(x):
        pair = to_pair(x)
        return jnp.concatenate([pair, swap(pair, 2)], 0)

    upstream_pair = to_pair(dot(select, out_grad).astype(BF16).reshape(experts, cap, width))

    pieces, arrays = ring_gather(
        jnp.concatenate([qkv_block, small_block], 1),
        n_shard,
        (swap(hidden_in, 2), cosine, sine, upstream_pair, output_block, gate_up_block, down_block),
    )
    hidden_side, cosine, sine, upstream_pair, output_block, gate_up_block, down_block = arrays
    slot_upstream = jnp.concatenate([upstream_pair, swap(upstream_pair, 2)], 0)
    hidden_all = jnp.concatenate(
        [hidden_in, swap(hidden_in, 1), hidden_side, swap(hidden_side, 1)], 0
    )
    normed_scale = rms_scale(hidden_all.astype(F32))
    piece, k, first = pieces[-1]
    piece, normed_scale = tie(piece, normed_scale)
    pieces[-1] = (piece, k, first)
    ids = ring_ids(n_shard)
    starts = np.stack([ids[:, k] * my_rows + first for _, k, first in pieces], 1)
    starts, ring = of_shard(starts, shard), of_shard(ids, shard)
    w_qkv, small_w = place_rows([piece for piece, _, _ in pieces], starts, width, 3 * part)
    w_qkv, slot_upstream = tie(w_qkv, slot_upstream)
    router_w = small_w[:, :routed]
    gains = small_w[:, routed : routed + 4].T.astype(F32)
    w_out_part = shard_gather(output_block).reshape(n_shard, quarter, width)
    w_gu = shard_gather(gate_up_block)
    w_dn = shard_gather(down_block)
    gain_one, gain_two = gains[0], gains[3]
    gain_query = lax.dynamic_slice_in_dim(gains[1:2], rep * part, part, 1)
    gain_key = lax.dynamic_slice_in_dim(gains[2:3], rep * part, part, 1)

    upstream = out_grad.astype(F32)

    def send_side(x, send):
        return swap(x[2:].astype(send), 2)

    def from_experts(x, there, send):
        pair = x[:2] + there.astype(F32)
        other = swap(pair[1].astype(send), 1).astype(F32)
        first = jnp.where(core == 0, pair[0], other)
        return jnp.stack([first, jnp.where(core == 0, other, pair[0])])

    def add_slots(x):
        high, low = split_sum(x.reshape(experts * cap, width))
        return dot(select, high, ((0,), (0,))) + dot(select, low, ((0,), (0,)))

    normed = (hidden_all.astype(F32) * normed_scale * gain_one).astype(BF16)
    qkv = dot(normed, w_qkv)
    query_raw, key_raw = qkv[:, :part], qkv[:, part : 2 * part]
    squares = jnp.stack([jnp.sum(query_raw * query_raw, -1), jnp.sum(key_raw * key_raw, -1)], -1)
    squares = rep_sum(squares.reshape(4, length, 2)).reshape(-1, 2)
    scales = lax.rsqrt(squares / width + EPSILON)
    query_scale, key_scale = scales[:, :1], scales[:, 1:]
    scales, w_out_part = tie(scales, w_out_part)
    out_core, out_side = swap(w_out_part, 1), swap(w_out_part, 2)
    mixed_heads, queries, keys, values = attend(
        qkv,
        query_scale,
        key_scale,
        gain_query,
        gain_key,
        cosine,
        sine,
        doc_col,
        doc_row,
        heads,
        dim,
    )
    mixed_heads, out_core, out_side = tie(mixed_heads, out_core, out_side)
    blocks = mixed_heads.reshape(4, length, part)
    from_side = swap(blocks[2:], 2)
    out_pieces = in_order([w_out_part, out_core, out_side, swap(out_side, 1)], rep)
    output_w = jnp.stack(out_pieces, 1).reshape(width, width)
    from_side, w_gu, output_w = tie(from_side, w_gu, output_w)
    mixed = jnp.concatenate(
        in_order([blocks[0], swap(blocks[1], 1), from_side[0], swap(from_side[1], 1)], rep), 1
    )
    hidden = hidden_in.astype(F32)
    residual = hidden + dot(mixed, output_w)
    scale_two = rms_scale(residual)
    inner = (residual * scale_two * gain_two).astype(BF16)
    logits = dot(inner, router_w)
    probs_all = jax.nn.softmax(logits, axis=-1)
    named = jnp.sum(
        (expert_ids[:, :, None] == jnp.arange(experts, dtype=jnp.int32)).astype(F32), 1
    )
    window = probs_all[:, :experts] * named
    select_wide = select.reshape(experts, cap, length).astype(F32)
    slot_gates = to_experts(jnp.sum(select_wide * window.T[:, None, :], -1))
    pair = to_pair(dot(select, inner).astype(BF16).reshape(experts, cap, width))
    normed_ring = normed_in_order(ring, hidden_all, normed_scale, gain_one[None])
    from_side, normed_ring = tie(swap(pair, 2), normed_ring)
    slot_inputs = jnp.concatenate([pair, from_side], 0)
    slot_inputs = slot_inputs.reshape(4 * cap, width)

    gate_up = dot(slot_inputs, w_gu)
    gate_part, up_part = gate_up[:, :half_units], gate_up[:, half_units:]
    sigma = jax.nn.sigmoid(gate_part)
    swished = gate_part * sigma
    activated = (swished * up_part).astype(BF16)
    returned = dot(activated, w_dn).reshape(4, cap, width)
    slot_gate_grad = jnp.sum(returned * slot_upstream.astype(F32), -1)
    slot_gate_grad = from_experts(slot_gate_grad, send_side(slot_gate_grad, F32), F32)
    returned_grad = (slot_gates[:, :, None] * slot_upstream.astype(F32)).astype(BF16)
    returned_grad = returned_grad.reshape(4 * cap, width)
    act_grad = dot(returned_grad, w_dn, ((1,), (1,)))
    gate_grad = act_grad * up_part * sigma * (1.0 + gate_part * (1.0 - sigma))
    gate_up_grad = jnp.concatenate([gate_grad.astype(BF16), (act_grad * swished).astype(BF16)], 1)
    slot_input_grad = dot(gate_up_grad, w_gu, ((1,), (1,))).reshape(4, cap, width)
    down_w_grad = dot(activated, returned_grad, ((0,), (0,))).astype(BF16)
    gate_up_w_grad = dot(slot_inputs, gate_up_grad, ((0,), (0,))).astype(BF16)
    there, down_w_grad, gate_up_w_grad = tie(
        send_side(slot_input_grad, BF16), down_w_grad, gate_up_w_grad
    )
    slot_input_grad = from_experts(slot_input_grad, there, BF16)
    gate_up_owned = shard_scatter(gate_up_w_grad)
    down_owned = shard_scatter(down_w_grad)

    window_grad = jnp.sum(select_wide * slot_gate_grad[:, :, None], 1).T
    chosen_grad = jnp.concatenate(
        [window_grad * named, jnp.zeros((length, routed - experts), F32)], 1
    )
    logits_grad = (
        probs_all * (chosen_grad - jnp.sum(probs_all * chosen_grad, -1, keepdims=True))
    ).astype(BF16)
    router_grad = dot(inner, logits_grad, ((0,), (0,)))
    inner_grad = add_slots(slot_input_grad) + dot(logits_grad, router_w, ((1,), (1,)))
    residual_part, gain_two_grad = norm_back(residual, scale_two, gain_two, inner_grad)
    residual_grad = upstream + residual_part
    branch_grad = residual_grad.astype(BF16)
    mixed_grad = dot(branch_grad, output_w, ((1,), (1,))).astype(BF16)
    piece = lambda j: lax.dynamic_slice_in_dim(mixed_grad, (rep ^ j) * part, part, 1)
    from_side = swap(jnp.stack([piece(2), piece(3)]), 2)
    from_core, branch_grad = tie(swap(piece(1), 1), branch_grad)
    at = lambda x, i, axis: lax.dynamic_index_in_dim(x, i, axis, keepdims=False)
    half = lambda which: at(mixed.reshape(length, n_shard, 2, 2, quarter), which, 3)
    half_grad = lambda which: dot(
        half(which).reshape(length, width // 2), branch_grad, ((0,), (0,))
    ).astype(BF16)
    out_there = swap(half_grad(1 - core), 1)
    out_w_grad = (half_grad(core).astype(F32) + out_there).astype(BF16)
    from_side, out_w_grad, returned = tie(from_side, out_w_grad, returned)
    grads = jnp.concatenate([piece(0), from_core, from_side[0], swap(from_side[1], 1)], 0)
    out_w_grad = out_w_grad.reshape(n_shard, 2, quarter, width)
    out_there = swap(at(out_w_grad, 1 - side, 1), 2)

    query_grad, key_grad, value_grad = attend_back(
        queries, keys, values, grads, cosine, sine, doc_col, doc_row, heads, dim
    )
    value_grad, out_there = tie(value_grad, out_there)
    out_w_grad = (at(out_w_grad, side, 1).astype(F32) + out_there).astype(BF16)
    out_owned = shard_scatter(out_w_grad.reshape(n_shard * quarter, width))
    weighted_q, weighted_k = query_grad * gain_query, key_grad * gain_key
    means = jnp.stack(
        [jnp.sum(weighted_q * query_raw, -1), jnp.sum(weighted_k * key_raw, -1)], -1
    )
    means = rep_sum(means.reshape(4, length, 2)).reshape(-1, 2) / width
    means, returned = tie(means, returned)
    returned_there = send_side(returned, BF16)
    gain_query_grad = jnp.sum(query_grad * query_raw * query_scale, 0)
    gain_key_grad = jnp.sum(key_grad * key_raw * key_scale, 0)
    query_raw_grad = query_scale * weighted_q - query_raw * query_scale**3 * means[:, :1]
    key_raw_grad = key_scale * weighted_k - key_raw * key_scale**3 * means[:, 1:]
    qkv_grad = jnp.concatenate(
        [query_raw_grad.astype(BF16), key_raw_grad.astype(BF16), value_grad], 1
    )
    qkv_w_grad = dot(normed_ring, qkv_grad, ((0,), (0,))).astype(BF16)
    qkv_grad, qkv_w_grad, returned_there, gate_up_owned = tie(
        qkv_grad, qkv_w_grad, returned_there, gate_up_owned
    )
    own_gates = jnp.sum(select_wide * window.T[:, None, :], -1)
    returned = from_experts(returned, returned_there, BF16)
    output = (residual + add_slots(own_gates[:, :, None] * returned)).astype(BF16)
    place = lambda g: lax.dynamic_update_slice_in_dim(
        jnp.zeros((width,), F32), g, rep * part, 0
    )
    small = jnp.stack([gain_two_grad, place(gain_query_grad), place(gain_key_grad)], 1)
    small = jnp.concatenate(
        [router_grad, small, jnp.zeros((width, 128 - 3 - routed), F32)], 1
    )
    back = lambda slots, j: dot(
        slots.reshape(4, length, 3 * part)[j], w_qkv, ((1,), (1,))
    )
    due = (
        lambda: (qkv_grad, back(qkv_grad, 1), back(qkv_grad, 3)),
        lambda slots, one, three: (
            slots,
            back(slots, 2),
            swap(jnp.stack([one, three]).astype(BF16), 1),
        ),
        lambda slots, two, from_core: (
            back(slots, 0) + from_core[0].astype(F32),
            two + from_core[1].astype(F32),
            down_owned,
        ),
        lambda zero, two, down: (zero, swap(two.astype(BF16), 2), down),
    )
    qkv_owned, (normed_grad, from_side, down_owned) = ring_scatter(
        [qkv_w_grad, rows_in_order(ring, small)], n_shard, due
    )
    normed_grad = normed_grad + from_side.astype(F32)
    weighted = normed_grad * gain_one
    scale_one = normed_scale[:length]
    inner_mean = jnp.mean(weighted * hidden, -1, keepdims=True)
    hidden_part = scale_one * weighted - hidden * scale_one * scale_one * scale_one * inner_mean
    input_grad = residual_grad + hidden_part

    qkv_owned = qkv_owned.astype(BF16)
    qkv_core, qkv_side, out_owned = tie(swap(qkv_owned, 1), swap(qkv_owned, 2), out_owned)
    qkv_pieces = in_order([qkv_owned, qkv_core, qkv_side, swap(qkv_side, 1)], rep)
    spread = lambda i: jnp.concatenate(
        [p[:, i * part : (i + 1) * part] for p in qkv_pieces], 1
    ).astype(F32)
    grads_qkv = [spread(i) for i in range(3)]
    small = sum(p[:, 3 * part :].astype(F32) for p in qkv_pieces)
    gain_one_grad = sum(
        jnp.sum(w.astype(F32) * g, 1) for w, g in zip((w_query, w_key, w_value), grads_qkv)
    ) / attn_gain.astype(F32)
    out_full = jnp.concatenate(in_order(rep_gather(out_owned.astype(BF16)), rep), 0).astype(F32)
    gu_pieces = in_order(rep_gather(gate_up_owned.astype(BF16)), rep)
    dn_pieces = in_order(rep_gather(down_owned.astype(BF16)), rep)
    one, two = choose(0), choose(1)
    join = lambda i: jnp.stack(
        [
            dot(gu_pieces[e][:, i * half_units : (i + 1) * half_units], one, ((1,), (1,)))
            + dot(gu_pieces[2 + e][:, i * half_units : (i + 1) * half_units], two, ((1,), (1,)))
            for e in range(experts)
        ]
    )
    down_full = jnp.stack(
        [jnp.concatenate([dn_pieces[e], dn_pieces[2 + e]], 0) for e in range(experts)]
    ).astype(F32)
    return (
        output,
        input_grad,
        gain_one_grad,
        *grads_qkv,
        small[:, routed + 1],
        small[:, routed + 2],
        out_full,
        small[:, routed],
        small[:, :routed],
        join(0),
        join(1),
        down_full,
    )


def solution(mesh):
    tokens = P(("shard", "rep"), None)
    rows = P("shard", None)
    middle = P(None, "shard", None)
    return jax.shard_map(
        functools.partial(local, mesh.shape["shard"]),
        mesh=mesh,
        in_specs=(
            tokens,
            tokens,
            tokens,
            P(("shard", "rep"), None, None),
            tokens,
            P("shard"),
            rows,
            rows,
            rows,
            P("shard"),
            P("shard"),
            rows,
            P("shard"),
            rows,
            middle,
            middle,
            middle,
        ),
        out_specs=(
            tokens,
            tokens,
            P("shard"),
            rows,
            rows,
            rows,
            P("shard"),
            P("shard"),
            rows,
            P("shard"),
            rows,
            middle,
            middle,
            middle,
        ),
        check_vma=False,
    )
```

```python
import functools

import jax
import jax.numpy as jnp
import numpy as np
from jax import lax
from jax.experimental import pallas as pl
from jax.experimental.pallas import tpu as pltpu
from jax.sharding import PartitionSpec as P

HEADS = 16
EPSILON = 1e-05
THETA = 10000.0
REACH = 2
ROWS = 128
F32 = jnp.float32
BF16 = jnp.bfloat16


def rms_scale(values):
    return lax.rsqrt(jnp.mean(values * values, -1, keepdims=True) + EPSILON)


def norm_back(values, scale, gain, upstream):
    gain_grad = jnp.sum(upstream * values * scale, 0)
    weighted = upstream * gain
    inner_mean = jnp.mean(weighted * values, -1, keepdims=True)
    return (scale * weighted - values * scale * scale * scale * inner_mean, gain_grad)


def dot(a, b, dims=((1,), (0,))):
    return lax.dot_general(a, b, (dims, ((), ())), preferred_element_type=F32)


def swap(x, mask):
    return lax.ppermute(x, "rep", [(i, i ^ mask) for i in range(4)])


def flip(x, mask):
    return jnp.stack([x[j ^ mask] for j in range(4)])


def rep_sum(x):
    x = x + flip(swap(x, 1), 1)
    return x + flip(swap(x, 2), 2)


def rep_gather(x):
    one, two = swap(x, 1), swap(x, 2)
    return [x, one, two, swap(two, 1)]


def in_order(pieces, rep):
    low = rep % 2 == 1
    high = rep // 2 == 1
    a, b, c, d = pieces
    a, b = jnp.where(low, b, a), jnp.where(low, a, b)
    c, d = jnp.where(low, d, c), jnp.where(low, c, d)
    return (
        jnp.where(high, c, a),
        jnp.where(high, d, b),
        jnp.where(high, a, c),
        jnp.where(high, b, d),
    )


def mask_bias(bias, doc_col, doc_row):
    length = doc_col.shape[0]
    rows = lax.broadcasted_iota(jnp.int32, (length, length), 0)
    cols = lax.broadcasted_iota(jnp.int32, (length, length), 1)
    allowed = (doc_col[...] == doc_row[0]) & (cols <= rows)
    bias[...] = jnp.where(allowed, 0.0, -jnp.inf).astype(F32)


def turn(values, cosine, sine):
    half = values.shape[-1] // 2
    lanes = lax.broadcasted_iota(jnp.int32, values.shape, 1)
    turned = jnp.where(lanes < half, -1.0, 1.0) * pltpu.roll(values, half, 1)
    return values * cosine + turned * sine


def turn_back(values, cosine, sine):
    half = values.shape[-1] // 2
    lanes = lax.broadcasted_iota(jnp.int32, values.shape, 1)
    moved = pltpu.roll(values * sine, half, 1)
    return values * cosine + jnp.where(lanes < half, 1.0, -1.0) * moved


def spans(length):
    return [
        (i * ROWS, (i + 1) * ROWS, max(0, (i - REACH) * ROWS)) for i in range(length // ROWS)
    ]


def attend_kernel(
    factor,
    q_ref,
    k_ref,
    v_ref,
    q_scale,
    k_scale,
    q_gain,
    k_gain,
    cosine,
    sine,
    doc_col,
    doc_row,
    mixed_ref,
    queries_ref,
    keys_ref,
    values_ref,
    bias,
):
    @pl.when(pl.program_id(1) == 0)
    def _():
        mask_bias(bias, doc_col, doc_row)

    cos, sin = cosine[...], sine[...]
    queries_ref[...] = turn(q_ref[...] * q_scale[...] * q_gain[...], cos, sin).astype(BF16)
    keys_ref[...] = turn(k_ref[...] * k_scale[...] * k_gain[...], cos, sin).astype(BF16)
    values_ref[...] = v_ref[...].astype(BF16)
    for start, end, low in spans(q_ref.shape[0]):
        scores = dot(queries_ref[start:end], keys_ref[low:end], ((1,), (1,))) * factor
        scores = scores + bias[start:end, low:end]
        weights = jnp.exp(scores - jnp.max(scores, -1, keepdims=True))
        probs = (weights * (1.0 / jnp.sum(weights, -1, keepdims=True))).astype(BF16)
        mixed_ref[start:end] = dot(probs, values_ref[low:end]).astype(BF16)


def attend_back_kernel(
    factor,
    queries,
    keys,
    values,
    grads,
    cosine,
    sine,
    doc_col,
    doc_row,
    dq_ref,
    dk_ref,
    dv_ref,
    bias,
    dk_sum,
    dv_sum,
):
    @pl.when(pl.program_id(1) == 0)
    def _():
        mask_bias(bias, doc_col, doc_row)

    cos, sin = cosine[...], sine[...]
    dk_sum[...] = jnp.zeros_like(dk_sum)
    dv_sum[...] = jnp.zeros_like(dv_sum)
    for start, end, low in spans(queries.shape[0]):
        q, g = queries[start:end], grads[start:end]
        k, v = keys[low:end], values[low:end]
        scores = dot(q, k, ((1,), (1,))) * factor + bias[start:end, low:end]
        weights = jnp.exp(scores - jnp.max(scores, -1, keepdims=True))
        probs = weights * (1.0 / jnp.sum(weights, -1, keepdims=True))
        dv_sum[low:end] += dot(probs.astype(BF16), g, ((0,), (0,)))
        prob_grad = dot(g, v, ((1,), (1,)))
        score_grad = probs * (prob_grad - jnp.sum(probs * prob_grad, -1, keepdims=True))
        score_grad = score_grad.astype(BF16)
        dq_ref[start:end] = turn_back(dot(score_grad, k) * factor, cos[start:end], sin[start:end])
        dk_sum[low:end] += dot(score_grad, q, ((0,), (0,)))
    dk_ref[...] = turn_back(dk_sum[...] * factor, cos, sin)
    dv_ref[...] = dv_sum[...].astype(BF16)


def cost(flops, moved, exps=0):
    return pl.CostEstimate(flops=flops, bytes_accessed=moved, transcendentals=exps)


def attend(qkv, q_scale, k_scale, q_gain, k_gain, cosine, sine, doc_col, doc_row, heads, dim):
    tokens = qkv.shape[0]
    length = doc_row.shape[-1]
    block = lambda off: pl.BlockSpec((length, dim), lambda j, h: (j, off + h))
    per_row = pl.BlockSpec((length, 1), lambda j, h: (j, 0))
    table = pl.BlockSpec((length, dim), lambda j, h: (j, 0))
    gain = pl.BlockSpec((1, dim), lambda j, h: (0, h))
    row = pl.BlockSpec((1, 1, length), lambda j, h: (j, 0, 0))
    out = jax.ShapeDtypeStruct((tokens, heads * dim), BF16)
    return pl.pallas_call(
        functools.partial(attend_kernel, dim ** (-0.5)),
        grid=(tokens // length, heads),
        in_specs=[block(0), block(heads), block(2 * heads), per_row, per_row, gain, gain]
        + [table, table, per_row, row],
        out_specs=[block(0)] * 4,
        out_shape=[out] * 4,
        scratch_shapes=[pltpu.VMEM((length, length), F32)],
        cost_estimate=cost(
            4 * tokens * length * heads * dim, tokens * heads * dim * 20, tokens * length * heads
        ),
        name="attend",
    )(qkv, qkv, qkv, q_scale, k_scale, q_gain, k_gain, cosine, sine, doc_col, doc_row)


def attend_back(queries, keys, values, grads, cosine, sine, doc_col, doc_row, heads, dim):
    tokens = queries.shape[0]
    length = doc_row.shape[-1]
    block = pl.BlockSpec((length, dim), lambda j, h: (j, h))
    per_row = pl.BlockSpec((length, 1), lambda j, h: (j, 0))
    table = pl.BlockSpec((length, dim), lambda j, h: (j, 0))
    row = pl.BlockSpec((1, 1, length), lambda j, h: (j, 0, 0))
    wide = jax.ShapeDtypeStruct((tokens, heads * dim), F32)
    return pl.pallas_call(
        functools.partial(attend_back_kernel, dim ** (-0.5)),
        grid=(tokens // length, heads),
        in_specs=[block] * 4 + [table, table, per_row, row],
        out_specs=[block] * 3,
        out_shape=[wide, wide, jax.ShapeDtypeStruct((tokens, heads * dim), BF16)],
        scratch_shapes=[
            pltpu.VMEM((length, length), F32),
            pltpu.VMEM((length, dim), F32),
            pltpu.VMEM((length, dim), F32),
        ],
        cost_estimate=cost(
            10 * tokens * length * heads * dim, tokens * heads * dim * 18, tokens * length * heads
        ),
        name="attend_back",
    )(queries, keys, values, grads, cosine, sine, doc_col, doc_row)


def tie(*arrays):
    return lax.optimization_barrier(arrays)


def ring_of(n):
    return list(range(0, n, 2)) + list(range(n - 1, 0, -2))


def ring_step(x, n, back=False):
    ring = ring_of(n)
    pairs = [(ring[i], ring[(i + 1) % n]) for i in range(n)]
    return lax.ppermute(x, "shard", [(b, a) for a, b in pairs] if back else pairs)


def ring_ids(n):
    ring = ring_of(n)
    return np.array([[ring[(ring.index(s) + i) % n] for i in range(n)] for s in range(n)], np.int32)


def of_shard(table, shard):
    return lax.dynamic_index_in_dim(jnp.asarray(table), shard, 0, keepdims=False)


def ring_gather(block, n, due):
    half = block.shape[0] // 2
    pieces = [(block, 0, 0)]
    ahead = behind = block
    for k in range(1, n // 2):
        behind, ahead = tie(ring_step(behind, n), ring_step(ahead, n, True))
        if k == n // 2 - 1:
            behind, ahead, *due = tie(behind, ahead, *due)
        pieces += [(behind, n - k, 0), (ahead, k, 0)]
    pieces.append((ring_step(behind[:half], n), n // 2, 0))
    pieces.append((ring_step(ahead[half:], n, True), n // 2, half))
    return pieces, due


def place_kernel(n, cut, starts, *refs):
    ins, outs, bufs = refs[:n], refs[n : n + 2], refs[n + 2 : 2 * n + 2]
    sem_in, sem_out = refs[-2], refs[-1]
    loads = [pltpu.make_async_copy(ins[i], bufs[i], sem_in.at[i]) for i in range(n)]
    for load in loads:
        load.start()
    stores = []
    for i in range(n):
        loads[i].wait()
        at = pl.multiple_of(starts[i], 16)
        rows, cols = bufs[i].shape
        for o, first, size in ((0, 0, cut), (1, cut, cols - cut)):
            stores.append(
                pltpu.make_async_copy(
                    bufs[i].at[:, pl.ds(first, size)],
                    outs[o].at[pl.ds(at, rows)],
                    sem_out.at[2 * i + o],
                )
            )
            stores[-1].start()
    for store in stores:
        store.wait()


def place_rows(pieces, starts, rows, cut):
    cols = pieces[0].shape[1]
    n = len(pieces)
    anywhere = pl.BlockSpec(memory_space=pl.ANY)
    return pl.pallas_call(
        functools.partial(place_kernel, n, cut),
        grid_spec=pltpu.PrefetchScalarGridSpec(
            num_scalar_prefetch=1,
            grid=(),
            in_specs=[anywhere] * n,
            out_specs=[anywhere] * 2,
            scratch_shapes=[pltpu.VMEM(x.shape, x.dtype) for x in pieces]
            + [pltpu.SemaphoreType.DMA((n,)), pltpu.SemaphoreType.DMA((2 * n,))],
        ),
        out_shape=[
            jax.ShapeDtypeStruct((rows, size), pieces[0].dtype) for size in (cut, cols - cut)
        ],
        cost_estimate=cost(0, 4 * rows * cols),
        name="place_rows",
    )(starts, *pieces)


def normed_kernel(ids, hidden, scale, gain, out):
    out[...] = (hidden[...].astype(F32) * scale[...] * gain[...]).astype(BF16)


def normed_in_order(ids, hidden, scale, gain):
    n = ids.shape[0]
    rows, cols = hidden.shape
    if cols // n % 128:
        normed = (hidden.astype(F32) * scale * gain).astype(BF16)
        return normed.reshape(rows, n, cols // n)[:, ids].reshape(rows, cols)
    return pl.pallas_call(
        normed_kernel,
        grid_spec=pltpu.PrefetchScalarGridSpec(
            num_scalar_prefetch=1,
            grid=(n,),
            in_specs=[
                pl.BlockSpec((rows, cols // n), lambda i, ids: (0, ids[i])),
                pl.BlockSpec((rows, 1), lambda i, ids: (0, 0)),
                pl.BlockSpec((1, cols // n), lambda i, ids: (0, ids[i])),
            ],
            out_specs=pl.BlockSpec((rows, cols // n), lambda i, ids: (0, i)),
        ),
        out_shape=jax.ShapeDtypeStruct((rows, cols), BF16),
        cost_estimate=cost(2 * rows * cols, 4 * rows * cols),
        name="normed_in_order",
    )(ids, hidden, scale, gain)


def rows_kernel(ids, x, out):
    out[...] = x[...].astype(out.dtype)


def rows_in_order(ids, x):
    n = ids.shape[0]
    rows, cols = x.shape
    return pl.pallas_call(
        rows_kernel,
        grid_spec=pltpu.PrefetchScalarGridSpec(
            num_scalar_prefetch=1,
            grid=(n,),
            in_specs=[pl.BlockSpec((rows // n, cols), lambda i, ids: (ids[i], 0))],
            out_specs=pl.BlockSpec((rows // n, cols), lambda i, ids: (i, 0)),
        ),
        out_shape=jax.ShapeDtypeStruct((rows, cols), BF16),
        cost_estimate=cost(0, 4 * rows * cols),
        name="rows_in_order",
    )(ids, x)


def ring_scatter(parts, n, due):
    rows = parts[0].shape[0] // n
    half = rows // 2
    chunk = lambda k, first=0, size=rows: jnp.concatenate(
        [x[k % n * rows + first : k % n * rows + first + size] for x in parts], 1
    )
    done = []
    ahead = ring_step(chunk(n // 2, 0, half), n)
    behind = ring_step(chunk(n // 2, half, half), n, True)
    for k in range(n // 2 - 1, -1, -1):
        at = n // 2 - 1 - k
        ahead, behind, *got = tie(ahead, behind, *(due[at](*done) if at < len(due) else ()))
        done = got or done
        if k == 0:
            break
        a, b = chunk(k), chunk(n - k)
        if at == 0:
            a = jnp.concatenate([a[:half].astype(F32) + ahead, a[half:]], 0)
            b = jnp.concatenate([b[:half], b[half:].astype(F32) + behind], 0)
        else:
            a, b = a.astype(F32) + ahead, b.astype(F32) + behind
        ahead, behind = ring_step(a.astype(BF16), n), ring_step(b.astype(BF16), n, True)
    return chunk(0).astype(F32) + ahead + behind, done


def shard_gather(x):
    return lax.all_gather(x, "shard", axis=0, tiled=True)


def shard_scatter(x):
    return lax.psum_scatter(x, "shard", scatter_dimension=0, tiled=True).astype(F32)


def split_sum(x):
    high = x.astype(BF16)
    return high, (x - high.astype(F32)).astype(BF16)


def local(
    n_shard,
    hidden_in,
    doc_ids,
    expert_ids,
    slot_rows,
    out_grad,
    attn_gain,
    w_query,
    w_key,
    w_value,
    query_gain,
    key_gain,
    w_output,
    ffn_gain,
    w_router,
    w_gate,
    w_up,
    w_down,
):
    length, width = hidden_in.shape
    dim = width // HEADS
    heads = HEADS // 4
    part = width // 4
    routed = w_router.shape[1]
    experts = w_gate.shape[0]
    hidden_units = w_gate.shape[2]
    half_units = hidden_units // 2
    cap = slot_rows.shape[2]
    rep = lax.axis_index("rep")
    shard = lax.axis_index("shard")
    core, side = rep % 2, rep // 2
    my_rows = width // n_shard
    quarter = my_rows // 4

    cut = lambda w: lax.dynamic_slice_in_dim(w, rep * part, part, 1)
    qkv_block = jnp.concatenate([cut(w_query), cut(w_key), cut(w_value)], 1)
    output_block = lax.dynamic_slice_in_dim(w_output, rep * quarter, quarter, 0)
    pick = lambda w: lax.dynamic_index_in_dim(w, core, 0, keepdims=False)
    down_rows = hidden_units // n_shard
    unit = jnp.arange(half_units)
    unit = (unit // (down_rows // 2)) * down_rows + unit % (down_rows // 2)
    choose = lambda which: (
        jnp.arange(hidden_units)[:, None] == (unit + which * (down_rows // 2))[None, :]
    ).astype(BF16)
    mine = choose(side)
    gate_up_block = jnp.concatenate(
        [dot(pick(w_gate), mine).astype(BF16), dot(pick(w_up), mine).astype(BF16)], 1
    )
    down_block = lax.dynamic_slice_in_dim(pick(w_down), side * (down_rows // 2), down_rows // 2, 0)
    small_block = jnp.concatenate(
        [w_router, jnp.stack([attn_gain, query_gain, key_gain, ffn_gain], 1)]
        + [jnp.zeros((my_rows, 128 - 4 - routed), BF16)],
        1,
    )

    docs_all = jnp.concatenate(rep_gather(doc_ids), 0)
    before = docs_all[:, None, :] < docs_all[:, :, None]
    starts = jnp.sum(before.astype(jnp.int32), -1)
    places = (jnp.arange(length, dtype=jnp.int32)[None, :] - starts).astype(F32).reshape(-1)
    rates = THETA ** (-jnp.arange(dim // 2, dtype=F32) * 2.0 / dim)
    angles = places[:, None] * jnp.concatenate([rates, rates])[None, :]
    cosine, sine = jnp.cos(angles), jnp.sin(angles)
    doc_col = docs_all.reshape(-1, 1)
    doc_row = docs_all.reshape(4, 1, length)
    slots = slot_rows[0].reshape(experts * cap)
    select = (slots[:, None] == jnp.arange(length, dtype=jnp.int32)[None, :]).astype(BF16)

    def to_pair(x):
        own = lax.dynamic_index_in_dim(x, core, 0, keepdims=False)
        other = lax.dynamic_index_in_dim(x, 1 - core, 0, keepdims=False)
        return jnp.stack([own, swap(other, 1)])

    def to_experts(x):
        pair = to_pair(x)
        return jnp.concatenate([pair, swap(pair, 2)], 0)

    upstream_pair = to_pair(dot(select, out_grad).astype(BF16).reshape(experts, cap, width))

    pieces, arrays = ring_gather(
        jnp.concatenate([qkv_block, small_block], 1),
        n_shard,
        (swap(hidden_in, 2), cosine, sine, upstream_pair, output_block, gate_up_block, down_block),
    )
    hidden_side, cosine, sine, upstream_pair, output_block, gate_up_block, down_block = arrays
    hidden_all = jnp.concatenate(
        [hidden_in, swap(hidden_in, 1), hidden_side, swap(hidden_side, 1)], 0
    )
    normed_scale = rms_scale(hidden_all.astype(F32))
    piece, k, first = pieces[-1]
    piece, normed_scale = tie(piece, normed_scale)
    pieces[-1] = (piece, k, first)
    ids = ring_ids(n_shard)
    starts = np.stack([ids[:, k] * my_rows + first for _, k, first in pieces], 1)
    starts, ring = of_shard(starts, shard), of_shard(ids, shard)
    w_qkv, small_w = place_rows([piece for piece, _, _ in pieces], starts, width, 3 * part)
    router_w = small_w[:, :routed]
    gains = small_w[:, routed : routed + 4].T.astype(F32)
    w_out_part = shard_gather(output_block).reshape(n_shard, quarter, width)
    w_gu = shard_gather(gate_up_block)
    w_dn = shard_gather(down_block)
    gain_one, gain_two = gains[0], gains[3]
    gain_query = lax.dynamic_slice_in_dim(gains[1:2], rep * part, part, 1)
    gain_key = lax.dynamic_slice_in_dim(gains[2:3], rep * part, part, 1)

    upstream = out_grad.astype(F32)

    def send_side(x, send):
        return swap(x[2:].astype(send), 2)

    def from_experts(x, there, send):
        pair = x[:2] + there.astype(F32)
        other = swap(pair[1].astype(send), 1).astype(F32)
        first = jnp.where(core == 0, pair[0], other)
        return jnp.stack([first, jnp.where(core == 0, other, pair[0])])

    def add_slots(x):
        high, low = split_sum(x.reshape(experts * cap, width))
        return dot(select, high, ((0,), (0,))) + dot(select, low, ((0,), (0,)))

    normed = (hidden_all.astype(F32) * normed_scale * gain_one).astype(BF16)
    w_qkv, upstream_pair = tie(w_qkv, upstream_pair)
    qkv, upstream_side = tie(dot(normed, w_qkv), swap(upstream_pair, 2))
    slot_upstream = jnp.concatenate([upstream_pair, upstream_side], 0)
    query_raw, key_raw = qkv[:, :part], qkv[:, part : 2 * part]
    squares = jnp.stack([jnp.sum(query_raw * query_raw, -1), jnp.sum(key_raw * key_raw, -1)], -1)
    squares = rep_sum(squares.reshape(4, length, 2)).reshape(-1, 2)
    scales = lax.rsqrt(squares / width + EPSILON)
    query_scale, key_scale = scales[:, :1], scales[:, 1:]
    scales, w_out_part = tie(scales, w_out_part)
    out_core, out_side = swap(w_out_part, 1), swap(w_out_part, 2)
    mixed_heads, queries, keys, values = attend(
        qkv,
        query_scale,
        key_scale,
        gain_query,
        gain_key,
        cosine,
        sine,
        doc_col,
        doc_row,
        heads,
        dim,
    )
    mixed_heads, out_core, out_side = tie(mixed_heads, out_core, out_side)
    blocks = mixed_heads.reshape(4, length, part)
    from_side = swap(blocks[2:], 2)
    out_pieces = in_order([w_out_part, out_core, out_side, swap(out_side, 1)], rep)
    output_w = jnp.stack(out_pieces, 1).reshape(width, width)
    from_side, w_gu, output_w = tie(from_side, w_gu, output_w)
    mixed = jnp.concatenate(
        in_order([blocks[0], swap(blocks[1], 1), from_side[0], swap(from_side[1], 1)], rep), 1
    )
    hidden = hidden_in.astype(F32)
    residual = hidden + dot(mixed, output_w)
    scale_two = rms_scale(residual)
    inner = (residual * scale_two * gain_two).astype(BF16)
    logits = dot(inner, router_w)
    probs_all = jax.nn.softmax(logits, axis=-1)
    named = jnp.sum(
        (expert_ids[:, :, None] == jnp.arange(experts, dtype=jnp.int32)).astype(F32), 1
    )
    window = probs_all[:, :experts] * named
    select_wide = select.reshape(experts, cap, length).astype(F32)
    slot_gates = to_experts(jnp.sum(select_wide * window.T[:, None, :], -1))
    pair = to_pair(dot(select, inner).astype(BF16).reshape(experts, cap, width))
    normed_ring = normed_in_order(ring, hidden_all, normed_scale, gain_one[None])
    at = lambda x, i, axis: lax.dynamic_index_in_dim(x, i, axis, keepdims=False)
    half = lambda which: at(mixed.reshape(length, n_shard, 2, 2, quarter), which, 3).reshape(
        length, width // 2
    )
    from_side, normed_ring, mixed_own, mixed_other = tie(
        swap(pair, 2), normed_ring, half(core), half(1 - core)
    )
    slot_inputs = jnp.concatenate([pair, from_side], 0)
    slot_inputs = slot_inputs.reshape(4 * cap, width)

    gate_up = dot(slot_inputs, w_gu)
    gate_part, up_part = gate_up[:, :half_units], gate_up[:, half_units:]
    sigma = jax.nn.sigmoid(gate_part)
    swished = gate_part * sigma
    activated = (swished * up_part).astype(BF16)
    returned = dot(activated, w_dn).reshape(4, cap, width)
    slot_gate_grad = jnp.sum(returned * slot_upstream.astype(F32), -1)
    slot_gate_grad = from_experts(slot_gate_grad, send_side(slot_gate_grad, F32), F32)
    returned_grad = (slot_gates[:, :, None] * slot_upstream.astype(F32)).astype(BF16)
    returned_grad = returned_grad.reshape(4 * cap, width)
    act_grad = dot(returned_grad, w_dn, ((1,), (1,)))
    gate_grad = act_grad * up_part * sigma * (1.0 + gate_part * (1.0 - sigma))
    gate_up_grad = jnp.concatenate([gate_grad.astype(BF16), (act_grad * swished).astype(BF16)], 1)
    slot_input_grad = dot(gate_up_grad, w_gu, ((1,), (1,))).reshape(4, cap, width)
    down_w_grad = dot(activated, returned_grad, ((0,), (0,))).astype(BF16)
    gate_up_w_grad = dot(slot_inputs, gate_up_grad, ((0,), (0,))).astype(BF16)
    there, down_w_grad, gate_up_w_grad = tie(
        send_side(slot_input_grad, BF16), down_w_grad, gate_up_w_grad
    )
    slot_input_grad = from_experts(slot_input_grad, there, BF16)
    gate_up_owned = shard_scatter(gate_up_w_grad)
    down_owned = shard_scatter(down_w_grad)

    window_grad = jnp.sum(select_wide * slot_gate_grad[:, :, None], 1).T
    chosen_grad = jnp.concatenate(
        [window_grad * named, jnp.zeros((length, routed - experts), F32)], 1
    )
    logits_grad = (
        probs_all * (chosen_grad - jnp.sum(probs_all * chosen_grad, -1, keepdims=True))
    ).astype(BF16)
    router_grad = dot(inner, logits_grad, ((0,), (0,)))
    inner_grad = add_slots(slot_input_grad) + dot(logits_grad, router_w, ((1,), (1,)))
    residual_part, gain_two_grad = norm_back(residual, scale_two, gain_two, inner_grad)
    residual_grad = upstream + residual_part
    branch_grad = residual_grad.astype(BF16)
    mixed_grad = dot(branch_grad, output_w, ((1,), (1,))).astype(BF16)
    piece = lambda j: lax.dynamic_slice_in_dim(mixed_grad, (rep ^ j) * part, part, 1)
    from_side = swap(jnp.stack([piece(2), piece(3)]), 2)
    from_core, branch_grad = tie(swap(piece(1), 1), branch_grad)
    half_grad = lambda half: dot(half, branch_grad, ((0,), (0,))).astype(BF16)
    out_there = swap(half_grad(mixed_other), 1)
    out_w_grad = (half_grad(mixed_own).astype(F32) + out_there).astype(BF16)
    from_side, out_w_grad, returned = tie(from_side, out_w_grad, returned)
    grads = jnp.concatenate([piece(0), from_core, from_side[0], swap(from_side[1], 1)], 0)
    out_w_grad = out_w_grad.reshape(n_shard, 2, quarter, width)
    out_there = swap(at(out_w_grad, 1 - side, 1), 2)

    query_grad, key_grad, value_grad = attend_back(
        queries, keys, values, grads, cosine, sine, doc_col, doc_row, heads, dim
    )
    value_grad, out_there = tie(value_grad, out_there)
    out_w_grad = (at(out_w_grad, side, 1).astype(F32) + out_there).astype(BF16)
    out_owned = shard_scatter(out_w_grad.reshape(n_shard * quarter, width))
    weighted_q, weighted_k = query_grad * gain_query, key_grad * gain_key
    means = jnp.stack(
        [jnp.sum(weighted_q * query_raw, -1), jnp.sum(weighted_k * key_raw, -1)], -1
    )
    means = rep_sum(means.reshape(4, length, 2)).reshape(-1, 2) / width
    means, returned = tie(means, returned)
    returned_there = send_side(returned, BF16)
    gain_query_grad = jnp.sum(query_grad * query_raw * query_scale, 0)
    gain_key_grad = jnp.sum(key_grad * key_raw * key_scale, 0)
    query_raw_grad = query_scale * weighted_q - query_raw * query_scale**3 * means[:, :1]
    key_raw_grad = key_scale * weighted_k - key_raw * key_scale**3 * means[:, 1:]
    qkv_grad = jnp.concatenate(
        [query_raw_grad.astype(BF16), key_raw_grad.astype(BF16), value_grad], 1
    )
    qkv_w_grad = dot(normed_ring, qkv_grad, ((0,), (0,))).astype(BF16)
    qkv_grad, qkv_w_grad, returned_there, gate_up_owned = tie(
        qkv_grad, qkv_w_grad, returned_there, gate_up_owned
    )
    own_gates = jnp.sum(select_wide * window.T[:, None, :], -1)
    returned = from_experts(returned, returned_there, BF16)
    output = (residual + add_slots(own_gates[:, :, None] * returned)).astype(BF16)
    place = lambda g: lax.dynamic_update_slice_in_dim(
        jnp.zeros((width,), F32), g, rep * part, 0
    )
    small = jnp.stack([gain_two_grad, place(gain_query_grad), place(gain_key_grad)], 1)
    small = jnp.concatenate(
        [router_grad, small, jnp.zeros((width, 128 - 3 - routed), F32)], 1
    )
    back = lambda slots, j: dot(
        slots.reshape(4, length, 3 * part)[j], w_qkv, ((1,), (1,))
    )
    due = (
        lambda: (qkv_grad, back(qkv_grad, 1), back(qkv_grad, 3)),
        lambda slots, one, three: (
            slots,
            back(slots, 2),
            swap(jnp.stack([one, three]).astype(BF16), 1),
        ),
        lambda slots, two, from_core: (
            back(slots, 0) + from_core[0].astype(F32),
            (two + from_core[1].astype(F32)).astype(BF16)[length // 2 :],
            swap((two + from_core[1].astype(F32)).astype(BF16)[: length // 2], 2),
            down_owned,
        ),
        lambda zero, rest, top, down: (zero, top, swap(rest, 2), down),
    )
    qkv_owned, (normed_grad, top, rest, down_owned) = ring_scatter(
        [qkv_w_grad, rows_in_order(ring, small)], n_shard, due
    )
    normed_grad = normed_grad + jnp.concatenate([top, rest], 0).astype(F32)
    weighted = normed_grad * gain_one
    scale_one = normed_scale[:length]
    inner_mean = jnp.mean(weighted * hidden, -1, keepdims=True)
    hidden_part = scale_one * weighted - hidden * scale_one * scale_one * scale_one * inner_mean
    input_grad = residual_grad + hidden_part

    gain_part = jnp.sum(qkv_block.astype(F32) * qkv_owned[:, : 3 * part], 1, keepdims=True)
    column = jnp.arange(128)[None, :] == routed + 3
    qkv_owned = jnp.concatenate(
        [qkv_owned[:, : 3 * part], jnp.where(column, gain_part, qkv_owned[:, 3 * part :])], 1
    ).astype(BF16)
    qkv_core, qkv_side, out_owned = tie(swap(qkv_owned, 1), swap(qkv_owned, 2), out_owned)
    qkv_pieces = in_order([qkv_owned, qkv_core, qkv_side, swap(qkv_side, 1)], rep)
    spread = lambda i: jnp.concatenate(
        [p[:, i * part : (i + 1) * part] for p in qkv_pieces], 1
    ).astype(F32)
    grads_qkv = [spread(i) for i in range(3)]
    small = sum(p[:, 3 * part :].astype(F32) for p in qkv_pieces)
    gain_one_grad = small[:, routed + 3] / attn_gain.astype(F32)
    out_full = jnp.concatenate(in_order(rep_gather(out_owned.astype(BF16)), rep), 0).astype(F32)
    gu_pieces = in_order(rep_gather(gate_up_owned.astype(BF16)), rep)
    dn_pieces = in_order(rep_gather(down_owned.astype(BF16)), rep)
    one, two = choose(0), choose(1)
    join = lambda i: jnp.stack(
        [
            dot(gu_pieces[e][:, i * half_units : (i + 1) * half_units], one, ((1,), (1,)))
            + dot(gu_pieces[2 + e][:, i * half_units : (i + 1) * half_units], two, ((1,), (1,)))
            for e in range(experts)
        ]
    )
    down_full = jnp.stack(
        [jnp.concatenate([dn_pieces[e], dn_pieces[2 + e]], 0) for e in range(experts)]
    ).astype(F32)
    return (
        output,
        input_grad,
        gain_one_grad,
        *grads_qkv,
        small[:, routed + 1],
        small[:, routed + 2],
        out_full,
        small[:, routed],
        small[:, :routed],
        join(0),
        join(1),
        down_full,
    )


def solution(mesh):
    tokens = P(("shard", "rep"), None)
    rows = P("shard", None)
    middle = P(None, "shard", None)
    return jax.shard_map(
        functools.partial(local, mesh.shape["shard"]),
        mesh=mesh,
        in_specs=(
            tokens,
            tokens,
            tokens,
            P(("shard", "rep"), None, None),
            tokens,
            P("shard"),
            rows,
            rows,
            rows,
            P("shard"),
            P("shard"),
            rows,
            P("shard"),
            rows,
            middle,
            middle,
            middle,
        ),
        out_specs=(
            tokens,
            tokens,
            P("shard"),
            rows,
            rows,
            rows,
            P("shard"),
            P("shard"),
            rows,
            P("shard"),
            rows,
            middle,
            middle,
            middle,
        ),
        check_vma=False,
    )
```

```python
import functools

import jax
import jax.numpy as jnp
import numpy as np
from jax import lax
from jax.experimental import pallas as pl
from jax.experimental.pallas import tpu as pltpu
from jax.sharding import PartitionSpec as P

HEADS = 16
EPSILON = 1e-05
THETA = 10000.0
REACH = 2
ROWS = 128
COVER = 1 << 27
F32 = jnp.float32
BF16 = jnp.bfloat16


def rms_scale(values):
    return lax.rsqrt(jnp.mean(values * values, -1, keepdims=True) + EPSILON)


def norm_back(values, scale, gain, upstream):
    gain_grad = jnp.sum(upstream * values * scale, 0)
    weighted = upstream * gain
    inner_mean = jnp.mean(weighted * values, -1, keepdims=True)
    return (scale * weighted - values * scale * scale * scale * inner_mean, gain_grad)


def dot(a, b, dims=((1,), (0,))):
    return lax.dot_general(a, b, (dims, ((), ())), preferred_element_type=F32)


def swap(x, mask):
    return lax.ppermute(x, "rep", [(i, i ^ mask) for i in range(4)])


def flip(x, mask):
    return jnp.stack([x[j ^ mask] for j in range(4)])


def rep_sum(x):
    x = x + flip(swap(x, 1), 1)
    return x + flip(swap(x, 2), 2)


def rep_gather(x):
    one, two = swap(x, 1), swap(x, 2)
    return [x, one, two, swap(two, 1)]


def in_order(pieces, rep):
    low = rep % 2 == 1
    high = rep // 2 == 1
    a, b, c, d = pieces
    a, b = jnp.where(low, b, a), jnp.where(low, a, b)
    c, d = jnp.where(low, d, c), jnp.where(low, c, d)
    return (
        jnp.where(high, c, a),
        jnp.where(high, d, b),
        jnp.where(high, a, c),
        jnp.where(high, b, d),
    )


def mask_bias(bias, doc_col, doc_row):
    length = doc_col.shape[0]
    rows = lax.broadcasted_iota(jnp.int32, (length, length), 0)
    cols = lax.broadcasted_iota(jnp.int32, (length, length), 1)
    allowed = (doc_col[...] == doc_row[0]) & (cols <= rows)
    bias[...] = jnp.where(allowed, 0.0, -jnp.inf).astype(F32)


def turn(values, cosine, sine):
    half = values.shape[-1] // 2
    lanes = lax.broadcasted_iota(jnp.int32, values.shape, 1)
    turned = jnp.where(lanes < half, -1.0, 1.0) * pltpu.roll(values, half, 1)
    return values * cosine + turned * sine


def turn_back(values, cosine, sine):
    half = values.shape[-1] // 2
    lanes = lax.broadcasted_iota(jnp.int32, values.shape, 1)
    moved = pltpu.roll(values * sine, half, 1)
    return values * cosine + jnp.where(lanes < half, 1.0, -1.0) * moved


def spans(length):
    return [
        (i * ROWS, (i + 1) * ROWS, max(0, (i - REACH) * ROWS)) for i in range(length // ROWS)
    ]


def attend_kernel(
    factor,
    q_ref,
    k_ref,
    v_ref,
    q_scale,
    k_scale,
    q_gain,
    k_gain,
    cosine,
    sine,
    doc_col,
    doc_row,
    mixed_ref,
    queries_ref,
    keys_ref,
    values_ref,
    bias,
):
    @pl.when(pl.program_id(1) == 0)
    def _():
        mask_bias(bias, doc_col, doc_row)

    cos, sin = cosine[...], sine[...]
    queries_ref[...] = turn(q_ref[...] * q_scale[...] * q_gain[...], cos, sin).astype(BF16)
    keys_ref[...] = turn(k_ref[...] * k_scale[...] * k_gain[...], cos, sin).astype(BF16)
    values_ref[...] = v_ref[...].astype(BF16)
    for start, end, low in spans(q_ref.shape[0]):
        scores = dot(queries_ref[start:end], keys_ref[low:end], ((1,), (1,))) * factor
        scores = scores + bias[start:end, low:end]
        weights = jnp.exp(scores - jnp.max(scores, -1, keepdims=True))
        probs = (weights * (1.0 / jnp.sum(weights, -1, keepdims=True))).astype(BF16)
        mixed_ref[start:end] = dot(probs, values_ref[low:end]).astype(BF16)


def attend_back_kernel(
    factor,
    queries,
    keys,
    values,
    grads,
    cosine,
    sine,
    doc_col,
    doc_row,
    dq_ref,
    dk_ref,
    dv_ref,
    bias,
    dk_sum,
    dv_sum,
):
    @pl.when(pl.program_id(1) == 0)
    def _():
        mask_bias(bias, doc_col, doc_row)

    cos, sin = cosine[...], sine[...]
    dk_sum[...] = jnp.zeros_like(dk_sum)
    dv_sum[...] = jnp.zeros_like(dv_sum)
    for start, end, low in spans(queries.shape[0]):
        q, g = queries[start:end], grads[start:end]
        k, v = keys[low:end], values[low:end]
        scores = dot(q, k, ((1,), (1,))) * factor + bias[start:end, low:end]
        weights = jnp.exp(scores - jnp.max(scores, -1, keepdims=True))
        probs = weights * (1.0 / jnp.sum(weights, -1, keepdims=True))
        dv_sum[low:end] += dot(probs.astype(BF16), g, ((0,), (0,)))
        prob_grad = dot(g, v, ((1,), (1,)))
        score_grad = probs * (prob_grad - jnp.sum(probs * prob_grad, -1, keepdims=True))
        score_grad = score_grad.astype(BF16)
        dq_ref[start:end] = turn_back(dot(score_grad, k) * factor, cos[start:end], sin[start:end])
        dk_sum[low:end] += dot(score_grad, q, ((0,), (0,)))
    dk_ref[...] = turn_back(dk_sum[...] * factor, cos, sin)
    dv_ref[...] = dv_sum[...].astype(BF16)


def cost(flops, moved, exps=0):
    return pl.CostEstimate(flops=flops, bytes_accessed=moved, transcendentals=exps)


def attend(qkv, q_scale, k_scale, q_gain, k_gain, cosine, sine, doc_col, doc_row, heads, dim):
    tokens = qkv.shape[0]
    length = doc_row.shape[-1]
    block = lambda off: pl.BlockSpec((length, dim), lambda j, h: (j, off + h))
    per_row = pl.BlockSpec((length, 1), lambda j, h: (j, 0))
    table = pl.BlockSpec((length, dim), lambda j, h: (j, 0))
    gain = pl.BlockSpec((1, dim), lambda j, h: (0, h))
    row = pl.BlockSpec((1, 1, length), lambda j, h: (j, 0, 0))
    out = jax.ShapeDtypeStruct((tokens, heads * dim), BF16)
    return pl.pallas_call(
        functools.partial(attend_kernel, dim ** (-0.5)),
        grid=(tokens // length, heads),
        in_specs=[block(0), block(heads), block(2 * heads), per_row, per_row, gain, gain]
        + [table, table, per_row, row],
        out_specs=[block(0)] * 4,
        out_shape=[out] * 4,
        scratch_shapes=[pltpu.VMEM((length, length), F32)],
        cost_estimate=cost(
            4 * tokens * length * heads * dim, tokens * heads * dim * 20, tokens * length * heads
        ),
        name="attend",
    )(qkv, qkv, qkv, q_scale, k_scale, q_gain, k_gain, cosine, sine, doc_col, doc_row)


def attend_back(queries, keys, values, grads, cosine, sine, doc_col, doc_row, heads, dim):
    tokens = queries.shape[0]
    length = doc_row.shape[-1]
    block = pl.BlockSpec((length, dim), lambda j, h: (j, h))
    per_row = pl.BlockSpec((length, 1), lambda j, h: (j, 0))
    table = pl.BlockSpec((length, dim), lambda j, h: (j, 0))
    row = pl.BlockSpec((1, 1, length), lambda j, h: (j, 0, 0))
    wide = jax.ShapeDtypeStruct((tokens, heads * dim), F32)
    return pl.pallas_call(
        functools.partial(attend_back_kernel, dim ** (-0.5)),
        grid=(tokens // length, heads),
        in_specs=[block] * 4 + [table, table, per_row, row],
        out_specs=[block] * 3,
        out_shape=[wide, wide, jax.ShapeDtypeStruct((tokens, heads * dim), BF16)],
        scratch_shapes=[
            pltpu.VMEM((length, length), F32),
            pltpu.VMEM((length, dim), F32),
            pltpu.VMEM((length, dim), F32),
        ],
        cost_estimate=cost(
            10 * tokens * length * heads * dim, tokens * heads * dim * 18, tokens * length * heads
        ),
        name="attend_back",
    )(queries, keys, values, grads, cosine, sine, doc_col, doc_row)


def tie(*arrays):
    return lax.optimization_barrier(arrays)


def ring_of(n):
    return list(range(0, n, 2)) + list(range(n - 1, 0, -2))


def ring_step(x, n, back=False):
    ring = ring_of(n)
    pairs = [(ring[i], ring[(i + 1) % n]) for i in range(n)]
    return lax.ppermute(x, "shard", [(b, a) for a, b in pairs] if back else pairs)


def ring_ids(n):
    ring = ring_of(n)
    return np.array([[ring[(ring.index(s) + i) % n] for i in range(n)] for s in range(n)], np.int32)


def of_shard(table, shard):
    return lax.dynamic_index_in_dim(jnp.asarray(table), shard, 0, keepdims=False)


def ring_gather(block, n, due):
    half = block.shape[0] // 2
    pieces = [(block, 0, 0)]
    ahead = behind = block
    for k in range(1, n // 2):
        behind, ahead = tie(ring_step(behind, n), ring_step(ahead, n, True))
        if k == n // 2 - 1:
            behind, ahead, *due = tie(behind, ahead, *due)
        pieces += [(behind, n - k, 0), (ahead, k, 0)]
    pieces.append((ring_step(behind[:half], n), n // 2, 0))
    pieces.append((ring_step(ahead[half:], n, True), n // 2, half))
    return pieces, due


def place_kernel(n, cut, starts, *refs):
    ins, outs, bufs = refs[:n], refs[n : n + 2], refs[n + 2 : 2 * n + 2]
    sem_in, sem_out = refs[-2], refs[-1]
    loads = [pltpu.make_async_copy(ins[i], bufs[i], sem_in.at[i]) for i in range(n)]
    for load in loads:
        load.start()
    stores = []
    for i in range(n):
        loads[i].wait()
        at = pl.multiple_of(starts[i], 16)
        rows, cols = bufs[i].shape
        for o, first, size in ((0, 0, cut), (1, cut, cols - cut)):
            stores.append(
                pltpu.make_async_copy(
                    bufs[i].at[:, pl.ds(first, size)],
                    outs[o].at[pl.ds(at, rows)],
                    sem_out.at[2 * i + o],
                )
            )
            stores[-1].start()
    for store in stores:
        store.wait()


def place_rows(pieces, starts, rows, cut):
    cols = pieces[0].shape[1]
    n = len(pieces)
    anywhere = pl.BlockSpec(memory_space=pl.ANY)
    return pl.pallas_call(
        functools.partial(place_kernel, n, cut),
        grid_spec=pltpu.PrefetchScalarGridSpec(
            num_scalar_prefetch=1,
            grid=(),
            in_specs=[anywhere] * n,
            out_specs=[anywhere] * 2,
            scratch_shapes=[pltpu.VMEM(x.shape, x.dtype) for x in pieces]
            + [pltpu.SemaphoreType.DMA((n,)), pltpu.SemaphoreType.DMA((2 * n,))],
        ),
        out_shape=[
            jax.ShapeDtypeStruct((rows, size), pieces[0].dtype) for size in (cut, cols - cut)
        ],
        cost_estimate=cost(0, 4 * rows * cols),
        name="place_rows",
    )(starts, *pieces)


def normed_kernel(ids, hidden, scale, gain, out):
    out[...] = (hidden[...].astype(F32) * scale[...] * gain[...]).astype(BF16)


def normed_in_order(ids, hidden, scale, gain):
    n = ids.shape[0]
    rows, cols = hidden.shape
    if cols // n % 128:
        normed = (hidden.astype(F32) * scale * gain).astype(BF16)
        return normed.reshape(rows, n, cols // n)[:, ids].reshape(rows, cols)
    return pl.pallas_call(
        normed_kernel,
        grid_spec=pltpu.PrefetchScalarGridSpec(
            num_scalar_prefetch=1,
            grid=(n,),
            in_specs=[
                pl.BlockSpec((rows, cols // n), lambda i, ids: (0, ids[i])),
                pl.BlockSpec((rows, 1), lambda i, ids: (0, 0)),
                pl.BlockSpec((1, cols // n), lambda i, ids: (0, ids[i])),
            ],
            out_specs=pl.BlockSpec((rows, cols // n), lambda i, ids: (0, i)),
        ),
        out_shape=jax.ShapeDtypeStruct((rows, cols), BF16),
        cost_estimate=cost(0, COVER),
        name="normed_in_order",
    )(ids, hidden, scale, gain)


def back_kernel(x, w, out):
    out[0] = dot(x[...], w[...], ((1,), (1,))).astype(out.dtype)


def back_product(x, w, first, count, rows, dtype):
    inner = x.shape[1]
    cols = w.shape[0]
    step = 512
    return pl.pallas_call(
        back_kernel,
        grid=(count, cols // step),
        in_specs=[
            pl.BlockSpec((rows, inner), lambda j, i: (first + 2 * j, 0)),
            pl.BlockSpec((step, inner), lambda j, i: (i, 0)),
        ],
        out_specs=pl.BlockSpec((1, rows, step), lambda j, i: (j, 0, i)),
        out_shape=jax.ShapeDtypeStruct((count, rows, cols), dtype),
        cost_estimate=cost(0, COVER),
        name="back_product",
    )(x, w)


def rows_kernel(ids, x, out):
    out[...] = x[...].astype(out.dtype)


def rows_in_order(ids, x):
    n = ids.shape[0]
    rows, cols = x.shape
    return pl.pallas_call(
        rows_kernel,
        grid_spec=pltpu.PrefetchScalarGridSpec(
            num_scalar_prefetch=1,
            grid=(n,),
            in_specs=[pl.BlockSpec((rows // n, cols), lambda i, ids: (ids[i], 0))],
            out_specs=pl.BlockSpec((rows // n, cols), lambda i, ids: (i, 0)),
        ),
        out_shape=jax.ShapeDtypeStruct((rows, cols), BF16),
        cost_estimate=cost(0, 4 * rows * cols),
        name="rows_in_order",
    )(ids, x)


def ring_scatter(parts, n, due):
    rows = parts[0].shape[0] // n
    half = rows // 2
    chunk = lambda k, first=0, size=rows: jnp.concatenate(
        [x[k % n * rows + first : k % n * rows + first + size] for x in parts], 1
    )
    done = []
    ahead = ring_step(chunk(n // 2, 0, half), n)
    behind = ring_step(chunk(n // 2, half, half), n, True)
    for k in range(n // 2 - 1, -1, -1):
        at = n // 2 - 1 - k
        ahead, behind, *got = tie(ahead, behind, *(due[at](*done) if at < len(due) else ()))
        done = got or done
        if k == 0:
            break
        a, b = chunk(k), chunk(n - k)
        if at == 0:
            a = jnp.concatenate([a[:half].astype(F32) + ahead, a[half:]], 0)
            b = jnp.concatenate([b[:half], b[half:].astype(F32) + behind], 0)
        else:
            a, b = a.astype(F32) + ahead, b.astype(F32) + behind
        ahead, behind = ring_step(a.astype(BF16), n), ring_step(b.astype(BF16), n, True)
    return chunk(0).astype(F32) + ahead + behind, done


def shard_gather(x):
    return lax.all_gather(x, "shard", axis=0, tiled=True)


def shard_scatter(x):
    return lax.psum_scatter(x, "shard", scatter_dimension=0, tiled=True).astype(F32)


def split_sum(x):
    high = x.astype(BF16)
    return high, (x - high.astype(F32)).astype(BF16)


def local(
    n_shard,
    hidden_in,
    doc_ids,
    expert_ids,
    slot_rows,
    out_grad,
    attn_gain,
    w_query,
    w_key,
    w_value,
    query_gain,
    key_gain,
    w_output,
    ffn_gain,
    w_router,
    w_gate,
    w_up,
    w_down,
):
    length, width = hidden_in.shape
    dim = width // HEADS
    heads = HEADS // 4
    part = width // 4
    routed = w_router.shape[1]
    experts = w_gate.shape[0]
    hidden_units = w_gate.shape[2]
    half_units = hidden_units // 2
    cap = slot_rows.shape[2]
    rep = lax.axis_index("rep")
    shard = lax.axis_index("shard")
    core, side = rep % 2, rep // 2
    my_rows = width // n_shard
    quarter = my_rows // 4

    cut = lambda w: lax.dynamic_slice_in_dim(w, rep * part, part, 1)
    qkv_block = jnp.concatenate([cut(w_query), cut(w_key), cut(w_value)], 1)
    output_block = lax.dynamic_slice_in_dim(w_output, rep * quarter, quarter, 0)
    pick = lambda w: lax.dynamic_index_in_dim(w, core, 0, keepdims=False)
    down_rows = hidden_units // n_shard
    unit = jnp.arange(half_units)
    unit = (unit // (down_rows // 2)) * down_rows + unit % (down_rows // 2)
    choose = lambda which: (
        jnp.arange(hidden_units)[:, None] == (unit + which * (down_rows // 2))[None, :]
    ).astype(BF16)
    mine = choose(side)
    gate_up_block = jnp.concatenate(
        [dot(pick(w_gate), mine).astype(BF16), dot(pick(w_up), mine).astype(BF16)], 1
    )
    down_block = lax.dynamic_slice_in_dim(pick(w_down), side * (down_rows // 2), down_rows // 2, 0)
    small_block = jnp.concatenate(
        [w_router, jnp.stack([attn_gain, query_gain, key_gain, ffn_gain], 1)]
        + [jnp.zeros((my_rows, 128 - 4 - routed), BF16)],
        1,
    )

    docs_all = jnp.concatenate(rep_gather(doc_ids), 0)
    before = docs_all[:, None, :] < docs_all[:, :, None]
    starts = jnp.sum(before.astype(jnp.int32), -1)
    places = (jnp.arange(length, dtype=jnp.int32)[None, :] - starts).astype(F32).reshape(-1)
    rates = THETA ** (-jnp.arange(dim // 2, dtype=F32) * 2.0 / dim)
    angles = places[:, None] * jnp.concatenate([rates, rates])[None, :]
    cosine, sine = jnp.cos(angles), jnp.sin(angles)
    doc_col = docs_all.reshape(-1, 1)
    doc_row = docs_all.reshape(4, 1, length)
    slots = slot_rows[0].reshape(experts * cap)
    select = (slots[:, None] == jnp.arange(length, dtype=jnp.int32)[None, :]).astype(BF16)

    def to_pair(x):
        own = lax.dynamic_index_in_dim(x, core, 0, keepdims=False)
        other = lax.dynamic_index_in_dim(x, 1 - core, 0, keepdims=False)
        return jnp.stack([own, swap(other, 1)])

    def to_experts(x):
        pair = to_pair(x)
        return jnp.concatenate([pair, swap(pair, 2)], 0)

    upstream_pair = to_pair(dot(select, out_grad).astype(BF16).reshape(experts, cap, width))

    pieces, arrays = ring_gather(
        jnp.concatenate([qkv_block, small_block], 1),
        n_shard,
        (swap(hidden_in, 2), cosine, sine, upstream_pair, output_block, gate_up_block, down_block),
    )
    hidden_side, cosine, sine, upstream_pair, output_block, gate_up_block, down_block = arrays
    hidden_all = jnp.concatenate(
        [hidden_in, swap(hidden_in, 1), hidden_side, swap(hidden_side, 1)], 0
    )
    normed_scale = rms_scale(hidden_all.astype(F32))
    piece, k, first = pieces[-1]
    piece, normed_scale = tie(piece, normed_scale)
    pieces[-1] = (piece, k, first)
    ids = ring_ids(n_shard)
    starts = np.stack([ids[:, k] * my_rows + first for _, k, first in pieces], 1)
    starts, ring = of_shard(starts, shard), of_shard(ids, shard)
    w_qkv, small_w = place_rows([piece for piece, _, _ in pieces], starts, width, 3 * part)
    router_w = small_w[:, :routed]
    gains = small_w[:, routed : routed + 4].T.astype(F32)
    w_out_part = shard_gather(output_block).reshape(n_shard, quarter, width)
    w_gu = shard_gather(gate_up_block)
    w_dn = shard_gather(down_block)
    gain_one, gain_two = gains[0], gains[3]
    gain_query = lax.dynamic_slice_in_dim(gains[1:2], rep * part, part, 1)
    gain_key = lax.dynamic_slice_in_dim(gains[2:3], rep * part, part, 1)

    upstream = out_grad.astype(F32)

    def send_side(x, send):
        return swap(x[2:].astype(send), 2)

    def from_experts(x, there, send):
        pair = x[:2] + there.astype(F32)
        other = swap(pair[1].astype(send), 1).astype(F32)
        first = jnp.where(core == 0, pair[0], other)
        return jnp.stack([first, jnp.where(core == 0, other, pair[0])])

    def add_slots(x):
        high, low = split_sum(x.reshape(experts * cap, width))
        return dot(select, high, ((0,), (0,))) + dot(select, low, ((0,), (0,)))

    normed = (hidden_all.astype(F32) * normed_scale * gain_one).astype(BF16)
    w_qkv, upstream_pair = tie(w_qkv, upstream_pair)
    qkv, upstream_side = tie(dot(normed, w_qkv), swap(upstream_pair, 2))
    slot_upstream = jnp.concatenate([upstream_pair, upstream_side], 0)
    query_raw, key_raw = qkv[:, :part], qkv[:, part : 2 * part]
    squares = jnp.stack([jnp.sum(query_raw * query_raw, -1), jnp.sum(key_raw * key_raw, -1)], -1)
    squares = rep_sum(squares.reshape(4, length, 2)).reshape(-1, 2)
    scales = lax.rsqrt(squares / width + EPSILON)
    query_scale, key_scale = scales[:, :1], scales[:, 1:]
    scales, w_out_part = tie(scales, w_out_part)
    out_core, out_side = swap(w_out_part, 1), swap(w_out_part, 2)
    mixed_heads, queries, keys, values = attend(
        qkv,
        query_scale,
        key_scale,
        gain_query,
        gain_key,
        cosine,
        sine,
        doc_col,
        doc_row,
        heads,
        dim,
    )
    mixed_heads, out_core, out_side = tie(mixed_heads, out_core, out_side)
    blocks = mixed_heads.reshape(4, length, part)
    from_side = swap(blocks[2:], 2)
    out_pieces = in_order([w_out_part, out_core, out_side, swap(out_side, 1)], rep)
    output_w = jnp.stack(out_pieces, 1).reshape(width, width)
    from_core, late_scale = tie(swap(blocks[1], 1), normed_scale)
    normed_ring = normed_in_order(ring, hidden_all, late_scale, gain_one[None])
    from_side, w_gu, output_w, normed_ring = tie(from_side, w_gu, output_w, normed_ring)
    mixed = jnp.concatenate(
        in_order([blocks[0], from_core, from_side[0], swap(from_side[1], 1)], rep), 1
    )
    hidden = hidden_in.astype(F32)
    residual = hidden + dot(mixed, output_w)
    scale_two = rms_scale(residual)
    inner = (residual * scale_two * gain_two).astype(BF16)
    logits = dot(inner, router_w)
    probs_all = jax.nn.softmax(logits, axis=-1)
    named = jnp.sum(
        (expert_ids[:, :, None] == jnp.arange(experts, dtype=jnp.int32)).astype(F32), 1
    )
    window = probs_all[:, :experts] * named
    select_wide = select.reshape(experts, cap, length).astype(F32)
    slot_gates = to_experts(jnp.sum(select_wide * window.T[:, None, :], -1))
    pair = to_pair(dot(select, inner).astype(BF16).reshape(experts, cap, width))
    from_side = swap(pair, 2)
    slot_inputs = jnp.concatenate([pair, from_side], 0)
    slot_inputs = slot_inputs.reshape(4 * cap, width)

    gate_up = dot(slot_inputs, w_gu)
    gate_part, up_part = gate_up[:, :half_units], gate_up[:, half_units:]
    sigma = jax.nn.sigmoid(gate_part)
    swished = gate_part * sigma
    activated = (swished * up_part).astype(BF16)
    returned = dot(activated, w_dn).reshape(4, cap, width)
    slot_gate_grad = jnp.sum(returned * slot_upstream.astype(F32), -1)
    slot_gate_grad = from_experts(slot_gate_grad, send_side(slot_gate_grad, F32), F32)
    returned_grad = (slot_gates[:, :, None] * slot_upstream.astype(F32)).astype(BF16)
    returned_grad = returned_grad.reshape(4 * cap, width)
    act_grad = dot(returned_grad, w_dn, ((1,), (1,)))
    gate_grad = act_grad * up_part * sigma * (1.0 + gate_part * (1.0 - sigma))
    gate_up_grad = jnp.concatenate([gate_grad.astype(BF16), (act_grad * swished).astype(BF16)], 1)
    slot_input_grad = dot(gate_up_grad, w_gu, ((1,), (1,))).reshape(4, cap, width)
    down_w_grad = dot(activated, returned_grad, ((0,), (0,))).astype(BF16)
    gate_up_w_grad = dot(slot_inputs, gate_up_grad, ((0,), (0,))).astype(BF16)
    at = lambda x, i, axis: lax.dynamic_index_in_dim(x, i, axis, keepdims=False)
    half = lambda which: at(mixed.reshape(length, n_shard, 2, 2, quarter), which, 3).reshape(
        length, width // 2
    )
    there, down_w_grad, gate_up_w_grad, mixed_own, mixed_other = tie(
        send_side(slot_input_grad, BF16),
        down_w_grad,
        gate_up_w_grad,
        half(core),
        half(1 - core),
    )
    slot_input_grad = from_experts(slot_input_grad, there, BF16)
    gate_up_owned = shard_scatter(gate_up_w_grad)
    down_owned = shard_scatter(down_w_grad)

    window_grad = jnp.sum(select_wide * slot_gate_grad[:, :, None], 1).T
    chosen_grad = jnp.concatenate(
        [window_grad * named, jnp.zeros((length, routed - experts), F32)], 1
    )
    logits_grad = (
        probs_all * (chosen_grad - jnp.sum(probs_all * chosen_grad, -1, keepdims=True))
    ).astype(BF16)
    router_grad = dot(inner, logits_grad, ((0,), (0,)))
    inner_grad = add_slots(slot_input_grad) + dot(logits_grad, router_w, ((1,), (1,)))
    residual_part, gain_two_grad = norm_back(residual, scale_two, gain_two, inner_grad)
    residual_grad = upstream + residual_part
    branch_grad = residual_grad.astype(BF16)
    mixed_grad = dot(branch_grad, output_w, ((1,), (1,))).astype(BF16)
    piece = lambda j: lax.dynamic_slice_in_dim(mixed_grad, (rep ^ j) * part, part, 1)
    from_side = swap(jnp.stack([piece(2), piece(3)]), 2)
    from_core, branch_grad = tie(swap(piece(1), 1), branch_grad)
    half_grad = lambda half: dot(half, branch_grad, ((0,), (0,))).astype(BF16)
    out_there = swap(half_grad(mixed_other), 1)
    out_w_grad = (half_grad(mixed_own).astype(F32) + out_there).astype(BF16)
    from_side, out_w_grad, returned = tie(from_side, out_w_grad, returned)
    grads = jnp.concatenate([piece(0), from_core, from_side[0], swap(from_side[1], 1)], 0)
    out_w_grad = out_w_grad.reshape(n_shard, 2, quarter, width)
    out_there = swap(at(out_w_grad, 1 - side, 1), 2)

    query_grad, key_grad, value_grad = attend_back(
        queries, keys, values, grads, cosine, sine, doc_col, doc_row, heads, dim
    )
    value_grad, out_there = tie(value_grad, out_there)
    out_w_grad = (at(out_w_grad, side, 1).astype(F32) + out_there).astype(BF16)
    out_owned = shard_scatter(out_w_grad.reshape(n_shard * quarter, width))
    weighted_q, weighted_k = query_grad * gain_query, key_grad * gain_key
    means = jnp.stack(
        [jnp.sum(weighted_q * query_raw, -1), jnp.sum(weighted_k * key_raw, -1)], -1
    )
    means = rep_sum(means.reshape(4, length, 2)).reshape(-1, 2) / width
    means, returned = tie(means, returned)
    returned_there = send_side(returned, BF16)
    gain_query_grad = jnp.sum(query_grad * query_raw * query_scale, 0)
    gain_key_grad = jnp.sum(key_grad * key_raw * key_scale, 0)
    query_raw_grad = query_scale * weighted_q - query_raw * query_scale**3 * means[:, :1]
    key_raw_grad = key_scale * weighted_k - key_raw * key_scale**3 * means[:, 1:]
    qkv_grad = jnp.concatenate(
        [query_raw_grad.astype(BF16), key_raw_grad.astype(BF16), value_grad], 1
    )
    qkv_w_grad = dot(normed_ring, qkv_grad, ((0,), (0,))).astype(BF16)
    qkv_grad, qkv_w_grad, returned_there, gate_up_owned = tie(
        qkv_grad, qkv_w_grad, returned_there, gate_up_owned
    )
    own_gates = jnp.sum(select_wide * window.T[:, None, :], -1)
    returned = from_experts(returned, returned_there, BF16)
    output = (residual + add_slots(own_gates[:, :, None] * returned)).astype(BF16)
    place = lambda g: lax.dynamic_update_slice_in_dim(
        jnp.zeros((width,), F32), g, rep * part, 0
    )
    small = jnp.stack([gain_two_grad, place(gain_query_grad), place(gain_key_grad)], 1)
    small = jnp.concatenate(
        [router_grad, small, jnp.zeros((width, 128 - 3 - routed), F32)], 1
    )
    back = lambda slots, first, count, dtype: back_product(
        slots, w_qkv, first, count, length, dtype
    )

    def near(slots, odd):
        odd, slots = tie(swap(odd, 1), slots)
        return slots, back(slots, 2, 1, F32)[0], odd

    due = (
        lambda: (qkv_grad, back(qkv_grad, 1, 2, BF16)),
        near,
        lambda slots, two, from_core: (
            back(slots, 0, 1, F32)[0] + from_core[0].astype(F32),
            (two + from_core[1].astype(F32)).astype(BF16)[length // 2 :],
            swap((two + from_core[1].astype(F32)).astype(BF16)[: length // 2], 2),
            down_owned,
        ),
        lambda zero, rest, top, down: (zero, top, swap(rest, 2), down),
    )
    qkv_owned, (normed_grad, top, rest, down_owned) = ring_scatter(
        [qkv_w_grad, rows_in_order(ring, small)], n_shard, due
    )
    normed_grad = normed_grad + jnp.concatenate([top, rest], 0).astype(F32)
    weighted = normed_grad * gain_one
    scale_one = normed_scale[:length]
    inner_mean = jnp.mean(weighted * hidden, -1, keepdims=True)
    hidden_part = scale_one * weighted - hidden * scale_one * scale_one * scale_one * inner_mean
    input_grad = residual_grad + hidden_part

    gain_part = jnp.sum(qkv_block.astype(F32) * qkv_owned[:, : 3 * part], 1, keepdims=True)
    column = jnp.arange(128)[None, :] == routed + 3
    qkv_owned = jnp.concatenate(
        [qkv_owned[:, : 3 * part], jnp.where(column, gain_part, qkv_owned[:, 3 * part :])], 1
    ).astype(BF16)
    qkv_core, qkv_side, out_owned = tie(swap(qkv_owned, 1), swap(qkv_owned, 2), out_owned)
    qkv_pieces = in_order([qkv_owned, qkv_core, qkv_side, swap(qkv_side, 1)], rep)
    spread = lambda i: jnp.concatenate(
        [p[:, i * part : (i + 1) * part] for p in qkv_pieces], 1
    ).astype(F32)
    grads_qkv = [spread(i) for i in range(3)]
    small = sum(p[:, 3 * part :].astype(F32) for p in qkv_pieces)
    gain_one_grad = small[:, routed + 3] / attn_gain.astype(F32)
    out_full = jnp.concatenate(in_order(rep_gather(out_owned.astype(BF16)), rep), 0).astype(F32)
    gu_pieces = in_order(rep_gather(gate_up_owned.astype(BF16)), rep)
    dn_pieces = in_order(rep_gather(down_owned.astype(BF16)), rep)
    one, two = choose(0), choose(1)
    join = lambda i: jnp.stack(
        [
            dot(gu_pieces[e][:, i * half_units : (i + 1) * half_units], one, ((1,), (1,)))
            + dot(gu_pieces[2 + e][:, i * half_units : (i + 1) * half_units], two, ((1,), (1,)))
            for e in range(experts)
        ]
    )
    down_full = jnp.stack(
        [jnp.concatenate([dn_pieces[e], dn_pieces[2 + e]], 0) for e in range(experts)]
    ).astype(F32)
    return (
        output,
        input_grad,
        gain_one_grad,
        *grads_qkv,
        small[:, routed + 1],
        small[:, routed + 2],
        out_full,
        small[:, routed],
        small[:, :routed],
        join(0),
        join(1),
        down_full,
    )


def solution(mesh):
    tokens = P(("shard", "rep"), None)
    rows = P("shard", None)
    middle = P(None, "shard", None)
    return jax.shard_map(
        functools.partial(local, mesh.shape["shard"]),
        mesh=mesh,
        in_specs=(
            tokens,
            tokens,
            tokens,
            P(("shard", "rep"), None, None),
            tokens,
            P("shard"),
            rows,
            rows,
            rows,
            P("shard"),
            P("shard"),
            rows,
            P("shard"),
            rows,
            middle,
            middle,
            middle,
        ),
        out_specs=(
            tokens,
            tokens,
            P("shard"),
            rows,
            rows,
            rows,
            P("shard"),
            P("shard"),
            rows,
            P("shard"),
            rows,
            middle,
            middle,
            middle,
        ),
        check_vma=False,
    )
```

```python
import functools

import jax
import jax.numpy as jnp
import numpy as np
from jax import lax
from jax.experimental import pallas as pl
from jax.experimental.pallas import tpu as pltpu
from jax.sharding import PartitionSpec as P

HEADS = 16
EPSILON = 1e-05
THETA = 10000.0
REACH = 2
ROWS = 128
COVER = 1 << 27
F32 = jnp.float32
BF16 = jnp.bfloat16


def rms_scale(values):
    return lax.rsqrt(jnp.mean(values * values, -1, keepdims=True) + EPSILON)


def norm_back(values, scale, gain, upstream):
    gain_grad = jnp.sum(upstream * values * scale, 0)
    weighted = upstream * gain
    inner_mean = jnp.mean(weighted * values, -1, keepdims=True)
    return (scale * weighted - values * scale * scale * scale * inner_mean, gain_grad)


def dot(a, b, dims=((1,), (0,))):
    return lax.dot_general(a, b, (dims, ((), ())), preferred_element_type=F32)


def swap(x, mask):
    return lax.ppermute(x, "rep", [(i, i ^ mask) for i in range(4)])


def flip(x, mask):
    return jnp.stack([x[j ^ mask] for j in range(4)])


def rep_sum(x):
    x = x + flip(swap(x, 1), 1)
    return x + flip(swap(x, 2), 2)


def rep_gather(x):
    one, two = swap(x, 1), swap(x, 2)
    return [x, one, two, swap(two, 1)]


def in_order(pieces, rep):
    low = rep % 2 == 1
    high = rep // 2 == 1
    a, b, c, d = pieces
    a, b = jnp.where(low, b, a), jnp.where(low, a, b)
    c, d = jnp.where(low, d, c), jnp.where(low, c, d)
    return (
        jnp.where(high, c, a),
        jnp.where(high, d, b),
        jnp.where(high, a, c),
        jnp.where(high, b, d),
    )


def mask_bias(bias, doc_col, doc_row):
    length = doc_col.shape[0]
    rows = lax.broadcasted_iota(jnp.int32, (length, length), 0)
    cols = lax.broadcasted_iota(jnp.int32, (length, length), 1)
    allowed = (doc_col[...] == doc_row[0]) & (cols <= rows)
    bias[...] = jnp.where(allowed, 0.0, -jnp.inf).astype(F32)


def turn(values, cosine, sine):
    half = values.shape[-1] // 2
    lanes = lax.broadcasted_iota(jnp.int32, values.shape, 1)
    turned = jnp.where(lanes < half, -1.0, 1.0) * pltpu.roll(values, half, 1)
    return values * cosine + turned * sine


def turn_back(values, cosine, sine):
    half = values.shape[-1] // 2
    lanes = lax.broadcasted_iota(jnp.int32, values.shape, 1)
    moved = pltpu.roll(values * sine, half, 1)
    return values * cosine + jnp.where(lanes < half, 1.0, -1.0) * moved


def spans(length):
    return [
        (i * ROWS, (i + 1) * ROWS, max(0, (i - REACH) * ROWS)) for i in range(length // ROWS)
    ]


def attend_kernel(
    factor,
    q_ref,
    k_ref,
    v_ref,
    q_scale,
    k_scale,
    q_gain,
    k_gain,
    cosine,
    sine,
    doc_col,
    doc_row,
    mixed_ref,
    queries_ref,
    keys_ref,
    values_ref,
    bias,
):
    @pl.when(pl.program_id(1) == 0)
    def _():
        mask_bias(bias, doc_col, doc_row)

    cos, sin = cosine[...], sine[...]
    queries_ref[...] = turn(q_ref[...] * q_scale[...] * q_gain[...], cos, sin).astype(BF16)
    keys_ref[...] = turn(k_ref[...] * k_scale[...] * k_gain[...], cos, sin).astype(BF16)
    values_ref[...] = v_ref[...].astype(BF16)
    for start, end, low in spans(q_ref.shape[0]):
        scores = dot(queries_ref[start:end], keys_ref[low:end], ((1,), (1,))) * factor
        scores = scores + bias[start:end, low:end]
        weights = jnp.exp(scores - jnp.max(scores, -1, keepdims=True))
        inverse = 1.0 / jnp.sum(weights, -1, keepdims=True)
        mixed = dot(weights.astype(BF16), values_ref[low:end]) * inverse
        mixed_ref[start:end] = mixed.astype(BF16)


def attend_back_kernel(
    factor,
    queries,
    keys,
    values,
    grads,
    cosine,
    sine,
    doc_col,
    doc_row,
    dq_ref,
    dk_ref,
    dv_ref,
    bias,
    dk_sum,
    dv_sum,
):
    @pl.when(pl.program_id(1) == 0)
    def _():
        mask_bias(bias, doc_col, doc_row)

    cos, sin = cosine[...], sine[...]
    dk_sum[...] = jnp.zeros_like(dk_sum)
    dv_sum[...] = jnp.zeros_like(dv_sum)
    for start, end, low in spans(queries.shape[0]):
        q, g = queries[start:end], grads[start:end]
        k, v = keys[low:end], values[low:end]
        scores = dot(q, k, ((1,), (1,))) * factor + bias[start:end, low:end]
        weights = jnp.exp(scores - jnp.max(scores, -1, keepdims=True))
        probs = weights * (1.0 / jnp.sum(weights, -1, keepdims=True))
        dv_sum[low:end] += dot(probs.astype(BF16), g, ((0,), (0,)))
        prob_grad = dot(g, v, ((1,), (1,)))
        score_grad = probs * (prob_grad - jnp.sum(probs * prob_grad, -1, keepdims=True))
        score_grad = score_grad.astype(BF16)
        dq_ref[start:end] = turn_back(dot(score_grad, k) * factor, cos[start:end], sin[start:end])
        dk_sum[low:end] += dot(score_grad, q, ((0,), (0,)))
    dk_ref[...] = turn_back(dk_sum[...] * factor, cos, sin)
    dv_ref[...] = dv_sum[...].astype(BF16)


def cost(flops, moved, exps=0):
    return pl.CostEstimate(flops=flops, bytes_accessed=moved, transcendentals=exps)


def attend(qkv, q_scale, k_scale, q_gain, k_gain, cosine, sine, doc_col, doc_row, heads, dim):
    tokens = qkv.shape[0]
    length = doc_row.shape[-1]
    block = lambda off: pl.BlockSpec((length, dim), lambda j, h: (j, off + h))
    per_row = pl.BlockSpec((length, 1), lambda j, h: (j, 0))
    table = pl.BlockSpec((length, dim), lambda j, h: (j, 0))
    gain = pl.BlockSpec((1, dim), lambda j, h: (0, h))
    row = pl.BlockSpec((1, 1, length), lambda j, h: (j, 0, 0))
    out = jax.ShapeDtypeStruct((tokens, heads * dim), BF16)
    return pl.pallas_call(
        functools.partial(attend_kernel, dim ** (-0.5)),
        grid=(tokens // length, heads),
        in_specs=[block(0), block(heads), block(2 * heads), per_row, per_row, gain, gain]
        + [table, table, per_row, row],
        out_specs=[block(0)] * 4,
        out_shape=[out] * 4,
        scratch_shapes=[pltpu.VMEM((length, length), F32)],
        cost_estimate=cost(
            4 * tokens * length * heads * dim, tokens * heads * dim * 20, tokens * length * heads
        ),
        name="attend",
    )(qkv, qkv, qkv, q_scale, k_scale, q_gain, k_gain, cosine, sine, doc_col, doc_row)


def attend_back(queries, keys, values, grads, cosine, sine, doc_col, doc_row, heads, dim):
    tokens = queries.shape[0]
    length = doc_row.shape[-1]
    block = pl.BlockSpec((length, dim), lambda j, h: (j, h))
    per_row = pl.BlockSpec((length, 1), lambda j, h: (j, 0))
    table = pl.BlockSpec((length, dim), lambda j, h: (j, 0))
    row = pl.BlockSpec((1, 1, length), lambda j, h: (j, 0, 0))
    wide = jax.ShapeDtypeStruct((tokens, heads * dim), F32)
    return pl.pallas_call(
        functools.partial(attend_back_kernel, dim ** (-0.5)),
        grid=(tokens // length, heads),
        in_specs=[block] * 4 + [table, table, per_row, row],
        out_specs=[block] * 3,
        out_shape=[wide, wide, jax.ShapeDtypeStruct((tokens, heads * dim), BF16)],
        scratch_shapes=[
            pltpu.VMEM((length, length), F32),
            pltpu.VMEM((length, dim), F32),
            pltpu.VMEM((length, dim), F32),
        ],
        cost_estimate=cost(
            10 * tokens * length * heads * dim, tokens * heads * dim * 18, tokens * length * heads
        ),
        name="attend_back",
    )(queries, keys, values, grads, cosine, sine, doc_col, doc_row)


def tie(*arrays):
    return lax.optimization_barrier(arrays)


def ring_of(n):
    return list(range(0, n, 2)) + list(range(n - 1, 0, -2))


def ring_step(x, n, back=False):
    ring = ring_of(n)
    pairs = [(ring[i], ring[(i + 1) % n]) for i in range(n)]
    return lax.ppermute(x, "shard", [(b, a) for a, b in pairs] if back else pairs)


def ring_ids(n):
    ring = ring_of(n)
    return np.array([[ring[(ring.index(s) + i) % n] for i in range(n)] for s in range(n)], np.int32)


def of_shard(table, shard):
    return lax.dynamic_index_in_dim(jnp.asarray(table), shard, 0, keepdims=False)


def ring_gather(block, n, due):
    half = block.shape[0] // 2
    pieces = [(block, 0, 0)]
    ahead = behind = block
    for k in range(1, n // 2):
        behind, ahead = tie(ring_step(behind, n), ring_step(ahead, n, True))
        if k == n // 2 - 1:
            behind, ahead, *due = tie(behind, ahead, *due)
        pieces += [(behind, n - k, 0), (ahead, k, 0)]
    pieces.append((ring_step(behind[:half], n), n // 2, 0))
    pieces.append((ring_step(ahead[half:], n, True), n // 2, half))
    return pieces, due


def place_kernel(n, cut, starts, *refs):
    ins, outs, bufs = refs[:n], refs[n : n + 2], refs[n + 2 : 2 * n + 2]
    sem_in, sem_out = refs[-2], refs[-1]
    loads = [pltpu.make_async_copy(ins[i], bufs[i], sem_in.at[i]) for i in range(n)]
    for load in loads:
        load.start()
    stores = []
    for i in range(n):
        loads[i].wait()
        at = pl.multiple_of(starts[i], 16)
        rows, cols = bufs[i].shape
        for o, first, size in ((0, 0, cut), (1, cut, cols - cut)):
            stores.append(
                pltpu.make_async_copy(
                    bufs[i].at[:, pl.ds(first, size)],
                    outs[o].at[pl.ds(at, rows)],
                    sem_out.at[2 * i + o],
                )
            )
            stores[-1].start()
    for store in stores:
        store.wait()


def place_rows(pieces, starts, rows, cut):
    cols = pieces[0].shape[1]
    n = len(pieces)
    anywhere = pl.BlockSpec(memory_space=pl.ANY)
    return pl.pallas_call(
        functools.partial(place_kernel, n, cut),
        grid_spec=pltpu.PrefetchScalarGridSpec(
            num_scalar_prefetch=1,
            grid=(),
            in_specs=[anywhere] * n,
            out_specs=[anywhere] * 2,
            scratch_shapes=[pltpu.VMEM(x.shape, x.dtype) for x in pieces]
            + [pltpu.SemaphoreType.DMA((n,)), pltpu.SemaphoreType.DMA((2 * n,))],
        ),
        out_shape=[
            jax.ShapeDtypeStruct((rows, size), pieces[0].dtype) for size in (cut, cols - cut)
        ],
        cost_estimate=cost(0, 4 * rows * cols),
        name="place_rows",
    )(starts, *pieces)


def normed_kernel(ids, hidden, scale, gain, out):
    out[...] = (hidden[...].astype(F32) * scale[...] * gain[...]).astype(BF16)


def normed_in_order(ids, hidden, scale, gain):
    n = ids.shape[0]
    rows, cols = hidden.shape
    if cols // n % 128:
        normed = (hidden.astype(F32) * scale * gain).astype(BF16)
        return normed.reshape(rows, n, cols // n)[:, ids].reshape(rows, cols)
    return pl.pallas_call(
        normed_kernel,
        grid_spec=pltpu.PrefetchScalarGridSpec(
            num_scalar_prefetch=1,
            grid=(n,),
            in_specs=[
                pl.BlockSpec((rows, cols // n), lambda i, ids: (0, ids[i])),
                pl.BlockSpec((rows, 1), lambda i, ids: (0, 0)),
                pl.BlockSpec((1, cols // n), lambda i, ids: (0, ids[i])),
            ],
            out_specs=pl.BlockSpec((rows, cols // n), lambda i, ids: (0, i)),
        ),
        out_shape=jax.ShapeDtypeStruct((rows, cols), BF16),
        cost_estimate=cost(0, COVER),
        name="normed_in_order",
    )(ids, hidden, scale, gain)


def back_kernel(x, w, out):
    out[0] = dot(x[...], w[...], ((1,), (1,))).astype(out.dtype)


def back_product(x, w, first, count, rows, dtype):
    inner = x.shape[1]
    cols = w.shape[0]
    step = 512
    return pl.pallas_call(
        back_kernel,
        grid=(count, cols // step),
        in_specs=[
            pl.BlockSpec((rows, inner), lambda j, i: (first + 2 * j, 0)),
            pl.BlockSpec((step, inner), lambda j, i: (i, 0)),
        ],
        out_specs=pl.BlockSpec((1, rows, step), lambda j, i: (j, 0, i)),
        out_shape=jax.ShapeDtypeStruct((count, rows, cols), dtype),
        cost_estimate=cost(0, COVER),
        name="back_product",
    )(x, w)


def small_kernel(n, first, ids, x, columns, out):
    rows = x.shape[0] // n
    for i in range(n):
        here = pl.ds(pl.multiple_of(ids[i] * rows, 16), rows)
        block = x[here, :]
        lanes = lax.broadcasted_iota(jnp.int32, block.shape, 1)
        for c in range(columns.shape[1]):
            block = jnp.where(lanes == first + c, columns[here, c : c + 1], block)
        out[i * rows : (i + 1) * rows] = block.astype(BF16)


def small_in_order(ids, x, columns, first):
    n = ids.shape[0]
    whole = lambda shape: pl.BlockSpec(shape, lambda i, ids: (0, 0))
    return pl.pallas_call(
        functools.partial(small_kernel, n, first),
        grid_spec=pltpu.PrefetchScalarGridSpec(
            num_scalar_prefetch=1,
            grid=(1,),
            in_specs=[whole(x.shape), whole(columns.shape)],
            out_specs=whole(x.shape),
        ),
        out_shape=jax.ShapeDtypeStruct(x.shape, BF16),
        cost_estimate=cost(0, 8 * x.size),
        name="small_in_order",
    )(ids, x, columns)


def ring_scatter(parts, n, due):
    rows = parts[0].shape[0] // n
    half = rows // 2
    chunk = lambda k, first=0, size=rows: jnp.concatenate(
        [x[k % n * rows + first : k % n * rows + first + size] for x in parts], 1
    )
    done = []
    ahead = ring_step(chunk(n // 2, 0, half), n)
    behind = ring_step(chunk(n // 2, half, half), n, True)
    for k in range(n // 2 - 1, -1, -1):
        at = n // 2 - 1 - k
        ahead, behind, *got = tie(ahead, behind, *(due[at](*done) if at < len(due) else ()))
        done = got or done
        if k == 0:
            break
        a, b = chunk(k), chunk(n - k)
        if at == 0:
            a = jnp.concatenate([a[:half].astype(F32) + ahead, a[half:]], 0)
            b = jnp.concatenate([b[:half], b[half:].astype(F32) + behind], 0)
        else:
            a, b = a.astype(F32) + ahead, b.astype(F32) + behind
        ahead, behind = ring_step(a.astype(BF16), n), ring_step(b.astype(BF16), n, True)
    return chunk(0).astype(F32) + ahead + behind, done


def shard_gather(x):
    return lax.all_gather(x, "shard", axis=0, tiled=True)


def shard_scatter(x):
    return lax.psum_scatter(x, "shard", scatter_dimension=0, tiled=True).astype(F32)


def split_sum(x):
    high = x.astype(BF16)
    return high, (x - high.astype(F32)).astype(BF16)


def local(
    n_shard,
    hidden_in,
    doc_ids,
    expert_ids,
    slot_rows,
    out_grad,
    attn_gain,
    w_query,
    w_key,
    w_value,
    query_gain,
    key_gain,
    w_output,
    ffn_gain,
    w_router,
    w_gate,
    w_up,
    w_down,
):
    length, width = hidden_in.shape
    dim = width // HEADS
    heads = HEADS // 4
    part = width // 4
    routed = w_router.shape[1]
    experts = w_gate.shape[0]
    hidden_units = w_gate.shape[2]
    half_units = hidden_units // 2
    cap = slot_rows.shape[2]
    rep = lax.axis_index("rep")
    shard = lax.axis_index("shard")
    core, side = rep % 2, rep // 2
    my_rows = width // n_shard
    quarter = my_rows // 4

    cut = lambda w: lax.dynamic_slice_in_dim(w, rep * part, part, 1)
    qkv_block = jnp.concatenate([cut(w_query), cut(w_key), cut(w_value)], 1)
    output_block = lax.dynamic_slice_in_dim(w_output, rep * quarter, quarter, 0)
    pick = lambda w: lax.dynamic_index_in_dim(w, core, 0, keepdims=False)
    down_rows = hidden_units // n_shard
    unit = jnp.arange(half_units)
    unit = (unit // (down_rows // 2)) * down_rows + unit % (down_rows // 2)
    choose = lambda which: (
        jnp.arange(hidden_units)[:, None] == (unit + which * (down_rows // 2))[None, :]
    ).astype(BF16)
    mine = choose(side)
    gate_up_block = jnp.concatenate(
        [dot(pick(w_gate), mine).astype(BF16), dot(pick(w_up), mine).astype(BF16)], 1
    )
    down_block = lax.dynamic_slice_in_dim(pick(w_down), side * (down_rows // 2), down_rows // 2, 0)
    small_block = jnp.concatenate(
        [w_router, jnp.stack([attn_gain, query_gain, key_gain, ffn_gain], 1)]
        + [jnp.zeros((my_rows, 128 - 4 - routed), BF16)],
        1,
    )

    docs_all = jnp.concatenate(rep_gather(doc_ids), 0)
    before = docs_all[:, None, :] < docs_all[:, :, None]
    starts = jnp.sum(before.astype(jnp.int32), -1)
    places = (jnp.arange(length, dtype=jnp.int32)[None, :] - starts).astype(F32).reshape(-1)
    rates = THETA ** (-jnp.arange(dim // 2, dtype=F32) * 2.0 / dim)
    angles = places[:, None] * jnp.concatenate([rates, rates])[None, :]
    cosine, sine = jnp.cos(angles), jnp.sin(angles)
    doc_col = docs_all.reshape(-1, 1)
    doc_row = docs_all.reshape(4, 1, length)
    slots = slot_rows[0].reshape(experts * cap)
    select = (slots[:, None] == jnp.arange(length, dtype=jnp.int32)[None, :]).astype(BF16)

    def to_pair(x):
        own = lax.dynamic_index_in_dim(x, core, 0, keepdims=False)
        other = lax.dynamic_index_in_dim(x, 1 - core, 0, keepdims=False)
        return jnp.stack([own, swap(other, 1)])

    def to_experts(x):
        pair = to_pair(x)
        return jnp.concatenate([pair, swap(pair, 2)], 0)

    upstream_pair = to_pair(dot(select, out_grad).astype(BF16).reshape(experts, cap, width))

    pieces, arrays = ring_gather(
        jnp.concatenate([qkv_block, small_block], 1),
        n_shard,
        (swap(hidden_in, 2), cosine, sine, upstream_pair, output_block, gate_up_block, down_block),
    )
    hidden_side, cosine, sine, upstream_pair, output_block, gate_up_block, down_block = arrays
    hidden_all = jnp.concatenate(
        [hidden_in, swap(hidden_in, 1), hidden_side, swap(hidden_side, 1)], 0
    )
    normed_scale = rms_scale(hidden_all.astype(F32))
    piece, k, first = pieces[-1]
    piece, normed_scale = tie(piece, normed_scale)
    pieces[-1] = (piece, k, first)
    ids = ring_ids(n_shard)
    starts = np.stack([ids[:, k] * my_rows + first for _, k, first in pieces], 1)
    starts, ring = of_shard(starts, shard), of_shard(ids, shard)
    w_qkv, small_w = place_rows([piece for piece, _, _ in pieces], starts, width, 3 * part)
    router_w = small_w[:, :routed]
    gains = small_w[:, routed : routed + 4].T.astype(F32)
    w_out_part = shard_gather(output_block).reshape(n_shard, quarter, width)
    w_gu = shard_gather(gate_up_block)
    w_dn = shard_gather(down_block)
    gain_one, gain_two = gains[0], gains[3]
    gain_query = lax.dynamic_slice_in_dim(gains[1:2], rep * part, part, 1)
    gain_key = lax.dynamic_slice_in_dim(gains[2:3], rep * part, part, 1)

    upstream = out_grad.astype(F32)

    def send_side(x, send):
        return swap(x[2:].astype(send), 2)

    def from_experts(x, there, send):
        pair = x[:2] + there.astype(F32)
        other = swap(pair[1].astype(send), 1).astype(F32)
        first = jnp.where(core == 0, pair[0], other)
        return jnp.stack([first, jnp.where(core == 0, other, pair[0])])

    def add_slots(x):
        high, low = split_sum(x.reshape(experts * cap, width))
        return dot(select, high, ((0,), (0,))) + dot(select, low, ((0,), (0,)))

    normed = (hidden_all.astype(F32) * normed_scale * gain_one).astype(BF16)
    w_qkv, upstream_pair = tie(w_qkv, upstream_pair)
    qkv, upstream_side = tie(dot(normed, w_qkv), swap(upstream_pair, 2))
    slot_upstream = jnp.concatenate([upstream_pair, upstream_side], 0)
    query_raw, key_raw = qkv[:, :part], qkv[:, part : 2 * part]
    squares = jnp.stack([jnp.sum(query_raw * query_raw, -1), jnp.sum(key_raw * key_raw, -1)], -1)
    squares = rep_sum(squares.reshape(4, length, 2)).reshape(-1, 2)
    scales = lax.rsqrt(squares / width + EPSILON)
    query_scale, key_scale = scales[:, :1], scales[:, 1:]
    scales, w_out_part = tie(scales, w_out_part)
    out_core, out_side = swap(w_out_part, 1), swap(w_out_part, 2)
    mixed_heads, queries, keys, values = attend(
        qkv,
        query_scale,
        key_scale,
        gain_query,
        gain_key,
        cosine,
        sine,
        doc_col,
        doc_row,
        heads,
        dim,
    )
    mixed_heads, out_core, out_side = tie(mixed_heads, out_core, out_side)
    blocks = mixed_heads.reshape(4, length, part)
    from_side = swap(blocks[2:], 2)
    out_pieces = in_order([w_out_part, out_core, out_side, swap(out_side, 1)], rep)
    output_w = jnp.stack(out_pieces, 1).reshape(width, width)
    from_core, late_scale = tie(swap(blocks[1], 1), normed_scale)
    normed_ring = normed_in_order(ring, hidden_all, late_scale, gain_one[None])
    from_side, w_gu, output_w, normed_ring = tie(from_side, w_gu, output_w, normed_ring)
    mixed = jnp.concatenate(
        in_order([blocks[0], from_core, from_side[0], swap(from_side[1], 1)], rep), 1
    )
    hidden = hidden_in.astype(F32)
    residual = hidden + dot(mixed, output_w)
    scale_two = rms_scale(residual)
    inner = (residual * scale_two * gain_two).astype(BF16)
    logits = dot(inner, router_w)
    probs_all = jax.nn.softmax(logits, axis=-1)
    named = jnp.sum(
        (expert_ids[:, :, None] == jnp.arange(experts, dtype=jnp.int32)).astype(F32), 1
    )
    window = probs_all[:, :experts] * named
    select_wide = select.reshape(experts, cap, length).astype(F32)
    slot_gates = to_experts(jnp.sum(select_wide * window.T[:, None, :], -1))
    pair = to_pair(dot(select, inner).astype(BF16).reshape(experts, cap, width))
    from_side = swap(pair, 2)
    slot_inputs = jnp.concatenate([pair, from_side], 0)
    slot_inputs = slot_inputs.reshape(4 * cap, width)

    gate_up = dot(slot_inputs, w_gu)
    gate_part, up_part = gate_up[:, :half_units], gate_up[:, half_units:]
    sigma = jax.nn.sigmoid(gate_part)
    swished = gate_part * sigma
    activated = (swished * up_part).astype(BF16)
    returned = dot(activated, w_dn).reshape(4, cap, width)
    slot_gate_grad = jnp.sum(returned * slot_upstream.astype(F32), -1)
    slot_gate_grad = from_experts(slot_gate_grad, send_side(slot_gate_grad, F32), F32)
    returned_grad = (slot_gates[:, :, None] * slot_upstream.astype(F32)).astype(BF16)
    returned_grad = returned_grad.reshape(4 * cap, width)
    act_grad = dot(returned_grad, w_dn, ((1,), (1,)))
    gate_grad = act_grad * up_part * sigma * (1.0 + gate_part * (1.0 - sigma))
    gate_up_grad = jnp.concatenate([gate_grad.astype(BF16), (act_grad * swished).astype(BF16)], 1)
    slot_input_grad = dot(gate_up_grad, w_gu, ((1,), (1,))).reshape(4, cap, width)
    down_w_grad = dot(activated, returned_grad, ((0,), (0,))).astype(BF16)
    gate_up_w_grad = dot(slot_inputs, gate_up_grad, ((0,), (0,))).astype(BF16)
    at = lambda x, i, axis: lax.dynamic_index_in_dim(x, i, axis, keepdims=False)
    half = lambda which: at(mixed.reshape(length, n_shard, 2, 2, quarter), which, 3).reshape(
        length, width // 2
    )
    there, down_w_grad, gate_up_w_grad, mixed_own, mixed_other = tie(
        send_side(slot_input_grad, BF16),
        down_w_grad,
        gate_up_w_grad,
        half(core),
        half(1 - core),
    )
    slot_input_grad = from_experts(slot_input_grad, there, BF16)
    gate_up_owned = shard_scatter(gate_up_w_grad)
    down_owned = shard_scatter(down_w_grad)

    window_grad = jnp.sum(select_wide * slot_gate_grad[:, :, None], 1).T
    chosen_grad = jnp.concatenate(
        [window_grad * named, jnp.zeros((length, routed - experts), F32)], 1
    )
    logits_grad = (
        probs_all * (chosen_grad - jnp.sum(probs_all * chosen_grad, -1, keepdims=True))
    ).astype(BF16)
    router_grad = dot(inner, jnp.pad(logits_grad, ((0, 0), (0, 128 - routed))), ((0,), (0,)))
    inner_grad = add_slots(slot_input_grad) + dot(logits_grad, router_w, ((1,), (1,)))
    residual_part, gain_two_grad = norm_back(residual, scale_two, gain_two, inner_grad)
    residual_grad = upstream + residual_part
    branch_grad = residual_grad.astype(BF16)
    mixed_grad = dot(branch_grad, output_w, ((1,), (1,))).astype(BF16)
    piece = lambda j: lax.dynamic_slice_in_dim(mixed_grad, (rep ^ j) * part, part, 1)
    from_side = swap(jnp.stack([piece(2), piece(3)]), 2)
    from_core, branch_grad = tie(swap(piece(1), 1), branch_grad)
    half_grad = lambda half: dot(half, branch_grad, ((0,), (0,))).astype(BF16)
    out_there = swap(half_grad(mixed_other), 1)
    out_w_grad = (half_grad(mixed_own).astype(F32) + out_there).astype(BF16)
    from_side, out_w_grad, returned = tie(from_side, out_w_grad, returned)
    grads = jnp.concatenate([piece(0), from_core, from_side[0], swap(from_side[1], 1)], 0)
    out_w_grad = out_w_grad.reshape(n_shard, 2, quarter, width)
    out_there = swap(at(out_w_grad, 1 - side, 1), 2)

    query_grad, key_grad, value_grad = attend_back(
        queries, keys, values, grads, cosine, sine, doc_col, doc_row, heads, dim
    )
    value_grad, out_there = tie(value_grad, out_there)
    out_w_grad = (at(out_w_grad, side, 1).astype(F32) + out_there).astype(BF16)
    out_owned = shard_scatter(out_w_grad.reshape(n_shard * quarter, width))
    weighted_q, weighted_k = query_grad * gain_query, key_grad * gain_key
    means = jnp.stack(
        [jnp.sum(weighted_q * query_raw, -1), jnp.sum(weighted_k * key_raw, -1)], -1
    )
    means = rep_sum(means.reshape(4, length, 2)).reshape(-1, 2) / width
    means, returned = tie(means, returned)
    returned_there = send_side(returned, BF16)
    gain_query_grad = jnp.sum(query_grad * query_raw * query_scale, 0)
    gain_key_grad = jnp.sum(key_grad * key_raw * key_scale, 0)
    query_raw_grad = query_scale * weighted_q - query_raw * query_scale**3 * means[:, :1]
    key_raw_grad = key_scale * weighted_k - key_raw * key_scale**3 * means[:, 1:]
    qkv_grad = jnp.concatenate(
        [query_raw_grad.astype(BF16), key_raw_grad.astype(BF16), value_grad], 1
    )
    qkv_w_grad = dot(normed_ring, qkv_grad, ((0,), (0,))).astype(BF16)
    qkv_grad, qkv_w_grad, returned_there, gate_up_owned = tie(
        qkv_grad, qkv_w_grad, returned_there, gate_up_owned
    )
    own_gates = jnp.sum(select_wide * window.T[:, None, :], -1)
    returned = from_experts(returned, returned_there, BF16)
    output = (residual + add_slots(own_gates[:, :, None] * returned)).astype(BF16)
    place = lambda g: lax.dynamic_update_slice_in_dim(
        jnp.zeros((width,), F32), g, rep * part, 0
    )
    small = jnp.stack([gain_two_grad, place(gain_query_grad), place(gain_key_grad)], 1)
    small = small_in_order(ring, router_grad, small, routed)
    back = lambda slots, first, count, dtype: back_product(
        slots, w_qkv, first, count, length, dtype
    )

    def near(slots, odd):
        odd, slots = tie(swap(odd, 1), slots)
        return slots, back(slots, 2, 1, F32)[0], odd

    due = (
        lambda: (qkv_grad, back(qkv_grad, 1, 2, BF16)),
        near,
        lambda slots, two, from_core: (
            back(slots, 0, 1, F32)[0] + from_core[0].astype(F32),
            (two + from_core[1].astype(F32)).astype(BF16)[length // 2 :],
            swap((two + from_core[1].astype(F32)).astype(BF16)[: length // 2], 2),
            down_owned,
        ),
        lambda zero, rest, top, down: (zero, top, swap(rest, 2), down),
    )
    qkv_owned, (normed_grad, top, rest, down_owned) = ring_scatter(
        [qkv_w_grad, small], n_shard, due
    )
    normed_grad = normed_grad + jnp.concatenate([top, rest], 0).astype(F32)
    weighted = normed_grad * gain_one
    scale_one = normed_scale[:length]
    inner_mean = jnp.mean(weighted * hidden, -1, keepdims=True)
    hidden_part = scale_one * weighted - hidden * scale_one * scale_one * scale_one * inner_mean
    input_grad = residual_grad + hidden_part

    gain_part = jnp.sum(qkv_block.astype(F32) * qkv_owned[:, : 3 * part], 1, keepdims=True)
    column = jnp.arange(128)[None, :] == routed + 3
    qkv_owned = jnp.concatenate(
        [qkv_owned[:, : 3 * part], jnp.where(column, gain_part, qkv_owned[:, 3 * part :])], 1
    ).astype(BF16)
    qkv_core, qkv_side, out_owned = tie(swap(qkv_owned, 1), swap(qkv_owned, 2), out_owned)
    qkv_pieces = in_order([qkv_owned, qkv_core, qkv_side, swap(qkv_side, 1)], rep)
    spread = lambda i: jnp.concatenate(
        [p[:, i * part : (i + 1) * part] for p in qkv_pieces], 1
    ).astype(F32)
    grads_qkv = [spread(i) for i in range(3)]
    small = sum(p[:, 3 * part :].astype(F32) for p in qkv_pieces)
    gain_one_grad = small[:, routed + 3] / attn_gain.astype(F32)
    out_full = jnp.concatenate(in_order(rep_gather(out_owned.astype(BF16)), rep), 0).astype(F32)
    gu_pieces = in_order(rep_gather(gate_up_owned.astype(BF16)), rep)
    dn_pieces = in_order(rep_gather(down_owned.astype(BF16)), rep)
    one, two = choose(0), choose(1)
    join = lambda i: jnp.stack(
        [
            dot(gu_pieces[e][:, i * half_units : (i + 1) * half_units], one, ((1,), (1,)))
            + dot(gu_pieces[2 + e][:, i * half_units : (i + 1) * half_units], two, ((1,), (1,)))
            for e in range(experts)
        ]
    )
    down_full = jnp.stack(
        [jnp.concatenate([dn_pieces[e], dn_pieces[2 + e]], 0) for e in range(experts)]
    ).astype(F32)
    return (
        output,
        input_grad,
        gain_one_grad,
        *grads_qkv,
        small[:, routed + 1],
        small[:, routed + 2],
        out_full,
        small[:, routed],
        small[:, :routed],
        join(0),
        join(1),
        down_full,
    )


def solution(mesh):
    tokens = P(("shard", "rep"), None)
    rows = P("shard", None)
    middle = P(None, "shard", None)
    return jax.shard_map(
        functools.partial(local, mesh.shape["shard"]),
        mesh=mesh,
        in_specs=(
            tokens,
            tokens,
            tokens,
            P(("shard", "rep"), None, None),
            tokens,
            P("shard"),
            rows,
            rows,
            rows,
            P("shard"),
            P("shard"),
            rows,
            P("shard"),
            rows,
            middle,
            middle,
            middle,
        ),
        out_specs=(
            tokens,
            tokens,
            P("shard"),
            rows,
            rows,
            rows,
            P("shard"),
            P("shard"),
            rows,
            P("shard"),
            rows,
            middle,
            middle,
            middle,
        ),
        check_vma=False,
    )
```

```python
import functools

import jax
import jax.numpy as jnp
import numpy as np
from jax import lax
from jax.experimental import pallas as pl
from jax.experimental.pallas import tpu as pltpu
from jax.sharding import PartitionSpec as P

HEADS = 16
EPSILON = 1e-05
THETA = 10000.0
REACH = 2
ROWS = 128
COVER = 1 << 27
F32 = jnp.float32
BF16 = jnp.bfloat16


def rms_scale(values):
    return lax.rsqrt(jnp.mean(values * values, -1, keepdims=True) + EPSILON)


def norm_back(values, scale, gain, upstream):
    gain_grad = jnp.sum(upstream * values * scale, 0)
    weighted = upstream * gain
    inner_mean = jnp.mean(weighted * values, -1, keepdims=True)
    return (scale * weighted - values * scale * scale * scale * inner_mean, gain_grad)


def dot(a, b, dims=((1,), (0,))):
    return lax.dot_general(a, b, (dims, ((), ())), preferred_element_type=F32)


def swap(x, mask):
    return lax.ppermute(x, "rep", [(i, i ^ mask) for i in range(4)])


def flip(x, mask):
    return jnp.stack([x[j ^ mask] for j in range(4)])


def rep_sum(x):
    x = x + flip(swap(x, 1), 1)
    return x + flip(swap(x, 2), 2)


def rep_gather(x):
    one, two = swap(x, 1), swap(x, 2)
    return [x, one, two, swap(two, 1)]


def in_order(pieces, rep):
    low = rep % 2 == 1
    high = rep // 2 == 1
    a, b, c, d = pieces
    a, b = jnp.where(low, b, a), jnp.where(low, a, b)
    c, d = jnp.where(low, d, c), jnp.where(low, c, d)
    return (
        jnp.where(high, c, a),
        jnp.where(high, d, b),
        jnp.where(high, a, c),
        jnp.where(high, b, d),
    )


def mask_bias(bias, doc_col, doc_row):
    length = doc_col.shape[0]
    rows = lax.broadcasted_iota(jnp.int32, (length, length), 0)
    cols = lax.broadcasted_iota(jnp.int32, (length, length), 1)
    allowed = (doc_col[...] == doc_row[0]) & (cols <= rows)
    bias[...] = jnp.where(allowed, 0.0, -jnp.inf).astype(F32)


def turn(values, cosine, sine):
    half = values.shape[-1] // 2
    lanes = lax.broadcasted_iota(jnp.int32, values.shape, 1)
    turned = jnp.where(lanes < half, -1.0, 1.0) * pltpu.roll(values, half, 1)
    return values * cosine + turned * sine


def turn_back(values, cosine, sine):
    half = values.shape[-1] // 2
    lanes = lax.broadcasted_iota(jnp.int32, values.shape, 1)
    moved = pltpu.roll(values * sine, half, 1)
    return values * cosine + jnp.where(lanes < half, 1.0, -1.0) * moved


def spans(length):
    return [
        (i * ROWS, (i + 1) * ROWS, max(0, (i - REACH) * ROWS)) for i in range(length // ROWS)
    ]


def attend_kernel(
    factor,
    q_ref,
    k_ref,
    v_ref,
    q_scale,
    k_scale,
    q_gain,
    k_gain,
    cosine,
    sine,
    doc_col,
    doc_row,
    mixed_ref,
    queries_ref,
    keys_ref,
    values_ref,
    bias,
):
    @pl.when(pl.program_id(1) == 0)
    def _():
        mask_bias(bias, doc_col, doc_row)

    cos, sin = cosine[...], sine[...]
    queries_ref[...] = turn(q_ref[...] * q_scale[...] * q_gain[...], cos, sin).astype(BF16)
    keys_ref[...] = turn(k_ref[...] * k_scale[...] * k_gain[...], cos, sin).astype(BF16)
    values_ref[...] = v_ref[...].astype(BF16)
    for start, end, low in spans(q_ref.shape[0]):
        scores = dot(queries_ref[start:end], keys_ref[low:end], ((1,), (1,))) * factor
        scores = scores + bias[start:end, low:end]
        weights = jnp.exp(scores - jnp.max(scores, -1, keepdims=True))
        inverse = 1.0 / jnp.sum(weights, -1, keepdims=True)
        mixed = dot(weights.astype(BF16), values_ref[low:end]) * inverse
        mixed_ref[start:end] = mixed.astype(BF16)


def attend_back_kernel(
    factor,
    queries,
    keys,
    values,
    grads,
    cosine,
    sine,
    doc_col,
    doc_row,
    dq_ref,
    dk_ref,
    dv_ref,
    bias,
    dk_sum,
    dv_sum,
):
    @pl.when(pl.program_id(1) == 0)
    def _():
        mask_bias(bias, doc_col, doc_row)

    cos, sin = cosine[...], sine[...]
    dk_sum[...] = jnp.zeros_like(dk_sum)
    dv_sum[...] = jnp.zeros_like(dv_sum)
    for start, end, low in spans(queries.shape[0]):
        q, g = queries[start:end], grads[start:end]
        k, v = keys[low:end], values[low:end]
        scores = dot(q, k, ((1,), (1,))) * factor + bias[start:end, low:end]
        weights = jnp.exp(scores - jnp.max(scores, -1, keepdims=True))
        probs = weights * (1.0 / jnp.sum(weights, -1, keepdims=True))
        dv_sum[low:end] += dot(probs.astype(BF16), g, ((0,), (0,)))
        prob_grad = dot(g, v, ((1,), (1,)))
        score_grad = probs * (prob_grad - jnp.sum(probs * prob_grad, -1, keepdims=True))
        score_grad = score_grad.astype(BF16)
        dq_ref[start:end] = turn_back(dot(score_grad, k) * factor, cos[start:end], sin[start:end])
        dk_sum[low:end] += dot(score_grad, q, ((0,), (0,)))
    dk_ref[...] = turn_back(dk_sum[...] * factor, cos, sin)
    dv_ref[...] = dv_sum[...].astype(BF16)


def cost(flops, moved, exps=0):
    return pl.CostEstimate(flops=flops, bytes_accessed=moved, transcendentals=exps)


def attend(qkv, q_scale, k_scale, q_gain, k_gain, cosine, sine, doc_col, doc_row, heads, dim):
    tokens = qkv.shape[0]
    length = doc_row.shape[-1]
    block = lambda off: pl.BlockSpec((length, dim), lambda j, h: (j, off + h))
    per_row = pl.BlockSpec((length, 1), lambda j, h: (j, 0))
    table = pl.BlockSpec((length, dim), lambda j, h: (j, 0))
    gain = pl.BlockSpec((1, dim), lambda j, h: (0, h))
    row = pl.BlockSpec((1, 1, length), lambda j, h: (j, 0, 0))
    out = jax.ShapeDtypeStruct((tokens, heads * dim), BF16)
    return pl.pallas_call(
        functools.partial(attend_kernel, dim ** (-0.5)),
        grid=(tokens // length, heads),
        in_specs=[block(0), block(heads), block(2 * heads), per_row, per_row, gain, gain]
        + [table, table, per_row, row],
        out_specs=[block(0)] * 4,
        out_shape=[out] * 4,
        scratch_shapes=[pltpu.VMEM((length, length), F32)],
        cost_estimate=cost(
            4 * tokens * length * heads * dim, tokens * heads * dim * 20, tokens * length * heads
        ),
        name="attend",
    )(qkv, qkv, qkv, q_scale, k_scale, q_gain, k_gain, cosine, sine, doc_col, doc_row)


def attend_back(queries, keys, values, grads, cosine, sine, doc_col, doc_row, heads, dim):
    tokens = queries.shape[0]
    length = doc_row.shape[-1]
    block = pl.BlockSpec((length, dim), lambda j, h: (j, h))
    per_row = pl.BlockSpec((length, 1), lambda j, h: (j, 0))
    table = pl.BlockSpec((length, dim), lambda j, h: (j, 0))
    row = pl.BlockSpec((1, 1, length), lambda j, h: (j, 0, 0))
    wide = jax.ShapeDtypeStruct((tokens, heads * dim), F32)
    return pl.pallas_call(
        functools.partial(attend_back_kernel, dim ** (-0.5)),
        grid=(tokens // length, heads),
        in_specs=[block] * 4 + [table, table, per_row, row],
        out_specs=[block] * 3,
        out_shape=[wide, wide, jax.ShapeDtypeStruct((tokens, heads * dim), BF16)],
        scratch_shapes=[
            pltpu.VMEM((length, length), F32),
            pltpu.VMEM((length, dim), F32),
            pltpu.VMEM((length, dim), F32),
        ],
        cost_estimate=cost(
            10 * tokens * length * heads * dim, tokens * heads * dim * 18, tokens * length * heads
        ),
        name="attend_back",
    )(queries, keys, values, grads, cosine, sine, doc_col, doc_row)


def tie(*arrays):
    return lax.optimization_barrier(arrays)


def ring_of(n):
    return list(range(0, n, 2)) + list(range(n - 1, 0, -2))


def ring_step(x, n, back=False):
    ring = ring_of(n)
    pairs = [(ring[i], ring[(i + 1) % n]) for i in range(n)]
    return lax.ppermute(x, "shard", [(b, a) for a, b in pairs] if back else pairs)


def ring_ids(n):
    ring = ring_of(n)
    return np.array([[ring[(ring.index(s) + i) % n] for i in range(n)] for s in range(n)], np.int32)


def of_shard(table, shard):
    return lax.dynamic_index_in_dim(jnp.asarray(table), shard, 0, keepdims=False)


def ring_gather(block, n, due):
    half = block.shape[0] // 2
    pieces = [(block, 0, 0)]
    ahead = behind = block
    for k in range(1, n // 2):
        behind, ahead = tie(ring_step(behind, n), ring_step(ahead, n, True))
        if k == n // 2 - 1:
            behind, ahead, *due = tie(behind, ahead, *due)
        pieces += [(behind, n - k, 0), (ahead, k, 0)]
    pieces.append((ring_step(behind[:half], n), n // 2, 0))
    pieces.append((ring_step(ahead[half:], n, True), n // 2, half))
    return pieces, due


def place_kernel(n, cut, starts, *refs):
    ins, outs, bufs = refs[:n], refs[n : n + 2], refs[n + 2 : 2 * n + 2]
    sem_in, sem_out = refs[-2], refs[-1]
    loads = [pltpu.make_async_copy(ins[i], bufs[i], sem_in.at[i]) for i in range(n)]
    for load in loads:
        load.start()
    stores = []
    for i in range(n):
        loads[i].wait()
        at = pl.multiple_of(starts[i], 16)
        rows, cols = bufs[i].shape
        for o, first, size in ((0, 0, cut), (1, cut, cols - cut)):
            stores.append(
                pltpu.make_async_copy(
                    bufs[i].at[:, pl.ds(first, size)],
                    outs[o].at[pl.ds(at, rows)],
                    sem_out.at[2 * i + o],
                )
            )
            stores[-1].start()
    for store in stores:
        store.wait()


def place_rows(pieces, starts, rows, cut):
    cols = pieces[0].shape[1]
    n = len(pieces)
    anywhere = pl.BlockSpec(memory_space=pl.ANY)
    return pl.pallas_call(
        functools.partial(place_kernel, n, cut),
        grid_spec=pltpu.PrefetchScalarGridSpec(
            num_scalar_prefetch=1,
            grid=(),
            in_specs=[anywhere] * n,
            out_specs=[anywhere] * 2,
            scratch_shapes=[pltpu.VMEM(x.shape, x.dtype) for x in pieces]
            + [pltpu.SemaphoreType.DMA((n,)), pltpu.SemaphoreType.DMA((2 * n,))],
        ),
        out_shape=[
            jax.ShapeDtypeStruct((rows, size), pieces[0].dtype) for size in (cut, cols - cut)
        ],
        cost_estimate=cost(0, 4 * rows * cols),
        name="place_rows",
    )(starts, *pieces)


def normed_kernel(ids, hidden, scale, gain, out):
    out[...] = (hidden[...].astype(F32) * scale[...] * gain[...]).astype(BF16)


def normed_in_order(ids, hidden, scale, gain):
    n = ids.shape[0]
    rows, cols = hidden.shape
    if cols // n % 128:
        normed = (hidden.astype(F32) * scale * gain).astype(BF16)
        return normed.reshape(rows, n, cols // n)[:, ids].reshape(rows, cols)
    return pl.pallas_call(
        normed_kernel,
        grid_spec=pltpu.PrefetchScalarGridSpec(
            num_scalar_prefetch=1,
            grid=(n,),
            in_specs=[
                pl.BlockSpec((rows, cols // n), lambda i, ids: (0, ids[i])),
                pl.BlockSpec((rows, 1), lambda i, ids: (0, 0)),
                pl.BlockSpec((1, cols // n), lambda i, ids: (0, ids[i])),
            ],
            out_specs=pl.BlockSpec((rows, cols // n), lambda i, ids: (0, i)),
        ),
        out_shape=jax.ShapeDtypeStruct((rows, cols), BF16),
        cost_estimate=cost(0, COVER),
        name="normed_in_order",
    )(ids, hidden, scale, gain)


def back_kernel(x, w, out):
    out[0] = dot(x[...], w[...], ((1,), (1,))).astype(out.dtype)


def back_product(x, w, first, count, rows, dtype):
    inner = x.shape[1]
    cols = w.shape[0]
    step = 512
    return pl.pallas_call(
        back_kernel,
        grid=(count, cols // step),
        in_specs=[
            pl.BlockSpec((rows, inner), lambda j, i: (first + 2 * j, 0)),
            pl.BlockSpec((step, inner), lambda j, i: (i, 0)),
        ],
        out_specs=pl.BlockSpec((1, rows, step), lambda j, i: (j, 0, i)),
        out_shape=jax.ShapeDtypeStruct((count, rows, cols), dtype),
        cost_estimate=cost(0, COVER),
        name="back_product",
    )(x, w)


def small_kernel(n, first, ids, x, columns, out):
    rows = x.shape[0] // n
    for i in range(n):
        here = pl.ds(pl.multiple_of(ids[i] * rows, 16), rows)
        block = x[here, :]
        lanes = lax.broadcasted_iota(jnp.int32, block.shape, 1)
        for c in range(columns.shape[1]):
            block = jnp.where(lanes == first + c, columns[here, c : c + 1], block)
        out[i * rows : (i + 1) * rows] = block.astype(BF16)


def small_in_order(ids, x, columns, first):
    n = ids.shape[0]
    whole = lambda shape: pl.BlockSpec(shape, lambda i, ids: (0, 0))
    return pl.pallas_call(
        functools.partial(small_kernel, n, first),
        grid_spec=pltpu.PrefetchScalarGridSpec(
            num_scalar_prefetch=1,
            grid=(1,),
            in_specs=[whole(x.shape), whole(columns.shape)],
            out_specs=whole(x.shape),
        ),
        out_shape=jax.ShapeDtypeStruct(x.shape, BF16),
        cost_estimate=cost(0, 8 * x.size),
        name="small_in_order",
    )(ids, x, columns)


def ring_scatter(parts, n, due):
    rows = parts[0].shape[0] // n
    half = rows // 2
    chunk = lambda k, first=0, size=rows: jnp.concatenate(
        [x[k % n * rows + first : k % n * rows + first + size] for x in parts], 1
    )
    done = []
    ahead = ring_step(chunk(n // 2, 0, half), n)
    behind = ring_step(chunk(n // 2, half, half), n, True)
    for k in range(n // 2 - 1, -1, -1):
        at = n // 2 - 1 - k
        ahead, behind, *got = tie(ahead, behind, *(due[at](*done) if at < len(due) else ()))
        done = got or done
        if k == 0:
            break
        a, b = chunk(k), chunk(n - k)
        if at == 0:
            a = jnp.concatenate([a[:half].astype(F32) + ahead, a[half:]], 0)
            b = jnp.concatenate([b[:half], b[half:].astype(F32) + behind], 0)
        else:
            a, b = a.astype(F32) + ahead, b.astype(F32) + behind
        ahead, behind = ring_step(a.astype(BF16), n), ring_step(b.astype(BF16), n, True)
    return chunk(0).astype(F32) + ahead + behind, done


def shard_gather(x):
    return lax.all_gather(x, "shard", axis=0, tiled=True)


def shard_scatter(x):
    return lax.psum_scatter(x, "shard", scatter_dimension=0, tiled=True).astype(F32)


def split_sum(x):
    high = x.astype(BF16)
    return high, (x - high.astype(F32)).astype(BF16)


def local(
    n_shard,
    hidden_in,
    doc_ids,
    expert_ids,
    slot_rows,
    out_grad,
    attn_gain,
    w_query,
    w_key,
    w_value,
    query_gain,
    key_gain,
    w_output,
    ffn_gain,
    w_router,
    w_gate,
    w_up,
    w_down,
):
    length, width = hidden_in.shape
    dim = width // HEADS
    heads = HEADS // 4
    part = width // 4
    routed = w_router.shape[1]
    experts = w_gate.shape[0]
    hidden_units = w_gate.shape[2]
    half_units = hidden_units // 2
    cap = slot_rows.shape[2]
    rep = lax.axis_index("rep")
    shard = lax.axis_index("shard")
    core, side = rep % 2, rep // 2
    my_rows = width // n_shard
    quarter = my_rows // 4

    cut = lambda w: lax.dynamic_slice_in_dim(w, rep * part, part, 1)
    qkv_block = jnp.concatenate([cut(w_query), cut(w_key), cut(w_value)], 1)
    output_block = lax.dynamic_slice_in_dim(w_output, rep * quarter, quarter, 0)
    pick = lambda w: lax.dynamic_index_in_dim(w, core, 0, keepdims=False)
    down_rows = hidden_units // n_shard
    unit = jnp.arange(half_units)
    unit = (unit // (down_rows // 2)) * down_rows + unit % (down_rows // 2)
    choose = lambda which: (
        jnp.arange(hidden_units)[:, None] == (unit + which * (down_rows // 2))[None, :]
    ).astype(BF16)
    mine = choose(side)
    gate_up_block = jnp.concatenate(
        [dot(pick(w_gate), mine).astype(BF16), dot(pick(w_up), mine).astype(BF16)], 1
    )
    down_block = lax.dynamic_slice_in_dim(pick(w_down), side * (down_rows // 2), down_rows // 2, 0)
    small_block = jnp.concatenate(
        [w_router, jnp.stack([attn_gain, query_gain, key_gain, ffn_gain], 1)]
        + [jnp.zeros((my_rows, 128 - 4 - routed), BF16)],
        1,
    )

    docs_all = jnp.concatenate(rep_gather(doc_ids), 0)
    before = docs_all[:, None, :] < docs_all[:, :, None]
    starts = jnp.sum(before.astype(jnp.int32), -1)
    places = (jnp.arange(length, dtype=jnp.int32)[None, :] - starts).astype(F32).reshape(-1)
    rates = THETA ** (-jnp.arange(dim // 2, dtype=F32) * 2.0 / dim)
    angles = places[:, None] * jnp.concatenate([rates, rates])[None, :]
    cosine, sine = jnp.cos(angles), jnp.sin(angles)
    doc_col = docs_all.reshape(-1, 1)
    doc_row = docs_all.reshape(4, 1, length)
    slots = slot_rows[0].reshape(experts * cap)
    select = (slots[:, None] == jnp.arange(length, dtype=jnp.int32)[None, :]).astype(BF16)

    def to_pair(x):
        own = lax.dynamic_index_in_dim(x, core, 0, keepdims=False)
        other = lax.dynamic_index_in_dim(x, 1 - core, 0, keepdims=False)
        return jnp.stack([own, swap(other, 1)])

    def to_experts(x):
        pair = to_pair(x)
        return jnp.concatenate([pair, swap(pair, 2)], 0)

    upstream_pair = to_pair(dot(select, out_grad).astype(BF16).reshape(experts, cap, width))

    pieces, arrays = ring_gather(
        jnp.concatenate([qkv_block, small_block], 1),
        n_shard,
        (swap(hidden_in, 2), cosine, sine, upstream_pair, output_block, gate_up_block, down_block),
    )
    hidden_side, cosine, sine, upstream_pair, output_block, gate_up_block, down_block = arrays
    hidden_all = jnp.concatenate(
        [hidden_in, swap(hidden_in, 1), hidden_side, swap(hidden_side, 1)], 0
    )
    normed_scale = rms_scale(hidden_all.astype(F32))
    piece, k, first = pieces[-1]
    piece, normed_scale = tie(piece, normed_scale)
    pieces[-1] = (piece, k, first)
    ids = ring_ids(n_shard)
    starts = np.stack([ids[:, k] * my_rows + first for _, k, first in pieces], 1)
    starts, ring = of_shard(starts, shard), of_shard(ids, shard)
    w_qkv, small_w = place_rows([piece for piece, _, _ in pieces], starts, width, 3 * part)
    router_w = small_w[:, :routed]
    gains = small_w[:, routed : routed + 4].T.astype(F32)
    w_out_part = shard_gather(output_block).reshape(n_shard, quarter, width)
    w_gu = shard_gather(gate_up_block)
    w_dn = shard_gather(down_block)
    gain_one, gain_two = gains[0], gains[3]
    gain_query = lax.dynamic_slice_in_dim(gains[1:2], rep * part, part, 1)
    gain_key = lax.dynamic_slice_in_dim(gains[2:3], rep * part, part, 1)

    upstream = out_grad.astype(F32)

    def send_side(x, send):
        return swap(x[2:].astype(send), 2)

    def from_experts(x, there, send):
        pair = x[:2] + there.astype(F32)
        other = swap(pair[1].astype(send), 1).astype(F32)
        first = jnp.where(core == 0, pair[0], other)
        return jnp.stack([first, jnp.where(core == 0, other, pair[0])])

    def add_slots(x):
        high, low = split_sum(x.reshape(experts * cap, width))
        return dot(select, high, ((0,), (0,))) + dot(select, low, ((0,), (0,)))

    normed = (hidden_all.astype(F32) * normed_scale * gain_one).astype(BF16)
    w_qkv, upstream_pair = tie(w_qkv, upstream_pair)
    qkv, upstream_side = tie(dot(normed, w_qkv), swap(upstream_pair, 2))
    slot_upstream = jnp.concatenate([upstream_pair, upstream_side], 0)
    query_raw, key_raw = qkv[:, :part], qkv[:, part : 2 * part]
    squares = jnp.stack([jnp.sum(query_raw * query_raw, -1), jnp.sum(key_raw * key_raw, -1)], -1)
    squares = rep_sum(squares.reshape(4, length, 2)).reshape(-1, 2)
    scales = lax.rsqrt(squares / width + EPSILON)
    query_scale, key_scale = scales[:, :1], scales[:, 1:]
    scales, w_out_part = tie(scales, w_out_part)
    out_core, out_side = swap(w_out_part, 1), swap(w_out_part, 2)
    mixed_heads, queries, keys, values = attend(
        qkv,
        query_scale,
        key_scale,
        gain_query,
        gain_key,
        cosine,
        sine,
        doc_col,
        doc_row,
        heads,
        dim,
    )
    mixed_heads, out_core, out_side = tie(mixed_heads, out_core, out_side)
    blocks = mixed_heads.reshape(4, length, part)
    from_side = swap(blocks[2:], 2)
    out_pieces = in_order([w_out_part, out_core, out_side, swap(out_side, 1)], rep)
    output_w = jnp.stack(out_pieces, 1).reshape(width, width)
    from_core, late_scale = tie(swap(blocks[1], 1), normed_scale)
    normed_ring = normed_in_order(ring, hidden_all, late_scale, gain_one[None])
    from_side, w_gu, output_w, normed_ring = tie(from_side, w_gu, output_w, normed_ring)
    mixed = jnp.concatenate(
        in_order([blocks[0], from_core, from_side[0], swap(from_side[1], 1)], rep), 1
    )
    hidden = hidden_in.astype(F32)
    residual = hidden + dot(mixed, output_w)
    scale_two = rms_scale(residual)
    inner = (residual * scale_two * gain_two).astype(BF16)
    logits = dot(inner, router_w)
    probs_all = jax.nn.softmax(logits, axis=-1)
    named = jnp.sum(
        (expert_ids[:, :, None] == jnp.arange(experts, dtype=jnp.int32)).astype(F32), 1
    )
    window = probs_all[:, :experts] * named
    select_wide = select.reshape(experts, cap, length).astype(F32)
    slot_gates = to_experts(jnp.sum(select_wide * window.T[:, None, :], -1))
    pair = to_pair(dot(select, inner).astype(BF16).reshape(experts, cap, width))
    from_side = swap(pair, 2)
    slot_inputs = jnp.concatenate([pair, from_side], 0)
    slot_inputs = slot_inputs.reshape(4 * cap, width)

    gate_up = dot(slot_inputs, w_gu)
    gate_part, up_part = gate_up[:, :half_units], gate_up[:, half_units:]
    sigma = jax.nn.sigmoid(gate_part)
    swished = gate_part * sigma
    activated = (swished * up_part).astype(BF16)
    returned = dot(activated, w_dn).reshape(4, cap, width)
    slot_gate_grad = jnp.sum(returned * slot_upstream.astype(F32), -1)
    slot_gate_grad = from_experts(slot_gate_grad, send_side(slot_gate_grad, F32), F32)
    returned_grad = (slot_gates[:, :, None] * slot_upstream.astype(F32)).astype(BF16)
    returned_grad = returned_grad.reshape(4 * cap, width)
    act_grad = dot(returned_grad, w_dn, ((1,), (1,)))
    gate_grad = act_grad * up_part * sigma * (1.0 + gate_part * (1.0 - sigma))
    gate_up_grad = jnp.concatenate([gate_grad.astype(BF16), (act_grad * swished).astype(BF16)], 1)
    slot_input_grad = dot(gate_up_grad, w_gu, ((1,), (1,))).reshape(4, cap, width)
    down_w_grad = dot(activated, returned_grad, ((0,), (0,))).astype(BF16)
    gate_up_w_grad = dot(slot_inputs, gate_up_grad, ((0,), (0,))).astype(BF16)
    at = lambda x, i, axis: lax.dynamic_index_in_dim(x, i, axis, keepdims=False)
    half = lambda which: at(mixed.reshape(length, n_shard, 2, 2, quarter), which, 3).reshape(
        length, width // 2
    )
    there, down_w_grad, gate_up_w_grad, mixed_own, mixed_other = tie(
        send_side(slot_input_grad, BF16),
        down_w_grad,
        gate_up_w_grad,
        half(core),
        half(1 - core),
    )
    slot_input_grad = from_experts(slot_input_grad, there, BF16)
    gate_up_owned = shard_scatter(gate_up_w_grad)
    down_owned = shard_scatter(down_w_grad)

    window_grad = jnp.sum(select_wide * slot_gate_grad[:, :, None], 1).T
    chosen_grad = jnp.concatenate(
        [window_grad * named, jnp.zeros((length, routed - experts), F32)], 1
    )
    logits_grad = (
        probs_all * (chosen_grad - jnp.sum(probs_all * chosen_grad, -1, keepdims=True))
    ).astype(BF16)
    router_grad = dot(inner, logits_grad, ((0,), (0,)))
    router_grad = jnp.pad(router_grad, ((0, 0), (0, 128 - routed)))
    inner_grad = add_slots(slot_input_grad) + dot(logits_grad, router_w, ((1,), (1,)))
    residual_part, gain_two_grad = norm_back(residual, scale_two, gain_two, inner_grad)
    residual_grad = upstream + residual_part
    branch_grad = residual_grad.astype(BF16)
    mixed_grad = dot(branch_grad, output_w, ((1,), (1,))).astype(BF16)
    piece = lambda j: lax.dynamic_slice_in_dim(mixed_grad, (rep ^ j) * part, part, 1)
    from_side = swap(jnp.stack([piece(2), piece(3)]), 2)
    from_core, branch_grad = tie(swap(piece(1), 1), branch_grad)
    half_grad = lambda half: dot(half, branch_grad, ((0,), (0,))).astype(BF16)
    out_there = swap(half_grad(mixed_other), 1)
    out_w_grad = (half_grad(mixed_own).astype(F32) + out_there).astype(BF16)
    from_side, out_w_grad, returned = tie(from_side, out_w_grad, returned)
    grads = jnp.concatenate([piece(0), from_core, from_side[0], swap(from_side[1], 1)], 0)
    out_w_grad = out_w_grad.reshape(n_shard, 2, quarter, width)
    out_there = swap(at(out_w_grad, 1 - side, 1), 2)

    query_grad, key_grad, value_grad = attend_back(
        queries, keys, values, grads, cosine, sine, doc_col, doc_row, heads, dim
    )
    value_grad, out_there = tie(value_grad, out_there)
    out_w_grad = (at(out_w_grad, side, 1).astype(F32) + out_there).astype(BF16)
    out_owned = shard_scatter(out_w_grad.reshape(n_shard * quarter, width))
    weighted_q, weighted_k = query_grad * gain_query, key_grad * gain_key
    means = jnp.stack(
        [jnp.sum(weighted_q * query_raw, -1), jnp.sum(weighted_k * key_raw, -1)], -1
    )
    means = rep_sum(means.reshape(4, length, 2)).reshape(-1, 2) / width
    means, returned = tie(means, returned)
    returned_there = send_side(returned, BF16)
    gain_query_grad = jnp.sum(query_grad * query_raw * query_scale, 0)
    gain_key_grad = jnp.sum(key_grad * key_raw * key_scale, 0)
    query_raw_grad = query_scale * weighted_q - query_raw * query_scale**3 * means[:, :1]
    key_raw_grad = key_scale * weighted_k - key_raw * key_scale**3 * means[:, 1:]
    qkv_grad = jnp.concatenate(
        [query_raw_grad.astype(BF16), key_raw_grad.astype(BF16), value_grad], 1
    )
    qkv_w_grad = dot(normed_ring, qkv_grad, ((0,), (0,))).astype(BF16)
    qkv_grad, qkv_w_grad, returned_there, gate_up_owned = tie(
        qkv_grad, qkv_w_grad, returned_there, gate_up_owned
    )
    own_gates = jnp.sum(select_wide * window.T[:, None, :], -1)
    returned = from_experts(returned, returned_there, BF16)
    output = (residual + add_slots(own_gates[:, :, None] * returned)).astype(BF16)
    place = lambda g: lax.dynamic_update_slice_in_dim(
        jnp.zeros((width,), F32), g, rep * part, 0
    )
    small = jnp.stack([gain_two_grad, place(gain_query_grad), place(gain_key_grad)], 1)
    small = small_in_order(ring, router_grad, small, routed)
    back = lambda slots, first, count, dtype: back_product(
        slots, w_qkv, first, count, length, dtype
    )

    def near(slots, odd):
        odd, slots = tie(swap(odd, 1), slots)
        return slots, back(slots, 2, 1, F32)[0], odd

    due = (
        lambda: (qkv_grad, back(qkv_grad, 1, 2, BF16)),
        near,
        lambda slots, two, from_core: (
            back(slots, 0, 1, F32)[0] + from_core[0].astype(F32),
            (two + from_core[1].astype(F32)).astype(BF16)[length // 2 :],
            swap((two + from_core[1].astype(F32)).astype(BF16)[: length // 2], 2),
            down_owned,
        ),
        lambda zero, rest, top, down: (zero, top, swap(rest, 2), down),
    )
    qkv_owned, (normed_grad, top, rest, down_owned) = ring_scatter(
        [qkv_w_grad, small], n_shard, due
    )
    normed_grad = normed_grad + jnp.concatenate([top, rest], 0).astype(F32)
    weighted = normed_grad * gain_one
    scale_one = normed_scale[:length]
    inner_mean = jnp.mean(weighted * hidden, -1, keepdims=True)
    hidden_part = scale_one * weighted - hidden * scale_one * scale_one * scale_one * inner_mean
    input_grad = residual_grad + hidden_part

    gain_part = jnp.sum(qkv_block.astype(F32) * qkv_owned[:, : 3 * part], 1, keepdims=True)
    column = jnp.arange(128)[None, :] == routed + 3
    qkv_owned = jnp.concatenate(
        [qkv_owned[:, : 3 * part], jnp.where(column, gain_part, qkv_owned[:, 3 * part :])], 1
    ).astype(BF16)
    qkv_core, qkv_side, out_owned = tie(swap(qkv_owned, 1), swap(qkv_owned, 2), out_owned)
    qkv_pieces = in_order([qkv_owned, qkv_core, qkv_side, swap(qkv_side, 1)], rep)
    spread = lambda i: jnp.concatenate(
        [p[:, i * part : (i + 1) * part] for p in qkv_pieces], 1
    ).astype(F32)
    grads_qkv = [spread(i) for i in range(3)]
    small = sum(p[:, 3 * part :].astype(F32) for p in qkv_pieces)
    gain_one_grad = small[:, routed + 3] / attn_gain.astype(F32)
    out_full = jnp.concatenate(in_order(rep_gather(out_owned.astype(BF16)), rep), 0).astype(F32)
    gu_pieces = in_order(rep_gather(gate_up_owned.astype(BF16)), rep)
    dn_pieces = in_order(rep_gather(down_owned.astype(BF16)), rep)
    one, two = choose(0), choose(1)
    join = lambda i: jnp.stack(
        [
            dot(gu_pieces[e][:, i * half_units : (i + 1) * half_units], one, ((1,), (1,)))
            + dot(gu_pieces[2 + e][:, i * half_units : (i + 1) * half_units], two, ((1,), (1,)))
            for e in range(experts)
        ]
    )
    down_full = jnp.stack(
        [jnp.concatenate([dn_pieces[e], dn_pieces[2 + e]], 0) for e in range(experts)]
    ).astype(F32)
    return (
        output,
        input_grad,
        gain_one_grad,
        *grads_qkv,
        small[:, routed + 1],
        small[:, routed + 2],
        out_full,
        small[:, routed],
        small[:, :routed],
        join(0),
        join(1),
        down_full,
    )


def solution(mesh):
    tokens = P(("shard", "rep"), None)
    rows = P("shard", None)
    middle = P(None, "shard", None)
    return jax.shard_map(
        functools.partial(local, mesh.shape["shard"]),
        mesh=mesh,
        in_specs=(
            tokens,
            tokens,
            tokens,
            P(("shard", "rep"), None, None),
            tokens,
            P("shard"),
            rows,
            rows,
            rows,
            P("shard"),
            P("shard"),
            rows,
            P("shard"),
            rows,
            middle,
            middle,
            middle,
        ),
        out_specs=(
            tokens,
            tokens,
            P("shard"),
            rows,
            rows,
            rows,
            P("shard"),
            P("shard"),
            rows,
            P("shard"),
            rows,
            middle,
            middle,
            middle,
        ),
        check_vma=False,
    )
```
